32 devices in a mesh: ctx: 16 (over z, y, core), wa: 2 (over x).
Axes of the slice: x: 2, y: 2, z: 4, core: 2. Of those that a mesh axis runs over, the one named last changes fastest.
Arguments:
- tokens: bfloat16 [2, 5120, 768], P('wa', 'ctx'), may hold values from -6 to 6
- segment_ids: int32 [2, 5120], P('wa', 'ctx'), may hold values from 0 to 31, never falling along the last dimension, each value on 1 to 3200 neighbouring positions
- cotangent: bfloat16 [2, 5120, 768], P('wa', 'ctx'), may hold values from -6 to 6
- w_query: bfloat16 [768, 768], P('wa'), may hold values from -0.21875 to 0.21875
- w_key: bfloat16 [768, 768], P('wa'), may hold values from -0.21875 to 0.21875
- w_value: bfloat16 [768, 768], P('wa'), may hold values from -0.21875 to 0.21875
- w_out: bfloat16 [768, 768], P('wa'), may hold values from -4 to 4
- w_up: bfloat16 [768, 3072], P('wa'), may hold values from -0.21875 to 0.21875
- w_down: bfloat16 [3072, 768], P('wa'), may hold values from -0.109375 to 0.109375
- b_query: bfloat16 [768], P('wa'), may hold values from -3 to 3
- b_value: bfloat16 [768], P('wa'), may hold values from -0.119628906 to 0.119628906
- b_out: bfloat16 [768], P('wa'), may hold values from -1.796875 to 1.796875
- gain_one: bfloat16 [768], P('wa'), may hold values from 0.5 to 1.5
- shift_one: bfloat16 [768], P('wa'), may hold values from -1.796875 to 1.796875
- b_up: bfloat16 [3072], P('wa'), may hold values from -1.796875 to 1.796875
- b_down: bfloat16 [768], P('wa'), may hold values from -1.796875 to 1.796875
- gain_two: bfloat16 [768], P('wa'), may hold values from 0.5 to 1.5
- shift_two: bfloat16 [768], P('wa'), may hold values from -1.796875 to 1.796875
Outputs:
- layer_out: bfloat16 [2, 5120, 768], P('wa', 'ctx')
- grad_tokens: float32 [2, 5120, 768], P('wa', 'ctx')
- grad_w_query: float32 [768, 768], P('wa')
- grad_w_key: float32 [768, 768], P('wa')
- grad_w_value: float32 [768, 768], P('wa')
- grad_w_out: float32 [768, 768], P('wa')
- grad_w_up: float32 [768, 3072], P('wa')
- grad_w_down: float32 [3072, 768], P('wa')
- grad_b_query: float32 [768], P('wa')
- grad_b_value: float32 [768], P('wa')
- grad_b_out: float32 [768], P('wa')
- grad_gain_one: float32 [768], P('wa')
- grad_shift_one: float32 [768], P('wa')
- grad_b_up: float32 [3072], P('wa')
- grad_b_down: float32 [768], P('wa')
- grad_gain_two: float32 [768], P('wa')
- grad_shift_two: float32 [768], P('wa')
The draws below stay inside these ranges and needn't reach their ends.
Inputs may be any that keep to these rules, and one draw needn't show every extreme that they name: `segment_ids`: within each sequence the ids never fall; each of the 32 ids names one document of 1 to 3200 tokens, and some document holds exactly 3200 tokens.
All inputs are finite; a program needn't handle non-finite values.
Results may differ from the reference program's by a relative error of at most 0.025.
Values may be sent and summed in bfloat16 or wider, within the bound.
No kernel may reach another device: no remote copies, remote signals or barrier semaphores. Data moves between devices by JAX's collectives and lax.ppermute only.
A program may use at most 192 MiB of HBM per device.

```python
import math
import jax
import jax.numpy as jnp
import numpy as np
from jax import lax

D = 768
HEADS = 12
HEAD_DIM = 64
FF = 3072
DOCS = 32
LEN = 5120
SEQS = 2
MOST = 3200


def block_scale(rng, shape, cuts, low, top_value):
    loudness = 1.0
    for dim, shards_of in cuts:
        draws = jax.random.uniform(jax.random.fold_in(jax.random.fold_in(rng, 6), dim), (shards_of,), jnp.float32, low / len(cuts), top_value / len(cuts))
        loudness = loudness * jnp.repeat(jnp.exp(draws), shape[dim] // shards_of).reshape((-1,) + (1,) * (len(shape) - 1 - dim))
    return loudness


def profile(amount, total, reach, skew):
    loads = [(1 << 20) // math.isqrt(rank ** skew) + 1 for rank in range(2, amount + 1)]
    rest, counts = total - reach - (amount - 1), [1] * (amount - 1)
    while rest > 0:
        movable = [i for i in range(amount - 1) if counts[i] < reach]
        mass, remaining = sum([loads[i] for i in movable]), rest
        for i in movable:
            extra = min(reach - counts[i], max(1, remaining * loads[i] // mass), rest)
            counts[i] = counts[i] + extra
            rest = rest - extra
    return np.array([reach] + counts)


def ragged_sizes(stream_key, amount, total, bound, skew):
    if amount == 2:
        one = jax.random.randint(stream_key, (), max(1, total - bound), min(bound, total - 1) + 1)
        return jnp.stack([one, total - one])
    lengths = jnp.asarray(profile(amount, total, bound, skew), jnp.int32)
    couples = (amount - 1) // 2
    giver, receiver = lengths[1:1 + 2 * couples:2], lengths[2:2 + 2 * couples:2]
    margin = jnp.minimum(giver - 1, bound - receiver)
    shifted = jax.random.randint(jax.random.fold_in(stream_key, 1), (couples,), 0, 1 << 20) % (margin + 1)
    lengths = lengths.at[1:1 + 2 * couples:2].set(giver - shifted).at[2:2 + 2 * couples:2].set(receiver + shifted)
    return lengths[jax.random.permutation(jax.random.fold_in(stream_key, 2), amount)]


def centred(rng, extent, scale, limit, pieces=(), kind=jnp.bfloat16):
    entries = jax.random.normal(rng, extent, jnp.float32) * scale
    if len(pieces) > 0:
        entries = block_scale(rng, extent, pieces, -0.22, 0.18) * entries
    return jnp.clip(entries, min=-limit, max=limit).astype(kind)


def setup_inputs(seed: int = 0) -> dict:
    key_list = jax.random.split(jax.random.key(seed), 19)
    tokens = centred(key_list[0], (SEQS, LEN, D), 1.0, 6.0, ((0, 2), (1, 16)))
    segment_ids = jax.vmap(lambda own: jnp.searchsorted(jnp.cumsum(ragged_sizes(own, DOCS, LEN, MOST, 2)), jnp.arange(LEN), side="right"))(jax.random.split(key_list[1], SEQS)).reshape((SEQS, LEN)).astype(jnp.int32)
    cotangent = centred(key_list[2], (SEQS, LEN, D), 1.0, 6.0, ((0, 2), (1, 16)))
    w_query = centred(key_list[3], (D, D), D ** -0.5, 0.21875, ((0, 2),))
    w_key = centred(key_list[4], (D, D), D ** -0.5, 0.21875, ((0, 2),))
    w_value = centred(key_list[5], (D, D), D ** -0.5, 0.21875, ((0, 2),))
    w_out = centred(key_list[6], (D, D), 2 ** -0.5, 4.0, ((0, 2),))
    w_up = centred(key_list[7], (D, FF), D ** -0.5, 0.21875, ((0, 2),))
    w_down = centred(key_list[8], (FF, D), FF ** -0.5, 0.109375, ((0, 2),))
    b_query = centred(key_list[9], (D,), 0.5, 3.0, ((0, 2),))
    b_value = centred(key_list[10], (D,), 0.02, 0.119628906, ((0, 2),))
    b_out = centred(key_list[11], (D,), 0.3, 1.796875, ((0, 2),))
    gain_one = jnp.clip(1.0 + 0.1 * jax.random.normal(key_list[12], (D,), jnp.float32), 0.5, 1.5).astype(jnp.bfloat16)
    shift_one = centred(key_list[13], (D,), 0.3, 1.796875, ((0, 2),))
    b_up = centred(key_list[14], (FF,), 0.3, 1.796875, ((0, 2),))
    b_down = centred(key_list[15], (D,), 0.3, 1.796875, ((0, 2),))
    gain_two = jnp.clip(1.0 + 0.1 * jax.random.normal(key_list[16], (D,), jnp.float32), 0.5, 1.5).astype(jnp.bfloat16)
    shift_two = centred(key_list[17], (D,), 0.3, 1.796875, ((0, 2),))
    return dict(tokens=tokens, segment_ids=segment_ids, cotangent=cotangent, w_query=w_query, w_key=w_key, w_value=w_value, w_out=w_out, w_up=w_up, w_down=w_down, b_query=b_query, b_value=b_value, b_out=b_out, gain_one=gain_one, shift_one=shift_one, b_up=b_up, b_down=b_down, gain_two=gain_two, shift_two=shift_two)


@jax.custom_vjp
def low(v):
    return lax.optimization_barrier(v.astype(jnp.bfloat16)).astype(jnp.float32)

@jax.custom_vjp
def low_back(v):
    return v

def low_keep(v):
    return (low(v), None)

def low_pass(kept, grad):
    return (grad,)

def back_keep(v):
    return (v, None)

def back_low(kept, grad):
    return (low(grad),)
low.defvjp(low_keep, low_pass)
low_back.defvjp(back_keep, back_low)
epsilon = 1e-05
highest = lax.Precision.HIGHEST

def product(left, right):
    return jnp.dot(left, right, precision=highest)

def normalize(values, gain, shift):
    centre = values - lax.optimization_barrier(jnp.mean(values, axis=-1, keepdims=True))
    spread = lax.optimization_barrier(jnp.mean(centre * centre, axis=-1, keepdims=True))
    return centre * lax.rsqrt(spread + epsilon) * gain + shift

def attend_rows(queries, keys, values, query_seg, key_seg):
    scores = jnp.einsum('qhd,khd->hqk', queries, keys, precision=highest) * 0.125
    scores = low_back(scores)
    allowed = (query_seg[:, None] == key_seg[None, :])[None]
    masked = jnp.where(allowed, scores, -1e+30)
    largest = lax.optimization_barrier(jnp.max(masked, axis=-1, keepdims=True))
    weights = jnp.where(allowed, jnp.exp(masked - largest), 0.0)
    probs = weights / lax.optimization_barrier(jnp.sum(weights, axis=-1, keepdims=True))
    mixed = jnp.einsum('hqk,khd->qhd', low(probs), values, precision=highest)
    return mixed.reshape(mixed.shape[0], HEADS * HEAD_DIM)

def attend_sequence(queries, keys, values, segments):
    rows = 512 if LEN % 512 == 0 else LEN
    blocks = LEN // rows
    query_blocks = queries.reshape(blocks, rows, HEADS, HEAD_DIM)
    seg_blocks = segments.reshape(blocks, rows)

    def one_block(pair):
        return attend_rows(pair[0], keys, values, pair[1], segments)
    mixed = lax.map(jax.checkpoint(one_block), (query_blocks, seg_blocks))
    return mixed.reshape(LEN, HEADS * HEAD_DIM)

def reference(tokens, segment_ids, cotangent, w_query, w_key, w_value, w_out, w_up, w_down, b_query, b_value, b_out, gain_one, shift_one, b_up, b_down, gain_two, shift_two):

    def widen(array):
        return array.astype(jnp.float32)

    def layer(inputs, p_query, p_key, p_value, p_out, p_up, p_down, c_query, c_value, c_out, g_one, s_one, c_up, c_down, g_two, s_two):
        queries = low_back(low(product(inputs, p_query) + c_query))
        keys = low_back(low(product(inputs, p_key)))
        values = low_back(low(product(inputs, p_value) + c_value))
        shaped = (SEQS, LEN, HEADS, HEAD_DIM)

        def one_sequence(group):
            return attend_sequence(group[0], group[1], group[2], group[3])
        mixed = lax.map(one_sequence, (queries.reshape(shaped), keys.reshape(shaped), values.reshape(shaped), segment_ids))
        mixed = low_back(low(mixed))
        attended = low_back(product(mixed, p_out) + c_out)
        hidden = normalize(inputs + attended, g_one, s_one)
        raised = low_back(product(low(hidden), p_up) + c_up)
        active = low(jax.nn.gelu(raised, approximate=False))
        lowered = low_back(product(active, p_down) + c_down)
        return normalize(hidden + lowered, g_two, s_two)
    result, pull = jax.vjp(layer, widen(tokens), widen(w_query), widen(w_key), widen(w_value), widen(w_out), widen(w_up), widen(w_down), widen(b_query), widen(b_value), widen(b_out), widen(gain_one), widen(shift_one), widen(b_up), widen(b_down), widen(gain_two), widen(shift_two))
    grads = pull(widen(cotangent))
    return (result.astype(jnp.bfloat16), grads[0], grads[1], grads[2], grads[3], grads[4], grads[5], grads[6], grads[7], grads[8], grads[9], grads[10], grads[11], grads[12], grads[13], grads[14], grads[15])
```

```python
import functools

import jax
import jax.numpy as jnp
from jax import lax
from jax.experimental import pallas as pl
from jax.experimental.pallas import tpu as pltpu
from jax.sharding import Mesh
from jax.sharding import PartitionSpec as P

D = 768
HEADS = 12
HEAD_DIM = 64
FF = 3072
DOCS = 32

GROUPS = 4
OWN = HEADS // GROUPS
WIDTH = OWN * HEAD_DIM
QTILE = 256
KTILE = 512

epsilon = 1e-05
masked_value = -1e30
NT = (((1,), (1,)), ((), ()))
NN = (((1,), (0,)), ((), ()))


def widen(array):
    return array.astype(jnp.float32)


def low(array):
    return array.astype(jnp.bfloat16)


def mm(left, right):
    return jnp.dot(left, right, preferred_element_type=jnp.float32)


def outer_sum(left, right):
    return lax.dot_general(
        left, right, (((0,), (0,)), ((), ())), preferred_element_type=jnp.float32
    )


def back_product(grad, weight):
    return lax.dot_general(grad, weight, NT, preferred_element_type=jnp.float32)


def norm_forward(values, gain, shift):
    centre = values - jnp.mean(values, axis=-1, keepdims=True)
    scale = lax.rsqrt(jnp.mean(centre * centre, axis=-1, keepdims=True) + epsilon)
    unit = centre * scale
    return (unit * gain + shift, unit, scale)


def norm_backward(grad, unit, scale, gain):
    grad_gain = jnp.sum(grad * unit, axis=0)
    grad_shift = jnp.sum(grad, axis=0)
    inner = grad * gain
    grad_in = scale * (
        inner
        - jnp.mean(inner, axis=-1, keepdims=True)
        - unit * jnp.mean(inner * unit, axis=-1, keepdims=True)
    )
    return (grad_in, grad_gain, grad_shift)


def gelu_pair(values):
    cumulative = 0.5 * (1.0 + lax.erf(values * 0.7071067811865476))
    density = jnp.exp(-0.5 * values * values) * 0.3989422804014327
    return (values * cumulative, cumulative + values * density)


def swap(array, axis, bit):
    size = lax.axis_size(axis)
    return lax.ppermute(array, axis, [(i, i ^ bit) for i in range(size)])


K_BLOCK = (0, 0, 1)
V_BLOCK = (2, 2, 1)
K_UPPER = (False, True, True)
V_UPPER = (False, True, False)


def lane_half(array, upper):
    lane = lax.broadcasted_iota(jnp.int32, array.shape, 1)
    keep = (lane >= 64) if upper else (lane < 64)
    return jnp.where(keep, array, jnp.zeros_like(array))


def load_pieces(where, ids, pieces, kv, sem, rows, classes):
    copies = []
    for piece, (mask, flips) in zip(pieces, where):
        for slot, flip in enumerate(flips):
            chunk = (ids[0] ^ flip) * classes + (ids[1] ^ mask)
            start = pl.multiple_of(chunk * rows, 64)
            copies.append(
                pltpu.make_async_copy(
                    piece.at[slot], kv.at[pl.ds(start, rows), :], sem.at[len(copies)]
                )
            )
    for copy in copies:
        copy.start()
    for copy in copies:
        copy.wait()


def forward_kernel(where, rows, classes, ids, flags, q, seg_q, seg_k, *rest):
    count = len(where)
    pieces = rest[:count]
    o_low, o_full, lse, kv, vt, qm, top, total, accum, sem = rest[count:]
    length = kv.shape[0]
    tiles = length // KTILE
    load_pieces(where, ids, pieces, kv, sem, rows, classes)

    @pl.loop(0, tiles)
    def _(t):
        start = pl.multiple_of(t * KTILE, KTILE)
        vt[0:128, pl.ds(start, KTILE)] = kv[pl.ds(start, KTILE), 128:256].T
        vt[128:256, pl.ds(start, KTILE)] = kv[pl.ds(start, KTILE), 256:384].T

    v_row = (128, 192, 0)

    @pl.loop(0, q.shape[0] // QTILE)
    def _(j):
        base = pl.multiple_of(j * QTILE, QTILE)
        for head in range(OWN):
            block = q[pl.ds(base, QTILE), pl.ds(128 * K_BLOCK[head], 128)]
            qm[head] = lane_half(block, K_UPPER[head])
        top[...] = jnp.full_like(top, masked_value)
        total[...] = jnp.zeros_like(total)
        accum[...] = jnp.zeros_like(accum)
        query_ids = seg_q[0:1, pl.ds(base, QTILE)]

        @pl.loop(0, tiles)
        def _(t):
            @pl.when(flags[j * tiles + t] > 0)
            def _():
                start = pl.multiple_of(t * KTILE, KTILE)
                ids_k = seg_k[pl.ds(start, KTILE), :]
                same = jnp.concatenate([ids_k] * (QTILE // 128), axis=1) == query_ids
                for head in range(OWN):
                    keys = kv[pl.ds(start, KTILE), 128 * K_BLOCK[head] : 128 * K_BLOCK[head] + 128]
                    scores = lax.dot_general(
                        keys, qm[head], NT, preferred_element_type=jnp.float32
                    )
                    scores = jnp.where(same, scores, masked_value)
                    old = top[head : head + 1, :]
                    new = jnp.maximum(old, jnp.max(scores, axis=0, keepdims=True))
                    weights = jnp.exp(scores - new)
                    factor = jnp.exp(old - new)
                    top[head : head + 1, :] = new
                    total[head : head + 1, :] = total[head : head + 1, :] * factor + jnp.sum(
                        weights, axis=0, keepdims=True
                    )
                    rows_v = slice(v_row[head], v_row[head] + 64)
                    accum[64 * head : 64 * head + 64, :] = accum[
                        64 * head : 64 * head + 64, :
                    ] * factor + jnp.dot(
                        vt[rows_v, pl.ds(start, KTILE)],
                        weights.astype(jnp.bfloat16),
                        preferred_element_type=jnp.float32,
                    )

        outs = [accum[64 * head : 64 * head + 64, :] / total[head : head + 1, :] for head in range(OWN)]
        lower = jnp.concatenate(outs[:2], axis=0).T
        upper = jnp.concatenate([outs[2], jnp.zeros_like(outs[2])], axis=0).T
        o_full[pl.ds(base, QTILE), 0:128] = lower
        o_full[pl.ds(base, QTILE), 128:256] = upper
        o_low[pl.ds(base, QTILE), 0:128] = lower.astype(jnp.bfloat16)
        o_low[pl.ds(base, QTILE), 128:192] = upper[:, 0:64].astype(jnp.bfloat16)
        lse[:, pl.ds(base, QTILE)] = top[...] + jnp.log(total[...])


def backward_kernel(where, rows, classes, out_where, ids, flags, q, seg_q, seg_k, grad, o_full, lse, *rest):
    count = len(where)
    pieces = rest[:count]
    rest = rest[count:]
    outs = rest[: len(out_where)]
    dq, kv, kt, qm, dom, stats, dqt, dkv, low_kv, sem = rest[len(out_where) :]
    length = kv.shape[0]
    tiles = length // KTILE
    load_pieces(where, ids, pieces, kv, sem, rows, classes)

    @pl.loop(0, tiles)
    def _(t):
        start = pl.multiple_of(t * KTILE, KTILE)
        kt[0:128, pl.ds(start, KTILE)] = kv[pl.ds(start, KTILE), 0:128].T
        kt[128:256, pl.ds(start, KTILE)] = kv[pl.ds(start, KTILE), 128:256].T
        dkv[pl.ds(start, KTILE), :] = jnp.zeros((KTILE, 384), jnp.float32)

    k_row = (0, 64, 192)

    @pl.loop(0, q.shape[0] // QTILE)
    def _(j):
        base = pl.multiple_of(j * QTILE, QTILE)
        for head in range(OWN):
            block = q[pl.ds(base, QTILE), pl.ds(128 * K_BLOCK[head], 128)]
            qm[head] = lane_half(block, K_UPPER[head])
            block = grad[pl.ds(base, QTILE), pl.ds(128 * (2 - V_BLOCK[head]), 128)]
            dom[head] = lane_half(block, V_UPPER[head])
        for part in range(2):
            product = (
                grad[pl.ds(base, QTILE), 128 * part : 128 * part + 128].astype(jnp.float32)
                * o_full[pl.ds(base, QTILE), 128 * part : 128 * part + 128]
            ).T
            for half in range(2):
                head = 2 * part + half
                if head < OWN:
                    stats[head : head + 1, :] = jnp.sum(
                        product[64 * half : 64 * half + 64], axis=0, keepdims=True
                    )
        dqt[...] = jnp.zeros_like(dqt)
        query_ids = seg_q[0:1, pl.ds(base, QTILE)]

        @pl.loop(0, tiles)
        def _(t):
            @pl.when(flags[j * tiles + t] > 0)
            def _():
                start = pl.multiple_of(t * KTILE, KTILE)
                ids_k = seg_k[pl.ds(start, KTILE), :]
                same = jnp.concatenate([ids_k] * (QTILE // 128), axis=1) == query_ids
                sums = [None, None, None]

                def add(block, term):
                    sums[block] = term if sums[block] is None else sums[block] + term

                for head in range(OWN):
                    kb, vb = K_BLOCK[head], V_BLOCK[head]
                    keys = kv[pl.ds(start, KTILE), 128 * kb : 128 * kb + 128]
                    vals = kv[pl.ds(start, KTILE), 128 * vb : 128 * vb + 128]
                    scores = lax.dot_general(
                        keys, qm[head], NT, preferred_element_type=jnp.float32
                    )
                    probs = jnp.where(
                        same, jnp.exp(scores - lse[head : head + 1, pl.ds(base, QTILE)]), 0.0
                    )
                    grad_probs = lax.dot_general(
                        vals, dom[head], NT, preferred_element_type=jnp.float32
                    )
                    grad_scores = (probs * (grad_probs - stats[head : head + 1, :])).astype(
                        jnp.bfloat16
                    )
                    add(vb, jnp.dot(probs.astype(jnp.bfloat16), dom[head], preferred_element_type=jnp.float32))
                    add(kb, jnp.dot(grad_scores, qm[head], preferred_element_type=jnp.float32))
                    rows_k = slice(k_row[head], k_row[head] + 64)
                    dqt[64 * head : 64 * head + 64, :] += jnp.dot(
                        kt[rows_k, pl.ds(start, KTILE)],
                        grad_scores,
                        preferred_element_type=jnp.float32,
                    )
                for block in range(3):
                    dkv[pl.ds(start, KTILE), 128 * block : 128 * block + 128] += sums[block]

        lower = dqt[0:128, :].T * 0.125
        upper = dqt[64:192, :].T * 0.125
        dq[pl.ds(base, QTILE), 0:128] = lower.astype(jnp.bfloat16)
        dq[pl.ds(base, QTILE), 128:192] = upper[:, 64:128].astype(jnp.bfloat16)

    @pl.loop(0, tiles)
    def _(t):
        start = pl.multiple_of(t * KTILE, KTILE)
        low_kv[pl.ds(start, KTILE), :] = dkv[pl.ds(start, KTILE), :].astype(jnp.bfloat16)

    copies = []
    for out, masks in zip(outs, out_where):
        for slot, mask in enumerate(masks):
            for flip in range(GROUPS):
                chunk = (ids[0] ^ flip) * classes + (ids[1] ^ mask)
                start = pl.multiple_of(chunk * rows, 64)
                copies.append(
                    pltpu.make_async_copy(
                        low_kv.at[pl.ds(start, rows), :], out.at[slot, flip], sem.at[len(copies)]
                    )
                )
    for copy in copies:
        copy.start()
    for copy in copies:
        copy.wait()


VMEM_SPEC = pl.BlockSpec(memory_space=pltpu.VMEM)
SMEM_SPEC = pl.BlockSpec(memory_space=pltpu.SMEM)
ANY_SPEC = pl.BlockSpec(memory_space=pl.ANY)
PARAMS = pltpu.CompilerParams(vmem_limit_bytes=56 * 1024 * 1024)


def attend_forward(ids, flags, q, seg_q, seg_k, pieces, where, rows, classes):
    length = seg_k.shape[0]
    queries = q.shape[0]
    copies = sum(len(flips) for _, flips in where)
    return pl.pallas_call(
        functools.partial(forward_kernel, where, rows, classes),
        out_shape=(
            jax.ShapeDtypeStruct((queries, WIDTH), jnp.bfloat16),
            jax.ShapeDtypeStruct((queries, 256), jnp.float32),
            jax.ShapeDtypeStruct((8, queries), jnp.float32),
        ),
        in_specs=[SMEM_SPEC, SMEM_SPEC, VMEM_SPEC, VMEM_SPEC, VMEM_SPEC]
        + [ANY_SPEC] * len(pieces),
        out_specs=(VMEM_SPEC,) * 3,
        scratch_shapes=[
            pltpu.VMEM((length, 384), jnp.bfloat16),
            pltpu.VMEM((256, length), jnp.bfloat16),
            pltpu.VMEM((OWN, QTILE, 128), jnp.bfloat16),
            pltpu.VMEM((8, QTILE), jnp.float32),
            pltpu.VMEM((8, QTILE), jnp.float32),
            pltpu.VMEM((WIDTH, QTILE), jnp.float32),
            pltpu.SemaphoreType.DMA((copies,)),
        ],
        compiler_params=PARAMS,
        cost_estimate=pl.CostEstimate(
            flops=queries * length * WIDTH * 4, bytes_accessed=8 << 20, transcendentals=0
        ),
        name="attend_forward",
    )(ids, flags, q, seg_q, seg_k, *pieces)


def attend_backward(ids, flags, q, seg_q, seg_k, grad, o_full, lse, pieces, where, rows, classes, out_where):
    length = seg_k.shape[0]
    queries = q.shape[0]
    copies = sum(len(flips) for _, flips in where)
    return pl.pallas_call(
        functools.partial(backward_kernel, where, rows, classes, out_where),
        out_shape=tuple(
            jax.ShapeDtypeStruct((len(masks), GROUPS, rows, 384), jnp.bfloat16)
            for masks in out_where
        )
        + (jax.ShapeDtypeStruct((queries, WIDTH), jnp.bfloat16),),
        in_specs=[SMEM_SPEC, SMEM_SPEC] + [VMEM_SPEC] * 6 + [ANY_SPEC] * len(pieces),
        out_specs=(ANY_SPEC,) * len(out_where) + (VMEM_SPEC,),
        scratch_shapes=[
            pltpu.VMEM((length, 384), jnp.bfloat16),
            pltpu.VMEM((256, length), jnp.bfloat16),
            pltpu.VMEM((OWN, QTILE, 128), jnp.bfloat16),
            pltpu.VMEM((OWN, QTILE, 128), jnp.bfloat16),
            pltpu.VMEM((8, QTILE), jnp.float32),
            pltpu.VMEM((WIDTH, QTILE), jnp.float32),
            pltpu.VMEM((length, 384), jnp.float32),
            pltpu.VMEM((length, 384), jnp.bfloat16),
            pltpu.SemaphoreType.DMA((copies,)),
        ],
        compiler_params=PARAMS,
        cost_estimate=pl.CostEstimate(
            flops=queries * length * WIDTH * 10, bytes_accessed=16 << 20, transcendentals=0
        ),
        name="attend_backward",
    )(ids, flags, q, seg_q, seg_k, grad, o_full, lse, *pieces)


def gather_rows(weight, core):
    half = weight.shape[0] // 2
    part = lax.dynamic_slice_in_dim(weight, core * half, half, 0)
    return lax.all_gather(part, ("wa", "c"), axis=0, tiled=True)


def reduce_blocks(grad):
    flat = grad.reshape((-1,) + grad.shape[2:])
    mine = lax.psum_scatter(flat, ("wa", "c"), scatter_dimension=0, tiled=True)
    mine = lax.psum_scatter(mine, "m", scatter_dimension=0, tiled=True)
    mine = lax.psum_scatter(mine, "h", scatter_dimension=0, tiled=True)
    return lax.all_gather(mine, ("c", "m", "h"), axis=0, tiled=True)


def pick_columns(weight, group):
    q, k, v = (lax.dynamic_slice_in_dim(w, group * WIDTH, WIDTH, w.ndim - 1) for w in weight)
    return jnp.concatenate(
        [
            k[..., :128],
            v[..., 128:],
            k[..., 128:],
            v[..., :128],
            q[..., :128],
            jnp.zeros_like(q[..., :64]),
            q[..., 128:],
        ],
        axis=-1,
    )


def per_device(
    tokens,
    segment_ids,
    cotangent,
    w_query,
    w_key,
    w_value,
    w_out,
    w_up,
    w_down,
    b_query,
    b_value,
    b_out,
    gain_one,
    shift_one,
    b_up,
    b_down,
    gain_two,
    shift_two,
):
    mid = lax.axis_size("m")
    wide = lax.axis_size("wa")
    classes = 2 * mid
    group = lax.axis_index("h")
    core = lax.axis_index("c")
    kind = lax.axis_index("m") * 2 + core
    side = lax.axis_index("wa")
    inputs = tokens[0]
    count = inputs.shape[0]
    length = count * GROUPS * classes
    tiles = length // KTILE
    ids = jnp.stack([group, kind]).astype(jnp.int32)
    order = group ^ jnp.arange(GROUPS)

    second = swap(inputs, "h", 1)
    third = swap(inputs, "h", 2)
    fourth = swap(third, "h", 1)

    smalls = [b_query, b_value, b_out, gain_one, shift_one, b_up, b_down, gain_two, shift_two]
    joined = lax.all_gather(jnp.concatenate(smalls), "wa", axis=0)
    full, place = [], 0
    for item in smalls:
        size = item.shape[0]
        full.append(widen(joined[:, place : place + size].reshape(-1)))
        place += size
    bias_query, bias_value, bias_out, gain_attn, shift_attn, bias_up, bias_down, gain_ffn, shift_ffn = full

    segs = lax.all_gather(segment_ids[0], ("h", "m", "c"), axis=0)
    w_group = lax.all_gather(
        pick_columns((w_query, w_key, w_value), group), "wa", axis=0, tiled=True
    )
    zero_bias = jnp.zeros_like(bias_query)
    b_group = pick_columns((bias_query, zero_bias, bias_value), group)

    full_out = gather_rows(w_out, core)
    full_up = gather_rows(w_up, core)
    full_down = gather_rows(w_down, core)
    full_query = gather_rows(w_query, core)
    full_key = gather_rows(w_key, core)
    full_value = gather_rows(w_value, core)

    own_segs = jnp.take(segs.reshape(GROUPS, classes, count), order, axis=0)
    own_segs = lax.dynamic_index_in_dim(own_segs, kind, 1, keepdims=False).reshape(-1)
    names = jnp.arange(DOCS)
    has_q = jnp.any(own_segs.reshape(-1, QTILE, 1) == names, axis=1)
    has_k = jnp.any(segs.reshape(tiles, KTILE, 1) == names, axis=1)
    flags = jnp.any(has_q[:, None, :] & has_k[None, :, :], axis=-1).astype(jnp.int32).reshape(-1)
    seg_q = jnp.broadcast_to(widen(own_segs)[None, :], (8, GROUPS * count))
    seg_k = jnp.broadcast_to(widen(segs).reshape(-1, 1), (length, 128))

    def project(chunks):
        joined = jnp.concatenate(chunks, axis=0)
        kv = low(mm(joined, w_group[:, :384]) + b_group[:384])
        return kv.reshape(len(chunks), count, 384)

    where, pieces = [], []
    for chunks, flips in (((inputs, second, third), (0, 1, 2)), ((fourth,), (3,))):
        have = {0: project(chunks)}
        bit = 1
        while bit < mid:
            for mask in list(have):
                have[mask | (bit << 1)] = swap(have[mask], "m", bit)
            bit *= 2
        for mask in list(have):
            have[mask | 1] = swap(have[mask], "c", 1)
        for mask, piece in have.items():
            where.append((mask, flips))
            pieces.append(piece)
    where = tuple(where)
    group_tokens = jnp.concatenate([inputs, second, third, fourth], axis=0)
    q_rows = low(mm(group_tokens, w_group[:, 384:]) + b_group[384:]) * jnp.bfloat16(0.125)

    o_low, o_full, lse = attend_forward(
        ids, flags, q_rows, seg_q, seg_k, pieces, where, count, classes
    )

    def send_back(rows):
        parts = rows.reshape(GROUPS, count, -1)
        return [parts[0]] + [swap(parts[flip], "h", flip) for flip in range(1, GROUPS)]

    def in_order(parts):
        return jnp.take(jnp.stack(parts), order, axis=0)

    attn_low = jnp.transpose(in_order(send_back(o_low)), (1, 0, 2)).reshape(count, D)
    attended = mm(attn_low, full_out) + bias_out
    hidden, unit_one, scale_one = norm_forward(widen(inputs) + attended, gain_attn, shift_attn)
    hidden_low = low(hidden)
    raised = mm(hidden_low, full_up) + bias_up
    active, slope = gelu_pair(raised)
    active_low = low(active)
    lowered = mm(active_low, full_down) + bias_down
    result, unit_two, scale_two = norm_forward(hidden + lowered, gain_ffn, shift_ffn)
    grad_sum_two, grad_gain_two, grad_shift_two = norm_backward(
        widen(cotangent[0]), unit_two, scale_two, gain_ffn
    )
    grad_lowered = low(grad_sum_two)
    grad_w_down = low(outer_sum(active_low, grad_lowered))
    grad_b_down = jnp.sum(widen(grad_lowered), axis=0)
    grad_raised = low(back_product(grad_lowered, full_down) * slope)
    grad_w_up = low(outer_sum(hidden_low, grad_raised))
    grad_b_up = jnp.sum(widen(grad_raised), axis=0)
    grad_hidden = grad_sum_two + back_product(grad_raised, full_up)
    grad_sum_one, grad_gain_one, grad_shift_one = norm_backward(
        grad_hidden, unit_one, scale_one, gain_attn
    )
    grad_attended = low(grad_sum_one)
    grad_w_out = low(outer_sum(attn_low, grad_attended))
    grad_b_out = jnp.sum(widen(grad_attended), axis=0)
    grad_attn = low(back_product(grad_attended, full_out))

    by_group = jnp.take(
        jnp.transpose(grad_attn.reshape(count, GROUPS, WIDTH), (1, 0, 2)), order, axis=0
    )
    grad_heads = [by_group[0]] + [swap(by_group[flip], "h", flip) for flip in range(1, GROUPS)]
    grad_rows = jnp.pad(jnp.concatenate(grad_heads, axis=0), ((0, 0), (0, 64)))

    keep, give = tuple(range(0, classes, 2)), tuple(range(1, classes, 2))
    kept, given, dq = attend_backward(
        ids, flags, q_rows, seg_q, seg_k, grad_rows, o_full, lse,
        pieces, where, count, classes, (keep, give),
    )

    blocks = 2 * wide
    vectors = jnp.concatenate(
        [grad_b_out, grad_gain_one, grad_shift_one, grad_b_down, grad_gain_two, grad_shift_two, grad_b_up]
    )
    vectors = jnp.pad(low(vectors).reshape(-1, D), ((0, 6), (0, 0)))
    down_rows, up_rows, out_rows = FF // blocks, FF // blocks, D // blocks
    ffn = jnp.concatenate(
        [
            grad_w_down.reshape(blocks, down_rows, D),
            grad_w_up.reshape(blocks, up_rows, D),
            grad_w_out.reshape(blocks, out_rows, D),
            jnp.broadcast_to(vectors[None], (blocks, 16, D)),
        ],
        axis=1,
    )
    ffn_sum = reduce_blocks(ffn).reshape(2, -1, D)
    out_down = widen(ffn_sum[:, :down_rows]).reshape(-1, D)
    out_up = widen(ffn_sum[:, down_rows : down_rows + up_rows]).reshape(-1, FF)
    place = down_rows + up_rows
    out_out = widen(ffn_sum[:, place : place + out_rows]).reshape(-1, D)
    small = widen(ffn_sum[0, place + out_rows :])

    def share(row, rows):
        vector = small[row : row + rows].reshape(-1)
        size = vector.shape[0] // wide
        return lax.dynamic_slice_in_dim(vector, side * size, size, 0)

    partial = widen(kept) + widen(swap(given, "c", 1))
    stay = list(keep)
    bit = mid // 2
    while bit >= 1:
        mask = bit << 1
        near = [i for i, m in enumerate(stay) if not m & mask]
        far = [i for i, m in enumerate(stay) if m & mask]
        sent = swap(low(partial[far[0] : far[-1] + 1]), "m", bit)
        partial = widen(low(partial[near[0] : near[-1] + 1])) + widen(sent)
        stay = [stay[i] for i in near]
        bit //= 2
    dkv = low(partial[0]).reshape(GROUPS * count, 384)
    both = jnp.concatenate([dkv, dq], axis=1)

    width = both.shape[1]
    w_grad = low(outer_sum(group_tokens, both)).reshape(blocks, D // blocks, width)
    b_grad = low(jnp.sum(widen(both), axis=0))
    b_grad = jnp.pad(b_grad[None], ((0, 15), (0, 0)))
    qkv = jnp.concatenate([w_grad, jnp.broadcast_to(b_grad[None], (blocks, 16, width))], axis=1)
    rows = qkv.shape[1]
    mine = lax.psum_scatter(qkv.reshape(blocks * rows, width), ("wa", "c"), scatter_dimension=0, tiled=True)
    mine = lax.psum(mine, "m")
    every = lax.all_gather(mine, ("c", "h"), axis=0).reshape(2, GROUPS, rows, width)
    every = widen(every)

    def columns(block):
        k = jnp.concatenate([block[..., :128], block[..., 192:256]], axis=-1)
        v = jnp.concatenate([block[..., 256:384], block[..., 128:192]], axis=-1)
        q = block[..., 384:576]
        return [
            jnp.transpose(item, (0, 2, 1, 3)).reshape(2, -1, D) for item in (q, k, v)
        ]

    out_query, out_key, out_value = (
        item.reshape(-1, D) for item in columns(every[:, :, : rows - 16])
    )
    bias_rows = columns(every[:, :, rows - 16 : rows - 15])
    part = D // wide
    out_b_query = lax.dynamic_slice_in_dim(bias_rows[0][0, 0], side * part, part, 0)
    out_b_value = lax.dynamic_slice_in_dim(bias_rows[2][0, 0], side * part, part, 0)

    back = in_order(send_back(both))
    own_key = jnp.concatenate([back[..., :128], back[..., 192:256]], axis=-1)
    own_value = jnp.concatenate([back[..., 256:384], back[..., 128:192]], axis=-1)
    own_query = back[..., 384:576]
    natural = [
        jnp.transpose(item, (1, 0, 2)).reshape(count, D) for item in (own_query, own_key, own_value)
    ]
    grad_inputs = (
        grad_sum_one
        + back_product(natural[0], full_query)
        + back_product(natural[1], full_key)
        + back_product(natural[2], full_value)
    )
    return (
        low(result)[None],
        grad_inputs[None],
        out_query,
        out_key,
        out_value,
        out_out,
        out_up,
        out_down,
        out_b_query,
        out_b_value,
        share(0, 1),
        share(1, 1),
        share(2, 1),
        share(6, 4),
        share(3, 1),
        share(4, 1),
        share(5, 1),
    )


def solution(mesh):
    chunks, wide = mesh.devices.shape
    finer = Mesh(
        mesh.devices.reshape(GROUPS, chunks // (2 * GROUPS), 2, wide), ("h", "m", "c", "wa")
    )
    ctx = ("h", "m", "c")
    seq3, seq2 = P("wa", ctx, None), P("wa", ctx)
    matrix, vector = P("wa", None), P("wa")
    return jax.shard_map(
        per_device,
        mesh=finer,
        in_specs=(seq3, seq2, seq3) + (matrix,) * 6 + (vector,) * 9,
        out_specs=(seq3, seq3) + (matrix,) * 6 + (vector,) * 9,
        check_vma=False,
    )
```

```python
import functools

import jax
import jax.numpy as jnp
from jax import lax
from jax.experimental import pallas as pl
from jax.experimental.pallas import tpu as pltpu
from jax.sharding import Mesh
from jax.sharding import PartitionSpec as P

D = 768
HEADS = 12
HEAD_DIM = 64
FF = 3072
DOCS = 32

GROUPS = 4
OWN = HEADS // GROUPS
WIDTH = OWN * HEAD_DIM
QTILE = 256
KTILE = 512

epsilon = 1e-05
masked_value = -1e30
NT = (((1,), (1,)), ((), ()))
NN = (((1,), (0,)), ((), ()))


def widen(array):
    return array.astype(jnp.float32)


def low(array):
    return array.astype(jnp.bfloat16)


def mm(left, right):
    return jnp.dot(left, right, preferred_element_type=jnp.float32)


def outer_sum(left, right):
    return lax.dot_general(
        left, right, (((0,), (0,)), ((), ())), preferred_element_type=jnp.float32
    )


def back_product(grad, weight):
    return lax.dot_general(grad, weight, NT, preferred_element_type=jnp.float32)


def norm_forward(values, gain, shift):
    centre = values - jnp.mean(values, axis=-1, keepdims=True)
    scale = lax.rsqrt(jnp.mean(centre * centre, axis=-1, keepdims=True) + epsilon)
    unit = centre * scale
    return (unit * gain + shift, unit, scale)


def norm_backward(grad, unit, scale, gain):
    grad_gain = jnp.sum(grad * unit, axis=0)
    grad_shift = jnp.sum(grad, axis=0)
    inner = grad * gain
    grad_in = scale * (
        inner
        - jnp.mean(inner, axis=-1, keepdims=True)
        - unit * jnp.mean(inner * unit, axis=-1, keepdims=True)
    )
    return (grad_in, grad_gain, grad_shift)


def gelu_pair(values):
    cumulative = 0.5 * (1.0 + lax.erf(values * 0.7071067811865476))
    density = jnp.exp(-0.5 * values * values) * 0.3989422804014327
    return (values * cumulative, cumulative + values * density)


def swap(array, axis, bit):
    size = lax.axis_size(axis)
    return lax.ppermute(array, axis, [(i, i ^ bit) for i in range(size)])


K_BLOCK = (0, 0, 1)
V_BLOCK = (2, 2, 1)
K_UPPER = (False, True, True)
V_UPPER = (False, True, False)


def lane_half(array, upper):
    lane = lax.broadcasted_iota(jnp.int32, array.shape, 1)
    keep = (lane >= 64) if upper else (lane < 64)
    return jnp.where(keep, array, jnp.zeros_like(array))


def piece_copies(where, ids, pieces, kv, sem, rows, classes):
    copies = []
    for piece, (mask, flips) in zip(pieces, where):
        for slot, flip in enumerate(flips):
            chunk = (ids[0] ^ flip) * classes + (ids[1] ^ mask)
            start = pl.multiple_of(chunk * rows, 64)
            copies.append(
                pltpu.make_async_copy(
                    piece.at[slot], kv.at[pl.ds(start, rows), :], sem.at[len(copies)]
                )
            )
    return copies


def allowed(spans, base, start):
    position = lax.broadcasted_iota(jnp.int32, (KTILE, QTILE), 0)
    first = spans[0:1, pl.ds(base, QTILE)] - start
    last = spans[1:2, pl.ds(base, QTILE)] - start
    return (position >= first) & (position < last)


def walk(steps, tiles, j, fetch, work):
    amount = steps[j * (tiles + 1)]

    def tile(i):
        index = steps[j * (tiles + 1) + 1 + jnp.minimum(i, amount - 1)]
        start = pl.multiple_of(index * KTILE, KTILE)
        return start, jnp.where(i < amount, start, -(1 << 24))

    fetch(0, tile(0)[0])

    @pl.loop(0, (amount + 1) // 2)
    def _(i):
        here, there, later = tile(2 * i), tile(2 * i + 1), tile(2 * i + 2)
        fetch(1, there[0])
        work(0, *here)
        fetch(0, later[0])
        work(1, *there)


def forward_kernel(where, rows, classes, ids, flags, q, spans, *rest):
    count = len(where)
    pieces = rest[:count]
    o_low, o_full, lse, kv, vt, qm, top, total, accum, first, second, sem = rest[count:]
    length = kv.shape[0]
    tiles = length // KTILE
    copies = piece_copies(where, ids, pieces, kv, sem, rows, classes)
    for copy in copies:
        copy.start()
    for copy in copies:
        copy.wait()

    @pl.loop(0, tiles)
    def _(t):
        start = pl.multiple_of(t * KTILE, KTILE)
        vt[0:128, pl.ds(start, KTILE)] = kv[pl.ds(start, KTILE), 128:256].T
        vt[128:256, pl.ds(start, KTILE)] = kv[pl.ds(start, KTILE), 256:384].T

    v_row = (128, 192, 0)

    @pl.loop(0, q.shape[0] // QTILE)
    def _(j):
        base = pl.multiple_of(j * QTILE, QTILE)
        for head in range(OWN):
            block = q[pl.ds(base, QTILE), pl.ds(128 * K_BLOCK[head], 128)]
            qm[head] = lane_half(block, K_UPPER[head])
        top[...] = jnp.full_like(top, masked_value)
        total[...] = jnp.zeros_like(total)
        accum[...] = jnp.zeros_like(accum)

        stages = (first, second)

        def fetch(stage, start):
            for head in range(OWN):
                block = 128 * K_BLOCK[head]
                stages[stage][head] = lax.dot_general(
                    kv[pl.ds(start, KTILE), block : block + 128],
                    qm[head],
                    NT,
                    preferred_element_type=jnp.float32,
                )

        def work(stage, start, position):
            same = allowed(spans, base, position)
            for head in range(OWN):
                scores = jnp.where(same, stages[stage][head], masked_value)
                old = top[head : head + 1, :]
                new = jnp.maximum(old, jnp.max(scores, axis=0, keepdims=True))
                weights = jnp.exp(scores - new)
                factor = jnp.exp(old - new)
                top[head : head + 1, :] = new
                total[head : head + 1, :] = total[head : head + 1, :] * factor + jnp.sum(
                    weights, axis=0, keepdims=True
                )
                rows_v = slice(v_row[head], v_row[head] + 64)
                place = slice(64 * head, 64 * head + 64)
                accum[place, :] = accum[place, :] * factor + jnp.dot(
                    vt[rows_v, pl.ds(start, KTILE)],
                    weights.astype(jnp.bfloat16),
                    preferred_element_type=jnp.float32,
                )

        walk(flags, tiles, j, fetch, work)
        outs = [
            accum[64 * head : 64 * head + 64, :] / total[head : head + 1, :] for head in range(OWN)
        ]
        lower = jnp.concatenate(outs[:2], axis=0).T
        upper = jnp.concatenate([outs[2], jnp.zeros_like(outs[2])], axis=0).T
        o_full[pl.ds(base, QTILE), 0:128] = lower
        o_full[pl.ds(base, QTILE), 128:256] = upper
        o_low[pl.ds(base, QTILE), 0:128] = lower.astype(jnp.bfloat16)
        o_low[pl.ds(base, QTILE), 128:192] = upper[:, 0:64].astype(jnp.bfloat16)
        lse[:, pl.ds(base, QTILE)] = top[...] + jnp.log(total[...])


def backward_kernel(where, rows, classes, out_where, extra, ids, flags, q, spans, grad, o_full, lse, *rest):
    count = len(where)
    pieces = rest[:count]
    rest = rest[count + extra :]
    outs = rest[: len(out_where)]
    dq, kv, kt, qm, dom, stats, dqt, dkv, low_kv, sem = rest[len(out_where) :]
    length = kv.shape[0]
    tiles = length // KTILE
    copies = piece_copies(where, ids, pieces, kv, sem, rows, classes)
    for copy in copies:
        copy.start()

    @pl.loop(0, tiles)
    def _(t):
        start = pl.multiple_of(t * KTILE, KTILE)
        dkv[pl.ds(start, KTILE), :] = jnp.zeros((KTILE, 384), jnp.float32)

    for copy in copies:
        copy.wait()

    @pl.loop(0, tiles)
    def _(t):
        start = pl.multiple_of(t * KTILE, KTILE)
        kt[0:128, pl.ds(start, KTILE)] = kv[pl.ds(start, KTILE), 0:128].T
        kt[128:256, pl.ds(start, KTILE)] = kv[pl.ds(start, KTILE), 128:256].T

    k_row = (0, 64, 192)

    @pl.loop(0, q.shape[0] // QTILE)
    def _(j):
        base = pl.multiple_of(j * QTILE, QTILE)
        for head in range(OWN):
            block = q[pl.ds(base, QTILE), pl.ds(128 * K_BLOCK[head], 128)]
            qm[head] = lane_half(block, K_UPPER[head])
            block = grad[pl.ds(base, QTILE), pl.ds(128 * (2 - V_BLOCK[head]), 128)]
            dom[head] = lane_half(block, V_UPPER[head])
        for part in range(2):
            product = (
                grad[pl.ds(base, QTILE), 128 * part : 128 * part + 128].astype(jnp.float32)
                * o_full[pl.ds(base, QTILE), 128 * part : 128 * part + 128]
            ).T
            for half in range(2):
                head = 2 * part + half
                if head < OWN:
                    stats[head : head + 1, :] = jnp.sum(
                        product[64 * half : 64 * half + 64], axis=0, keepdims=True
                    )
        dqt[...] = jnp.zeros_like(dqt)

        def product(place, block, right):
            left = kv[place, 128 * block : 128 * block + 128]
            return lax.dot_general(left, right, NT, preferred_element_type=jnp.float32)

        @pl.loop(0, flags[j * (tiles + 1)])
        def _(i):
            start = pl.multiple_of(flags[j * (tiles + 1) + 1 + i] * KTILE, KTILE)
            place = pl.ds(start, KTILE)
            same = allowed(spans, base, start)
            sums = [None, None, None]

            def add(block, left, right):
                term = jnp.dot(left, right, preferred_element_type=jnp.float32)
                sums[block] = term if sums[block] is None else sums[block] + term

            for head in range(OWN):
                scores = product(place, K_BLOCK[head], qm[head])
                grad_probs = product(place, V_BLOCK[head], dom[head])
                probs = jnp.where(
                    same, jnp.exp(scores - lse[head : head + 1, pl.ds(base, QTILE)]), 0.0
                )
                grad_scores = (probs * (grad_probs - stats[head : head + 1, :])).astype(jnp.bfloat16)
                add(V_BLOCK[head], probs.astype(jnp.bfloat16), dom[head])
                add(K_BLOCK[head], grad_scores, qm[head])
                rows_k = slice(k_row[head], k_row[head] + 64)
                dqt[64 * head : 64 * head + 64, :] += jnp.dot(
                    kt[rows_k, place], grad_scores, preferred_element_type=jnp.float32
                )
            for block in range(3):
                dkv[place, 128 * block : 128 * block + 128] += sums[block]

        lower = dqt[0:128, :].T * 0.125
        upper = dqt[64:192, :].T * 0.125
        dq[pl.ds(base, QTILE), 0:128] = lower.astype(jnp.bfloat16)
        dq[pl.ds(base, QTILE), 128:192] = upper[:, 64:128].astype(jnp.bfloat16)

    @pl.loop(0, tiles)
    def _(t):
        start = pl.multiple_of(t * KTILE, KTILE)
        low_kv[pl.ds(start, KTILE), :] = dkv[pl.ds(start, KTILE), :].astype(jnp.bfloat16)

    copies = []
    for out, masks in zip(outs, out_where):
        for slot, mask in enumerate(masks):
            for flip in range(GROUPS):
                chunk = (ids[0] ^ flip) * classes + (ids[1] ^ mask)
                start = pl.multiple_of(chunk * rows, 64)
                copies.append(
                    pltpu.make_async_copy(
                        low_kv.at[pl.ds(start, rows), :], out.at[slot, flip], sem.at[len(copies)]
                    )
                )
    for copy in copies:
        copy.start()
    for copy in copies:
        copy.wait()


VMEM_SPEC = pl.BlockSpec(memory_space=pltpu.VMEM)
SMEM_SPEC = pl.BlockSpec(memory_space=pltpu.SMEM)
ANY_SPEC = pl.BlockSpec(memory_space=pl.ANY)
PARAMS = pltpu.CompilerParams(vmem_limit_bytes=56 * 1024 * 1024)


def attend_forward(ids, flags, q, spans, pieces, where, rows, classes):
    length = rows * classes * GROUPS
    queries = q.shape[0]
    copies = sum(len(flips) for _, flips in where)
    return pl.pallas_call(
        functools.partial(forward_kernel, where, rows, classes),
        out_shape=(
            jax.ShapeDtypeStruct((queries, WIDTH), jnp.bfloat16),
            jax.ShapeDtypeStruct((queries, 256), jnp.float32),
            jax.ShapeDtypeStruct((8, queries), jnp.float32),
        ),
        in_specs=[SMEM_SPEC, SMEM_SPEC, VMEM_SPEC, VMEM_SPEC]
        + [ANY_SPEC] * len(pieces),
        out_specs=(VMEM_SPEC,) * 3,
        scratch_shapes=[
            pltpu.VMEM((length, 384), jnp.bfloat16),
            pltpu.VMEM((256, length), jnp.bfloat16),
            pltpu.VMEM((OWN, QTILE, 128), jnp.bfloat16),
            pltpu.VMEM((8, QTILE), jnp.float32),
            pltpu.VMEM((8, QTILE), jnp.float32),
            pltpu.VMEM((WIDTH, QTILE), jnp.float32),
            pltpu.VMEM((OWN, KTILE, QTILE), jnp.float32),
            pltpu.VMEM((OWN, KTILE, QTILE), jnp.float32),
            pltpu.SemaphoreType.DMA((copies,)),
        ],
        compiler_params=PARAMS,
        cost_estimate=pl.CostEstimate(
            flops=queries * length * WIDTH * 4, bytes_accessed=8 << 20, transcendentals=0
        ),
        name="attend_forward",
    )(ids, flags, q, spans, *pieces)


def attend_backward(
    ids, flags, q, spans, grad, o_full, lse, pieces, after, where, rows, classes, out_where
):
    length = rows * classes * GROUPS
    queries = q.shape[0]
    copies = sum(len(flips) for _, flips in where)
    return pl.pallas_call(
        functools.partial(backward_kernel, where, rows, classes, out_where, len(after)),
        out_shape=tuple(
            jax.ShapeDtypeStruct((len(masks), GROUPS, rows, 384), jnp.bfloat16)
            for masks in out_where
        )
        + (jax.ShapeDtypeStruct((queries, WIDTH), jnp.bfloat16),),
        in_specs=[SMEM_SPEC, SMEM_SPEC] + [VMEM_SPEC] * 5 + [ANY_SPEC] * (len(pieces) + len(after)),
        out_specs=(ANY_SPEC,) * len(out_where) + (VMEM_SPEC,),
        scratch_shapes=[
            pltpu.VMEM((length, 384), jnp.bfloat16),
            pltpu.VMEM((256, length), jnp.bfloat16),
            pltpu.VMEM((OWN, QTILE, 128), jnp.bfloat16),
            pltpu.VMEM((OWN, QTILE, 128), jnp.bfloat16),
            pltpu.VMEM((8, QTILE), jnp.float32),
            pltpu.VMEM((WIDTH, QTILE), jnp.float32),
            pltpu.VMEM((length, 384), jnp.float32),
            pltpu.VMEM((length, 384), jnp.bfloat16),
            pltpu.SemaphoreType.DMA((copies,)),
        ],
        compiler_params=PARAMS,
        cost_estimate=pl.CostEstimate(
            flops=queries * length * WIDTH * 10, bytes_accessed=16 << 20, transcendentals=0
        ),
        name="attend_backward",
    )(ids, flags, q, spans, grad, o_full, lse, *pieces, *after)


def tn(left, right):
    return lax.dot_general(
        left, right, (((0,), (0,)), ((), ())), preferred_element_type=jnp.float32
    )


def down_grad_kernel(extra, active, g_low, *rest):
    down = rest[extra]

    @pl.loop(0, 8)
    def _(i):
        part = tn(active[:, pl.ds(pl.multiple_of(i * 384, 128), 384)], g_low[...])
        down[pl.ds(pl.multiple_of(i * 384, 16), 384), :] = part.astype(jnp.bfloat16)


def down_grad(active, g_low, after):
    return pl.pallas_call(
        functools.partial(down_grad_kernel, len(after)),
        out_shape=jax.ShapeDtypeStruct((FF, D), jnp.bfloat16),
        in_specs=[VMEM_SPEC] * 2 + [ANY_SPEC] * len(after),
        out_specs=VMEM_SPEC,
        compiler_params=PARAMS,
        cost_estimate=pl.CostEstimate(
            flops=2 * active.shape[0] * D * FF, bytes_accessed=8 << 20, transcendentals=0
        ),
        name="down_grad",
    )(active, g_low, *after)


def upper_grad_kernel(extra, ids, hid, g_raised, attn, g_att, vec, *rest):
    upper = rest[extra]
    x, c, m, h = ids[0], ids[1], ids[2], ids[3]

    @pl.loop(0, 2)
    def _(i):
        left = hid[:, pl.ds(pl.multiple_of(i * 384, 128), 384)]
        attn_left = attn[:, pl.ds(pl.multiple_of(i * 384, 128), 384)]

        @pl.loop(0, 2)
        def _(j):
            outer = tn(attn_left, g_att[:, pl.ds(pl.multiple_of(j * 384, 128), 384)]).astype(jnp.bfloat16)

            for k in range(4):
                unit = j * 4 + k
                part = tn(left, g_raised[:, pl.ds(pl.multiple_of(unit * 384, 128), 384)]).astype(jnp.bfloat16)
                for b in range(2):
                    place = (((b ^ c) * 2 + (j ^ m)) * 2 + (i ^ x)) * 4 + (k ^ h)
                    upper[place, 0:192, :] = part[192 * b : 192 * b + 192]
                    upper[place, 192:240, :] = outer[192 * b + 48 * k : 192 * b + 48 * k + 48]
                    upper[place, 240:256, :] = vec[unit]


def upper_grad(ids, hid, g_raised, attn, g_att, vec, after):
    return pl.pallas_call(
        functools.partial(upper_grad_kernel, len(after)),
        out_shape=jax.ShapeDtypeStruct((32, 256, 384), jnp.bfloat16),
        in_specs=[SMEM_SPEC] + [VMEM_SPEC] * 5 + [ANY_SPEC] * len(after),
        out_specs=VMEM_SPEC,
        compiler_params=PARAMS,
        cost_estimate=pl.CostEstimate(
            flops=2 * hid.shape[0] * D * (FF + D), bytes_accessed=12 << 20, transcendentals=0
        ),
        name="upper_grad",
    )(ids, hid, g_raised, attn, g_att, vec, *after)


def unpack_ffn_kernel(ids, block, up, out, vec):
    up[...] = block[0, 0:192, :].astype(jnp.float32)
    out[...] = block[0, 192:240, :].astype(jnp.float32)
    vec[0] = block[0, 240:256, :].astype(jnp.float32)


def unpack_ffn(ids, pieces):
    def source(b, u, ids):
        j, k = u // 4, u % 4
        return (((b ^ ids[1]) * 2 + (j ^ ids[2])) * 4 + (k ^ ids[3]), 0, 0)

    return pl.pallas_call(
        unpack_ffn_kernel,
        out_shape=(
            jax.ShapeDtypeStruct((384, FF), jnp.float32),
            jax.ShapeDtypeStruct((384, D), jnp.float32),
            jax.ShapeDtypeStruct((8, 16, 384), jnp.float32),
        ),
        grid_spec=pltpu.PrefetchScalarGridSpec(
            num_scalar_prefetch=1,
            grid=(2, 8),
            in_specs=[pl.BlockSpec((1, 256, 384), source)],
            out_specs=(
                pl.BlockSpec((192, 384), lambda b, u, ids: (b, u)),
                pl.BlockSpec((48, 384), lambda b, u, ids: (b * 4 + u % 4, u // 4)),
                pl.BlockSpec((1, 16, 384), lambda b, u, ids: (u, 0, 0)),
            ),
        ),
        name="unpack_ffn",
    )(ids, pieces)


def qkv_grad_kernel(ids, tokens, dkv, dq, out):
    x, c = ids[0], ids[1]
    total = jnp.concatenate(
        [
            jnp.sum(dkv[...].astype(jnp.float32), axis=0, keepdims=True),
            jnp.sum(dq[...].astype(jnp.float32), axis=0, keepdims=True),
        ],
        axis=1,
    )
    first = lax.broadcasted_iota(jnp.int32, (16, 576), 0) == 0
    total = jnp.where(first, jnp.broadcast_to(total, (16, 576)), 0.0).astype(jnp.bfloat16)

    @pl.loop(0, 2)
    def _(i):
        left = tokens[:, pl.ds(pl.multiple_of(i * 384, 128), 384)]
        for right, low_lane, high_lane in ((dkv, 0, 384), (dq, 384, 576)):
            part = lax.dot_general(
                left, right[...], (((0,), (0,)), ((), ())), preferred_element_type=jnp.float32
            ).astype(jnp.bfloat16)
            for b in range(2):
                out[(b ^ c) * 2 + (i ^ x), 0:192, low_lane:high_lane] = part[192 * b : 192 * b + 192]
        for b in range(2):
            out[(b ^ c) * 2 + (i ^ x), 192:208, :] = total


def qkv_grads(ids, tokens, dkv, dq):
    return pl.pallas_call(
        qkv_grad_kernel,
        out_shape=jax.ShapeDtypeStruct((4, 208, 576), jnp.bfloat16),
        in_specs=[SMEM_SPEC] + [VMEM_SPEC] * 3,
        out_specs=VMEM_SPEC,
        compiler_params=PARAMS,
        cost_estimate=pl.CostEstimate(
            flops=2 * tokens.shape[0] * D * 576, bytes_accessed=4 << 20, transcendentals=0
        ),
        name="qkv_grads",
    )(ids, tokens, dkv, dq)


def unpack_qkv_kernel(ids, pieces, out_q, out_k, out_v, vec):
    c, h = ids[1], ids[3]
    for b in range(2):
        q, k, v = [], [], []
        for g in range(GROUPS):
            block = pieces[(b ^ c) * 4 + (g ^ h), 0:192, :].astype(jnp.float32)
            k += [block[:, 0:128], block[:, 192:256]]
            v += [block[:, 256:384], block[:, 128:192]]
            q += [block[:, 384:576]]
        for out, parts in ((out_q, q), (out_k, k), (out_v, v)):
            out[192 * b : 192 * b + 192, :] = jnp.concatenate(parts, axis=1)
    for g in range(GROUPS):
        vec[g] = pieces[c * 4 + (g ^ h), 192:208, :].astype(jnp.float32)


def unpack_qkv(ids, pieces):
    return pl.pallas_call(
        unpack_qkv_kernel,
        out_shape=(jax.ShapeDtypeStruct((384, D), jnp.float32),) * 3
        + (jax.ShapeDtypeStruct((GROUPS, 16, 576), jnp.float32),),
        in_specs=[SMEM_SPEC, VMEM_SPEC],
        out_specs=(VMEM_SPEC,) * 4,
        compiler_params=PARAMS,
        name="unpack_qkv",
    )(ids, pieces)


def token_grad_kernel(base, kv0, kv1, kv2, kv3, q0, q1, q2, q3, w_kv, w_q, out):
    total = base[...]
    for i, (kv, q) in enumerate(((kv0, q0), (kv1, q1), (kv2, q2), (kv3, q3))):
        total = total + lax.dot_general(kv[...], w_kv[i], NT, preferred_element_type=jnp.float32)
        total = total + lax.dot_general(q[...], w_q[i], NT, preferred_element_type=jnp.float32)
    out[...] = total


def token_grads(base, kv, q, w_kv, w_q):
    return pl.pallas_call(
        token_grad_kernel,
        out_shape=jax.ShapeDtypeStruct(base.shape, jnp.float32),
        in_specs=[VMEM_SPEC] * 11,
        out_specs=VMEM_SPEC,
        compiler_params=PARAMS,
        cost_estimate=pl.CostEstimate(
            flops=2 * base.shape[0] * D * 2304, bytes_accessed=8 << 20, transcendentals=0
        ),
        name="token_grads",
    )(base, *kv, *q, w_kv, w_q)


def gather_rows(weight, core):
    half = weight.shape[0] // 2
    part = lax.dynamic_slice_in_dim(weight, core * half, half, 0)
    return lax.all_gather(part, ("wa", "c"), axis=0, tiled=True)


def reduce_blocks(grad):
    flat = grad.reshape((-1,) + grad.shape[2:])
    mine = lax.psum_scatter(flat, ("wa", "c"), scatter_dimension=0, tiled=True)
    mine = lax.psum_scatter(mine, "m", scatter_dimension=0, tiled=True)
    mine = lax.psum_scatter(mine, "h", scatter_dimension=0, tiled=True)
    return lax.all_gather(mine, ("c", "m", "h"), axis=0, tiled=True)


def tie(array, *others):
    return lax.optimization_barrier((array,) + others)[0]


def halve(array, axis, bit):
    return array[0], swap(array[1], axis, bit)


def both_sum(near, far, *others):
    near = tie(near, *others)
    return low(widen(near) + widen(far))


def double(array, axis, bit):
    return jnp.concatenate([array, swap(array, axis, bit)], axis=0)


def reduce_rest(grad):
    mine = lax.psum_scatter(grad, "h", scatter_dimension=0, tiled=True)
    mine = lax.psum_scatter(mine, "m", scatter_dimension=0, tiled=True)
    return lax.all_gather(mine, ("c", "h", "m"), axis=0, tiled=True)


def pick_columns(weight, group):
    q, k, v = (lax.dynamic_slice_in_dim(w, group * WIDTH, WIDTH, w.ndim - 1) for w in weight)
    return jnp.concatenate(
        [
            k[..., :128],
            v[..., 128:],
            k[..., 128:],
            v[..., :128],
            q[..., :128],
            jnp.zeros_like(q[..., :64]),
            q[..., 128:],
        ],
        axis=-1,
    )


def per_device(
    tokens,
    segment_ids,
    cotangent,
    w_query,
    w_key,
    w_value,
    w_out,
    w_up,
    w_down,
    b_query,
    b_value,
    b_out,
    gain_one,
    shift_one,
    b_up,
    b_down,
    gain_two,
    shift_two,
):
    mid = lax.axis_size("m")
    wide = lax.axis_size("wa")
    paired = mid == 2 and wide == 2
    classes = 2 * mid
    group = lax.axis_index("h")
    core = lax.axis_index("c")
    kind = lax.axis_index("m") * 2 + core
    side = lax.axis_index("wa")
    inputs = tokens[0]
    count = inputs.shape[0]
    chunks = GROUPS * classes
    length = count * chunks
    tiles = length // KTILE
    ids = jnp.stack([group, kind]).astype(jnp.int32)
    place_ids = jnp.stack([side, core, lax.axis_index("m"), group]).astype(jnp.int32)
    order = group ^ jnp.arange(GROUPS)

    second = swap(inputs, "h", 1)
    third = swap(inputs, "h", 2)
    w_part = pick_columns((w_query, w_key, w_value), group)
    w_other = swap(w_part, "wa", 1) if wide == 2 else lax.all_gather(w_part, "wa", axis=0, tiled=True)

    segs = segment_ids
    segs = double(segs, "c", 1)
    bit = 1
    while bit < mid:
        segs = double(segs, "m", bit)
        bit *= 2
    segs = double(double(segs, "h", 1), "h", 2)

    smalls = [b_query, b_value, b_out, gain_one, shift_one, b_up, b_down, gain_two, shift_two]
    joined = lax.all_gather(jnp.concatenate(smalls), "wa", axis=0)
    second, third, w_other, segs, joined = lax.optimization_barrier(
        (second, third, w_other, segs, joined)
    )
    fourth = swap(third, "h", 1)
    if wide == 2:
        w_group = jnp.where(
            side == 0,
            jnp.concatenate([w_part, w_other], axis=0),
            jnp.concatenate([w_other, w_part], axis=0),
        )
    else:
        w_group = w_other
    own_segs = segs.reshape(GROUPS, classes, count)[:, 0].reshape(-1)
    segs = jnp.take(segs, (group * classes + kind) ^ jnp.arange(chunks), axis=0)
    full, place = [], 0
    for item in smalls:
        size = item.shape[0]
        full.append(widen(joined[:, place : place + size].reshape(-1)))
        place += size
    bias_query, bias_value, bias_out, gain_attn, shift_attn, bias_up, bias_down, gain_ffn, shift_ffn = full
    b_group = pick_columns((bias_query, jnp.zeros_like(bias_query), bias_value), group)

    w_group, w_out, w_up, w_down, w_query, w_key, w_value = lax.optimization_barrier(
        (w_group, w_out, w_up, w_down, w_query, w_key, w_value)
    )
    full_out = gather_rows(w_out, core)
    full_up = gather_rows(w_up, core)
    full_down = gather_rows(w_down, core)
    by_group = jnp.concatenate(
        [
            jnp.concatenate(
                [
                    w_key[:, 192 * g : 192 * g + 128],
                    w_value[:, 192 * g + 128 : 192 * g + 192],
                    w_key[:, 192 * g + 128 : 192 * g + 192],
                    w_value[:, 192 * g : 192 * g + 128],
                ],
                axis=1,
            )
            for g in range(GROUPS)
        ]
        + [w_query],
        axis=1,
    )
    by_group = gather_rows(by_group, core)
    back_kv = jnp.take(
        jnp.transpose(by_group[:, : 2 * D].reshape(D, GROUPS, 2 * WIDTH), (1, 0, 2)), order, axis=0
    )
    back_q = jnp.take(
        jnp.transpose(by_group[:, 2 * D :].reshape(D, GROUPS, WIDTH), (1, 0, 2)), order, axis=0
    )

    names = jnp.arange(DOCS)
    begins = jnp.sum((segs.reshape(-1, 1) < names).astype(jnp.int32), axis=0)
    ends = jnp.sum((segs.reshape(-1, 1) <= names).astype(jnp.int32), axis=0)
    chosen = own_segs[None, :] == names[:, None]
    begins = jnp.sum(jnp.where(chosen, begins[:, None], 0), axis=0)
    ends = jnp.sum(jnp.where(chosen, ends[:, None], 0), axis=0)
    spans = jnp.concatenate(
        [begins[None], ends[None], jnp.zeros((6, begins.shape[0]), jnp.int32)], axis=0
    )
    edges = (jnp.arange(tiles) * KTILE)[None, :, None]
    meets = (begins.reshape(-1, 1, QTILE) < edges + KTILE) & (ends.reshape(-1, 1, QTILE) > edges)
    meets = jnp.any(meets, axis=-1).astype(jnp.int32)
    rank = jnp.cumsum(meets, axis=1)
    slots = (rank[:, None, :] == jnp.arange(1, tiles + 1)[None, :, None]) & (meets[:, None, :] > 0)
    listed = jnp.sum(jnp.where(slots, jnp.arange(tiles), 0), axis=-1)
    flags = jnp.concatenate([rank[:, -1:], listed], axis=1).astype(jnp.int32).reshape(-1)

    def project(parts):
        joined = jnp.concatenate(parts, axis=0)
        kv = low(mm(joined, w_group[:, :384]) + b_group[:384])
        return kv.reshape(len(parts), count, 384)

    where, pieces = [], []

    def spread(piece, flips):
        have = {0: piece}
        bit = 1
        while bit < mid:
            for mask in list(have):
                have[mask | (bit << 1)] = swap(have[mask], "m", bit)
            bit *= 2
        for mask in list(have):
            have[mask | 1] = swap(have[mask], "c", 1)
        for mask, item in have.items():
            where.append((mask, flips))
            pieces.append(item)

    def queries(rows):
        return low(mm(rows, w_group[:, 384:]) + b_group[384:]) * jnp.bfloat16(0.125)

    first_kv = project((inputs, second, third))
    spread(first_kv, (0, 1, 2))
    first_q = queries(tie(jnp.concatenate([inputs, second, third], axis=0), first_kv))
    fourth, first_q, spans, flags = lax.optimization_barrier((fourth, first_q, spans, flags))
    last_kv = project((fourth,))
    spread(last_kv, (3,))
    where = tuple(where)
    last_q = queries(tie(fourth, last_kv))
    q_rows = jnp.concatenate([first_q, last_q], axis=0)
    group_tokens = jnp.concatenate([inputs, second, third, fourth], axis=0)

    o_low, o_full, lse = attend_forward(
        ids, flags, q_rows, spans, pieces, where, count, classes
    )

    def send_back(rows):
        parts = rows.reshape(GROUPS, count, -1)
        return [parts[0]] + [swap(parts[flip], "h", flip) for flip in range(1, GROUPS)]

    def in_order(parts):
        return jnp.take(jnp.stack(parts), order, axis=0)

    attn_low = jnp.transpose(in_order(send_back(o_low)), (1, 0, 2)).reshape(count, D)
    attended = mm(attn_low, full_out) + bias_out
    hidden, unit_one, scale_one = norm_forward(widen(inputs) + attended, gain_attn, shift_attn)
    hidden_low = low(hidden)
    raised = mm(hidden_low, full_up) + bias_up
    active, slope = gelu_pair(raised)
    active_low = low(active)
    lowered = mm(active_low, full_down) + bias_down
    result, unit_two, scale_two = norm_forward(hidden + lowered, gain_ffn, shift_ffn)
    grad_sum_two, grad_gain_two, grad_shift_two = norm_backward(
        widen(cotangent[0]), unit_two, scale_two, gain_ffn
    )
    grad_lowered = low(grad_sum_two)
    grad_b_down = jnp.sum(widen(grad_lowered), axis=0)
    grad_raised = low(back_product(grad_lowered, full_down) * slope)
    grad_b_up = jnp.sum(widen(grad_raised), axis=0)
    grad_hidden = grad_sum_two + back_product(grad_raised, full_up)
    grad_sum_one, grad_gain_one, grad_shift_one = norm_backward(
        grad_hidden, unit_one, scale_one, gain_attn
    )
    grad_attended = low(grad_sum_one)
    grad_b_out = jnp.sum(widen(grad_attended), axis=0)
    grad_attn = low(back_product(grad_attended, full_out))

    grad_parts = jnp.take(
        jnp.transpose(grad_attn.reshape(count, GROUPS, WIDTH), (1, 0, 2)), order, axis=0
    )
    grad_heads = [grad_parts[0]] + [swap(grad_parts[flip], "h", flip) for flip in range(1, GROUPS)]
    grad_rows = jnp.pad(jnp.concatenate(grad_heads, axis=0), ((0, 0), (0, 64)))

    vectors = jnp.concatenate(
        [grad_b_out, grad_gain_one, grad_shift_one, grad_b_down, grad_gain_two, grad_shift_two, grad_b_up]
    )
    blocks = 2 * wide
    if paired:
        vectors = jnp.pad(low(vectors), (0, 9216 - 7680)).reshape(8, 3, 384)
        vectors = jnp.pad(vectors, ((0, 0), (0, 13), (0, 0)))
        upper = upper_grad(
            place_ids, hidden_low, grad_raised, attn_low, grad_attended, vectors, (grad_parts, by_group)
        )
        upper = upper.reshape(2, 2, 2, 2, 2, 256, 384)
        near, far = halve(upper, "c", 1)
        down_sum = down_grad(active_low, grad_lowered, (upper,))
        upper = both_sum(near, far, down_sum)
        down_sum = lax.psum_scatter(down_sum, ("wa", "c"), scatter_dimension=0, tiled=True)
        upper_pair = halve(upper, "m", 1)
        after = (upper,)
    else:
        grad_w_down = low(outer_sum(active_low, grad_lowered))
        grad_w_up = low(outer_sum(hidden_low, grad_raised))
        grad_w_out = low(outer_sum(attn_low, grad_attended))
        vectors = jnp.pad(low(vectors).reshape(-1, D), ((0, 6), (0, 0)))
        down_rows, out_rows = FF // blocks, D // blocks
        ffn = jnp.concatenate(
            [
                grad_w_down.reshape(blocks, down_rows, D),
                grad_w_up.reshape(blocks, down_rows, D),
                grad_w_out.reshape(blocks, out_rows, D),
                jnp.broadcast_to(vectors[None], (blocks, 16, D)),
            ],
            axis=1,
        )
        after = ()
        ffn_sum = reduce_blocks(ffn).reshape(2, -1, D)
        out_down = widen(ffn_sum[:, :down_rows]).reshape(-1, D)
        out_up = widen(ffn_sum[:, down_rows : 2 * down_rows]).reshape(-1, FF)
        place = 2 * down_rows
        out_out = widen(ffn_sum[:, place : place + out_rows]).reshape(-1, D)
        small = widen(ffn_sum[0, place + out_rows :])

    def share(row, rows):
        vector = small[row : row + rows].reshape(-1)
        size = vector.shape[0] // wide
        return lax.dynamic_slice_in_dim(vector, side * size, size, 0)

    keep, give = tuple(range(0, classes, 2)), tuple(range(1, classes, 2))
    kept, given, dq = attend_backward(
        ids, flags, q_rows, spans, grad_rows, o_full, lse,
        pieces, after, where, count, classes, (keep, give),
    )

    given = swap(given, "c", 1)
    if paired:
        out_down = widen(reduce_rest(tie(down_sum, dq)))
        upper = both_sum(*upper_pair, dq)
        upper_pair = halve(upper, "wa", 1)
        kept = tie(kept, upper)
    partial = widen(kept) + widen(given)
    stay = list(keep)
    bit = mid // 2
    while bit >= 1:
        mask = bit << 1
        near = [i for i, m in enumerate(stay) if not m & mask]
        far = [i for i, m in enumerate(stay) if m & mask]
        sent = swap(low(partial[far[0] : far[-1] + 1]), "m", bit)
        partial = low(partial[near[0] : near[-1] + 1])
        if paired:
            back_q_parts = send_back(tie(dq, partial))
            upper = both_sum(*upper_pair, partial)
            upper_pair = halve(upper, "h", 2)
            partial = tie(partial, upper)
        partial = widen(partial) + widen(sent)
        stay = [stay[i] for i in near]
        bit //= 2
    if not paired:
        back_q_parts = send_back(dq)
    dkv = low(partial[0]).reshape(GROUPS * count, 384)
    back_kv_parts = send_back(dkv)

    part = D // wide
    if paired:
        qkv = qkv_grads(place_ids, group_tokens, dkv, dq)
        qkv_pair = halve(qkv.reshape(2, 2, 208, 576), "c", 1)
        upper = both_sum(*upper_pair, qkv)
        upper_pair = halve(upper, "h", 1)
        qkv = both_sum(*qkv_pair, upper)
        qkv_pair = halve(qkv, "wa", 1)
        upper = both_sum(*upper_pair, qkv)
        other = swap(upper, "h", 1)
        qkv = both_sum(*qkv_pair, upper)
        qkv_other = swap(qkv, "m", 1)
        upper = jnp.stack([tie(upper, qkv), other])
        other = swap(upper, "h", 2)
        qkv = both_sum(qkv, qkv_other, upper)
        qkv_other = swap(qkv, "h", 1)
        upper = jnp.concatenate([tie(upper, qkv), other], axis=0)
        other = swap(upper, "m", 1)
        qkv = jnp.stack([tie(qkv, upper), qkv_other])
        qkv_other = swap(qkv, "h", 2)
        grad_inputs = token_grads(
            tie(grad_sum_one, qkv), back_kv_parts, back_q_parts, back_kv, back_q
        )
        qkv = jnp.concatenate([tie(qkv, grad_inputs), qkv_other], axis=0)
        qkv_other = swap(qkv, "c", 1)
        upper = jnp.concatenate([tie(upper, qkv), other], axis=0)
        other = swap(upper, "c", 1)
        out_query, out_key, out_value, sums = unpack_qkv(
            place_ids, jnp.concatenate([tie(qkv, upper), qkv_other], axis=0)
        )
        sums = sums[:, 0]
        sums_v = jnp.concatenate([sums[:, 256:384], sums[:, 128:192]], axis=1).reshape(-1)
        sums_q = sums[:, 384:576].reshape(-1)
        upper = jnp.concatenate([tie(upper, out_query), other], axis=0)
        out_up, out_out, small = unpack_ffn(place_ids, upper)
        small = small[:, :3].reshape(-1)[:7680].reshape(10, D)
    else:
        both = jnp.concatenate([dkv, dq], axis=1)
        width = both.shape[1]
        w_grad = low(outer_sum(group_tokens, both)).reshape(blocks, D // blocks, width)
        b_grad = low(jnp.sum(widen(both), axis=0))
        b_grad = jnp.pad(b_grad[None], ((0, 15), (0, 0)))
        qkv = jnp.concatenate([w_grad, jnp.broadcast_to(b_grad[None], (blocks, 16, width))], axis=1)
        rows = qkv.shape[1]
        mine = lax.psum_scatter(
            qkv.reshape(blocks * rows, width), ("wa", "c"), scatter_dimension=0, tiled=True
        )
        mine = lax.psum(mine, "m")
        every = widen(lax.all_gather(mine, ("c", "h"), axis=0).reshape(2, GROUPS, rows, width))

        def columns(block):
            k = jnp.concatenate([block[..., :128], block[..., 192:256]], axis=-1)
            v = jnp.concatenate([block[..., 256:384], block[..., 128:192]], axis=-1)
            q = block[..., 384:576]
            return [jnp.transpose(item, (0, 2, 1, 3)).reshape(2, -1, D) for item in (q, k, v)]

        out_query, out_key, out_value = (
            item.reshape(-1, D) for item in columns(every[:, :, : rows - 16])
        )
        sums_q, _, sums_v = (item[0, 0] for item in columns(every[:, :, rows - 16 : rows - 15]))
        grad_inputs = token_grads(grad_sum_one, back_kv_parts, back_q_parts, back_kv, back_q)
    out_b_query = lax.dynamic_slice_in_dim(sums_q, side * part, part, 0)
    out_b_value = lax.dynamic_slice_in_dim(sums_v, side * part, part, 0)

    return (
        low(result)[None],
        grad_inputs[None],
        out_query,
        out_key,
        out_value,
        out_out,
        out_up,
        out_down,
        out_b_query,
        out_b_value,
        share(0, 1),
        share(1, 1),
        share(2, 1),
        share(6, 4),
        share(3, 1),
        share(4, 1),
        share(5, 1),
    )


def solution(mesh):
    chunks, wide = mesh.devices.shape
    finer = Mesh(
        mesh.devices.reshape(GROUPS, chunks // (2 * GROUPS), 2, wide), ("h", "m", "c", "wa")
    )
    ctx = ("h", "m", "c")
    seq3, seq2 = P("wa", ctx, None), P("wa", ctx)
    matrix, vector = P("wa", None), P("wa")
    return jax.shard_map(
        per_device,
        mesh=finer,
        in_specs=(seq3, seq2, seq3) + (matrix,) * 6 + (vector,) * 9,
        out_specs=(seq3, seq3) + (matrix,) * 6 + (vector,) * 9,
        check_vma=False,
    )
```

```python
import functools

import jax
import jax.numpy as jnp
from jax import lax
from jax.experimental import pallas as pl
from jax.experimental.pallas import tpu as pltpu
from jax.sharding import Mesh
from jax.sharding import PartitionSpec as P

D = 768
HEADS = 12
HEAD_DIM = 64
FF = 3072
DOCS = 32

GROUPS = 4
OWN = HEADS // GROUPS
WIDTH = OWN * HEAD_DIM
QTILE = 256
KTILE = 512

epsilon = 1e-05
masked_value = -1e30
NT = (((1,), (1,)), ((), ()))
NN = (((1,), (0,)), ((), ()))


def widen(array):
    return array.astype(jnp.float32)


def low(array):
    return array.astype(jnp.bfloat16)


def mm(left, right):
    return jnp.dot(left, right, preferred_element_type=jnp.float32)


def outer_sum(left, right):
    return lax.dot_general(
        left, right, (((0,), (0,)), ((), ())), preferred_element_type=jnp.float32
    )


def back_product(grad, weight):
    return lax.dot_general(grad, weight, NT, preferred_element_type=jnp.float32)


def norm_forward(values, gain, shift):
    centre = values - jnp.mean(values, axis=-1, keepdims=True)
    scale = lax.rsqrt(jnp.mean(centre * centre, axis=-1, keepdims=True) + epsilon)
    unit = centre * scale
    return (unit * gain + shift, unit, scale)


def norm_backward(grad, unit, scale, gain):
    grad_gain = jnp.sum(grad * unit, axis=0)
    grad_shift = jnp.sum(grad, axis=0)
    inner = grad * gain
    grad_in = scale * (
        inner
        - jnp.mean(inner, axis=-1, keepdims=True)
        - unit * jnp.mean(inner * unit, axis=-1, keepdims=True)
    )
    return (grad_in, grad_gain, grad_shift)


def gelu_pair(values):
    cumulative = 0.5 * (1.0 + lax.erf(values * 0.7071067811865476))
    density = jnp.exp(-0.5 * values * values) * 0.3989422804014327
    return (values * cumulative, cumulative + values * density)


def swap(array, axis, bit):
    size = lax.axis_size(axis)
    return lax.ppermute(array, axis, [(i, i ^ bit) for i in range(size)])


K_BLOCK = (0, 0, 1)
V_BLOCK = (2, 2, 1)
K_UPPER = (False, True, True)
V_UPPER = (False, True, False)


def lane_half(array, upper):
    lane = lax.broadcasted_iota(jnp.int32, array.shape, 1)
    keep = (lane >= 64) if upper else (lane < 64)
    return jnp.where(keep, array, jnp.zeros_like(array))


def piece_copies(where, ids, pieces, kv, sem, rows, classes):
    copies = []
    for piece, (mask, flips) in zip(pieces, where):
        for slot, flip in enumerate(flips):
            chunk = (ids[0] ^ flip) * classes + (ids[1] ^ mask)
            start = pl.multiple_of(chunk * rows, 64)
            copies.append(
                pltpu.make_async_copy(
                    piece.at[slot], kv.at[pl.ds(start, rows), :], sem.at[len(copies)]
                )
            )
    return copies


def allowed(spans, base, start):
    position = lax.broadcasted_iota(jnp.int32, (KTILE, QTILE), 0)
    first = spans[0:1, pl.ds(base, QTILE)] - start
    last = spans[1:2, pl.ds(base, QTILE)] - start
    return (position >= first) & (position < last)


def walk(steps, tiles, j, fetch, work):
    amount = steps[j * (tiles + 1)]

    def tile(i):
        index = steps[j * (tiles + 1) + 1 + jnp.minimum(i, amount - 1)]
        start = pl.multiple_of(index * KTILE, KTILE)
        return start, jnp.where(i < amount, start, -(1 << 24))

    fetch(0, tile(0)[0])

    @pl.loop(0, (amount + 1) // 2)
    def _(i):
        here, there, later = tile(2 * i), tile(2 * i + 1), tile(2 * i + 2)
        fetch(1, there[0])
        work(0, *here)
        fetch(0, later[0])
        work(1, *there)


def forward_kernel(where, rows, classes, ids, flags, q, spans, *rest):
    count = len(where)
    pieces = rest[:count]
    o_parts, o_first, o_second, lse, o_low, kv, vt, qm, top, total, accum, first, second, sem = rest[count:]
    length = kv.shape[0]
    tiles = length // KTILE
    copies = piece_copies(where, ids, pieces, kv, sem, rows, classes)
    for copy in copies:
        copy.start()
    for copy in copies:
        copy.wait()

    @pl.loop(0, tiles)
    def _(t):
        start = pl.multiple_of(t * KTILE, KTILE)
        vt[0:128, pl.ds(start, KTILE)] = kv[pl.ds(start, KTILE), 128:256].T
        vt[128:256, pl.ds(start, KTILE)] = kv[pl.ds(start, KTILE), 256:384].T

    v_row = (128, 192, 0)

    @pl.loop(0, q.shape[0] // QTILE)
    def _(j):
        base = pl.multiple_of(j * QTILE, QTILE)
        for head in range(OWN):
            block = q[pl.ds(base, QTILE), pl.ds(128 * K_BLOCK[head], 128)]
            qm[head] = lane_half(block, K_UPPER[head])
        top[...] = jnp.full_like(top, masked_value)
        total[...] = jnp.zeros_like(total)
        accum[...] = jnp.zeros_like(accum)

        stages = (first, second)

        def fetch(stage, start):
            for head in range(OWN):
                block = 128 * K_BLOCK[head]
                stages[stage][head] = lax.dot_general(
                    kv[pl.ds(start, KTILE), block : block + 128],
                    qm[head],
                    NT,
                    preferred_element_type=jnp.float32,
                )

        def work(stage, start, position):
            same = allowed(spans, base, position)
            for head in range(OWN):
                scores = jnp.where(same, stages[stage][head], masked_value)
                old = top[head : head + 1, :]
                new = jnp.maximum(old, jnp.max(scores, axis=0, keepdims=True))
                weights = jnp.exp(scores - new)
                factor = jnp.exp(old - new)
                top[head : head + 1, :] = new
                total[head : head + 1, :] = total[head : head + 1, :] * factor + jnp.sum(
                    weights, axis=0, keepdims=True
                )
                rows_v = slice(v_row[head], v_row[head] + 64)
                place = slice(64 * head, 64 * head + 64)
                accum[place, :] = accum[place, :] * factor + jnp.dot(
                    vt[rows_v, pl.ds(start, KTILE)],
                    weights.astype(jnp.bfloat16),
                    preferred_element_type=jnp.float32,
                )

        walk(flags, tiles, j, fetch, work)
        outs = [
            accum[64 * head : 64 * head + 64, :] / total[head : head + 1, :] for head in range(OWN)
        ]
        lower = jnp.concatenate(outs[:2], axis=0).T
        upper = jnp.concatenate([outs[2], jnp.zeros_like(outs[2])], axis=0).T
        o_first[pl.ds(base, QTILE), :] = lower
        o_second[pl.ds(base, QTILE), :] = upper
        o_low[pl.ds(base, QTILE), 0:128] = lower.astype(jnp.bfloat16)
        o_low[pl.ds(base, QTILE), 128:192] = upper[:, 0:64].astype(jnp.bfloat16)
        lse[:, pl.ds(base, QTILE)] = top[...] + jnp.log(total[...])

    for flip in range(GROUPS):
        o_parts[flip ^ ids[0]] = o_low[rows * flip : rows * flip + rows, :]


def backward_kernel(where, rows, classes, out_where, extra, ids, flags, q, spans, o_first, o_second, lse, *rest):
    count = len(where)
    grads, pieces = rest[0], rest[1 : 1 + count]
    rest = rest[1 + count + extra :]
    outs = rest[: len(out_where)]
    dq, grad, kv, kt, qm, dom, stats, dqt, dkv, low_kv, sem = rest[len(out_where) :]
    length = kv.shape[0]
    tiles = length // KTILE
    copies = piece_copies(where, ids, pieces, kv, sem, rows, classes)
    for copy in copies:
        copy.start()

    @pl.loop(0, tiles)
    def _(t):
        start = pl.multiple_of(t * KTILE, KTILE)
        dkv[pl.ds(start, KTILE), :] = jnp.zeros((KTILE, 384), jnp.float32)

    for flip in range(GROUPS):
        grad[rows * flip : rows * flip + rows, :] = jnp.concatenate(
            [grads[flip ^ ids[0]], jnp.zeros((rows, 64), jnp.bfloat16)], axis=1
        )

    for copy in copies:
        copy.wait()

    @pl.loop(0, tiles)
    def _(t):
        start = pl.multiple_of(t * KTILE, KTILE)
        kt[0:128, pl.ds(start, KTILE)] = kv[pl.ds(start, KTILE), 0:128].T
        kt[128:256, pl.ds(start, KTILE)] = kv[pl.ds(start, KTILE), 128:256].T

    k_row = (0, 64, 192)

    @pl.loop(0, q.shape[0] // QTILE)
    def _(j):
        base = pl.multiple_of(j * QTILE, QTILE)
        for head in range(OWN):
            block = q[pl.ds(base, QTILE), pl.ds(128 * K_BLOCK[head], 128)]
            qm[head] = lane_half(block, K_UPPER[head])
            block = grad[pl.ds(base, QTILE), pl.ds(128 * (2 - V_BLOCK[head]), 128)]
            dom[head] = lane_half(block, V_UPPER[head])
        for part in range(2):
            product = (
                grad[pl.ds(base, QTILE), 128 * part : 128 * part + 128].astype(jnp.float32)
                * (o_first, o_second)[part][pl.ds(base, QTILE), :]
            ).T
            for half in range(2):
                head = 2 * part + half
                if head < OWN:
                    stats[head : head + 1, :] = jnp.sum(
                        product[64 * half : 64 * half + 64], axis=0, keepdims=True
                    )
        dqt[...] = jnp.zeros_like(dqt)

        def product(place, block, right):
            left = kv[place, 128 * block : 128 * block + 128]
            return lax.dot_general(left, right, NT, preferred_element_type=jnp.float32)

        @pl.loop(0, flags[j * (tiles + 1)])
        def _(i):
            start = pl.multiple_of(flags[j * (tiles + 1) + 1 + i] * KTILE, KTILE)
            place = pl.ds(start, KTILE)
            same = allowed(spans, base, start)
            sums = [None, None, None]

            def add(block, left, right):
                term = jnp.dot(left, right, preferred_element_type=jnp.float32)
                sums[block] = term if sums[block] is None else sums[block] + term

            for head in range(OWN):
                scores = product(place, K_BLOCK[head], qm[head])
                grad_probs = product(place, V_BLOCK[head], dom[head])
                probs = jnp.where(
                    same, jnp.exp(scores - lse[head : head + 1, pl.ds(base, QTILE)]), 0.0
                )
                grad_scores = (probs * (grad_probs - stats[head : head + 1, :])).astype(jnp.bfloat16)
                add(V_BLOCK[head], probs.astype(jnp.bfloat16), dom[head])
                add(K_BLOCK[head], grad_scores, qm[head])
                rows_k = slice(k_row[head], k_row[head] + 64)
                dqt[64 * head : 64 * head + 64, :] += jnp.dot(
                    kt[rows_k, place], grad_scores, preferred_element_type=jnp.float32
                )
            for block in range(3):
                dkv[place, 128 * block : 128 * block + 128] += sums[block]

        lower = dqt[0:128, :].T * 0.125
        upper = dqt[64:192, :].T * 0.125
        dq[pl.ds(base, QTILE), 0:128] = lower.astype(jnp.bfloat16)
        dq[pl.ds(base, QTILE), 128:192] = upper[:, 64:128].astype(jnp.bfloat16)

    @pl.loop(0, tiles)
    def _(t):
        start = pl.multiple_of(t * KTILE, KTILE)
        low_kv[pl.ds(start, KTILE), :] = dkv[pl.ds(start, KTILE), :].astype(jnp.bfloat16)

    copies = []
    for out, masks in zip(outs, out_where):
        for slot, mask in enumerate(masks):
            for flip in range(GROUPS):
                chunk = (ids[0] ^ flip) * classes + (ids[1] ^ mask)
                start = pl.multiple_of(chunk * rows, 64)
                copies.append(
                    pltpu.make_async_copy(
                        low_kv.at[pl.ds(start, rows), :], out.at[slot, flip], sem.at[len(copies)]
                    )
                )
    for copy in copies:
        copy.start()
    for copy in copies:
        copy.wait()


VMEM_SPEC = pl.BlockSpec(memory_space=pltpu.VMEM)
SMEM_SPEC = pl.BlockSpec(memory_space=pltpu.SMEM)
ANY_SPEC = pl.BlockSpec(memory_space=pl.ANY)
PARAMS = pltpu.CompilerParams(vmem_limit_bytes=56 * 1024 * 1024)


def attend_forward(ids, flags, q, spans, pieces, where, rows, classes):
    length = rows * classes * GROUPS
    queries = q.shape[0]
    copies = sum(len(flips) for _, flips in where)
    return pl.pallas_call(
        functools.partial(forward_kernel, where, rows, classes),
        out_shape=(
            jax.ShapeDtypeStruct((GROUPS, rows, WIDTH), jnp.bfloat16),
            jax.ShapeDtypeStruct((queries, 128), jnp.float32),
            jax.ShapeDtypeStruct((queries, 128), jnp.float32),
            jax.ShapeDtypeStruct((8, queries), jnp.float32),
        ),
        in_specs=[SMEM_SPEC, SMEM_SPEC, VMEM_SPEC, VMEM_SPEC]
        + [ANY_SPEC] * len(pieces),
        out_specs=(VMEM_SPEC,) * 4,
        scratch_shapes=[
            pltpu.VMEM((queries, WIDTH), jnp.bfloat16),
            pltpu.VMEM((length, 384), jnp.bfloat16),
            pltpu.VMEM((256, length), jnp.bfloat16),
            pltpu.VMEM((OWN, QTILE, 128), jnp.bfloat16),
            pltpu.VMEM((8, QTILE), jnp.float32),
            pltpu.VMEM((8, QTILE), jnp.float32),
            pltpu.VMEM((WIDTH, QTILE), jnp.float32),
            pltpu.VMEM((OWN, KTILE, QTILE), jnp.float32),
            pltpu.VMEM((OWN, KTILE, QTILE), jnp.float32),
            pltpu.SemaphoreType.DMA((copies,)),
        ],
        compiler_params=PARAMS,
        cost_estimate=pl.CostEstimate(
            flops=queries * length * WIDTH * 4, bytes_accessed=8 << 20, transcendentals=0
        ),
        name="attend_forward",
    )(ids, flags, q, spans, *pieces)


def attend_backward(
    ids, flags, q, spans, grads, outputs, lse, pieces, after, where, rows, classes, out_where
):
    length = rows * classes * GROUPS
    queries = q.shape[0]
    copies = sum(len(flips) for _, flips in where)
    return pl.pallas_call(
        functools.partial(backward_kernel, where, rows, classes, out_where, len(after)),
        out_shape=tuple(
            jax.ShapeDtypeStruct((len(masks), GROUPS, rows, 384), jnp.bfloat16)
            for masks in out_where
        )
        + (jax.ShapeDtypeStruct((queries, WIDTH), jnp.bfloat16),),
        in_specs=[SMEM_SPEC, SMEM_SPEC] + [VMEM_SPEC] * 6 + [ANY_SPEC] * (len(pieces) + len(after)),
        out_specs=(ANY_SPEC,) * len(out_where) + (VMEM_SPEC,),
        scratch_shapes=[
            pltpu.VMEM((queries, 256), jnp.bfloat16),
            pltpu.VMEM((length, 384), jnp.bfloat16),
            pltpu.VMEM((256, length), jnp.bfloat16),
            pltpu.VMEM((OWN, QTILE, 128), jnp.bfloat16),
            pltpu.VMEM((OWN, QTILE, 128), jnp.bfloat16),
            pltpu.VMEM((8, QTILE), jnp.float32),
            pltpu.VMEM((WIDTH, QTILE), jnp.float32),
            pltpu.VMEM((length, 384), jnp.float32),
            pltpu.VMEM((length, 384), jnp.bfloat16),
            pltpu.SemaphoreType.DMA((copies,)),
        ],
        compiler_params=PARAMS,
        cost_estimate=pl.CostEstimate(
            flops=queries * length * WIDTH * 10, bytes_accessed=16 << 20, transcendentals=0
        ),
        name="attend_backward",
    )(ids, flags, q, spans, *outputs, lse, grads, *pieces, *after)


def pick_kernel(ids, w_q, w_k, w_v, out):
    odd = (ids[3] & 1) == 1
    start = pl.multiple_of((ids[3] // 2) * 384 + (ids[3] & 1) * 128, 128)

    def take(weight):
        both = weight[:, pl.ds(start, 256)]
        return jnp.where(odd, both[:, 64:256], both[:, 0:192])

    q, k, v = take(w_q), take(w_k), take(w_v)
    out[...] = jnp.concatenate(
        [k[:, :128], v[:, 128:], k[:, 128:], v[:, :128], q[:, :128], jnp.zeros_like(q[:, :64]), q[:, 128:]],
        axis=1,
    )


def pick_weights(ids, w_q, w_k, w_v):
    return pl.pallas_call(
        pick_kernel,
        out_shape=jax.ShapeDtypeStruct((w_q.shape[0], 640), jnp.bfloat16),
        in_specs=[SMEM_SPEC] + [VMEM_SPEC] * 3,
        out_specs=VMEM_SPEC,
        compiler_params=PARAMS,
        name="pick_weights",
    )(ids, w_q, w_k, w_v)


def project_kernel(count, parts, ids, bias, *rest):
    tokens, weights, (kv, q) = rest[:count], rest[count : count + parts], rest[count + parts :]
    rows = weights[0].shape[0]
    for i, chunk in enumerate(tokens):
        total = bias[...]
        for part, weight in enumerate(weights):
            lanes = (0 if parts == 1 else ids[0] ^ part) * rows
            left = chunk[:, pl.ds(pl.multiple_of(lanes, 128), rows)]
            total = total + jnp.dot(left, weight[...], preferred_element_type=jnp.float32)
        kv[i] = total[:, :384].astype(jnp.bfloat16)
        q[chunk.shape[0] * i : chunk.shape[0] * (i + 1), :] = (
            total[:, 384:].astype(jnp.bfloat16) * jnp.bfloat16(0.125)
        )


def project(ids, bias, chunks, weights):
    count, rows = len(chunks), chunks[0].shape[0]
    return pl.pallas_call(
        functools.partial(project_kernel, count, len(weights)),
        out_shape=(
            jax.ShapeDtypeStruct((count, rows, 384), jnp.bfloat16),
            jax.ShapeDtypeStruct((count * rows, 256), jnp.bfloat16),
        ),
        in_specs=[SMEM_SPEC] + [VMEM_SPEC] * (1 + count + len(weights)),
        out_specs=(VMEM_SPEC, VMEM_SPEC),
        compiler_params=PARAMS,
        cost_estimate=pl.CostEstimate(
            flops=2 * count * rows * D * 640, bytes_accessed=2 << 20, transcendentals=0
        ),
        name="project",
    )(ids, bias, *chunks, *weights)


def tn(left, right):
    return lax.dot_general(
        left, right, (((0,), (0,)), ((), ())), preferred_element_type=jnp.float32
    )


def down_grad_kernel(extra, active, g_low, *rest):
    down = rest[extra]

    @pl.loop(0, 8)
    def _(i):
        part = tn(active[:, pl.ds(pl.multiple_of(i * 384, 128), 384)], g_low[...]).astype(jnp.bfloat16)
        for unit in range(4):
            for half in range(2):
                place = (((i % 2) * 2 + unit // 2) * 2 + (i // 2) % 2) * 4 + (i // 4) * 2 + unit % 2
                start = pl.multiple_of(place * 192, 192) + 96 * half
                down[pl.ds(start, 96), :] = part[96 * unit : 96 * unit + 96, 384 * half : 384 * half + 384]


def down_grad(active, g_low, after):
    return pl.pallas_call(
        functools.partial(down_grad_kernel, len(after)),
        out_shape=jax.ShapeDtypeStruct((2 * FF, D // 2), jnp.bfloat16),
        in_specs=[VMEM_SPEC] * 2 + [ANY_SPEC] * len(after),
        out_specs=VMEM_SPEC,
        compiler_params=PARAMS,
        cost_estimate=pl.CostEstimate(
            flops=2 * active.shape[0] * D * FF, bytes_accessed=8 << 20, transcendentals=0
        ),
        name="down_grad",
    )(active, g_low, *after)


def turn(index):
    return (index & 1) * 2 + index // 2


def upper_grad_kernel(extra, ids, hid, g_raised, attn, g_att, vec, *rest):
    near, far = rest[extra:]
    x, c, m, h = ids[0], ids[1], ids[2], ids[3]

    @pl.loop(0, 2)
    def _(i):
        left = hid[:, pl.ds(pl.multiple_of(i * 384, 128), 384)]
        attn_left = attn[:, pl.ds(pl.multiple_of(i * 384, 128), 384)]

        @pl.loop(0, 2)
        def _(j):
            outer = tn(attn_left, g_att[:, pl.ds(pl.multiple_of(j * 384, 128), 384)]).astype(jnp.bfloat16)

            for k in range(4):
                unit = j * 4 + k
                part = tn(left, g_raised[:, pl.ds(pl.multiple_of(unit * 384, 128), 384)]).astype(jnp.bfloat16)
                for b in range(2):
                    place = ((j ^ m) * 2 + (i ^ x)) * 4 + turn(k ^ h)

                    def store(target):
                        target[place, 0:192, :] = part[192 * b : 192 * b + 192]
                        target[place, 192:240, :] = outer[192 * b + 48 * k : 192 * b + 48 * k + 48]
                        target[place, 240:256, :] = vec[unit]

                    pl.when(c == b)(functools.partial(store, near))
                    pl.when(c != b)(functools.partial(store, far))


def upper_grad(ids, hid, g_raised, attn, g_att, vec, after):
    return pl.pallas_call(
        functools.partial(upper_grad_kernel, len(after)),
        out_shape=(jax.ShapeDtypeStruct((16, 256, 384), jnp.bfloat16),) * 2,
        in_specs=[SMEM_SPEC] + [VMEM_SPEC] * 5 + [ANY_SPEC] * len(after),
        out_specs=(VMEM_SPEC,) * 2,
        compiler_params=PARAMS,
        cost_estimate=pl.CostEstimate(
            flops=2 * hid.shape[0] * D * (FF + D), bytes_accessed=12 << 20, transcendentals=0
        ),
        name="upper_grad",
    )(ids, hid, g_raised, attn, g_att, vec, *after)


def unpack_ffn_kernel(ids, block_own, block_other, up, out, down, *vecs):
    side, core, mid, group = ids[0], ids[1], ids[2], ids[3]
    b, j = pl.program_id(0) ^ core, pl.program_id(1)
    own = pl.program_id(0) == 0
    for k in range(GROUPS):
        place = turn(k ^ group)
        part = jnp.where(own, block_own[place], block_other[place]).astype(jnp.float32)
        up[:, 384 * k : 384 * k + 384] = part[0:192]
        out[48 * k : 48 * k + 48, :] = part[192:240]
        rows = pl.ds(pl.multiple_of(96 * j, 32) + 192 * k, 96)
        down[rows, 0:384] = part[256:352]
        down[rows, 384:768] = part[352:448]

    @pl.when(b == 0)
    def _():
        for u in range(8):
            place = turn((u % 4) ^ group)
            rows = jnp.where(own, block_own[place, 240:256, :], block_other[place, 240:256, :])
            rows = rows.astype(jnp.float32)
            for r in range(3):
                row = 3 * u + r
                if row < 12:
                    target, where, half = vecs[row // 2], 0, row % 2
                elif row < 20:
                    target, where, half = vecs[6], (row - 12) % 4, (row - 12) // 4
                else:
                    continue

                @pl.when((j == u // 4) & (side == half))
                def _():
                    target[384 * where : 384 * where + 384] = rows[r]


def unpack_ffn(ids, own, other):
    def source_own(d, j, ids):
        return (jnp.where(d == 0, j, 1) ^ ids[2], 0, 0)

    def source_other(d, j, ids):
        return (jnp.where(d == 0, 0, j) ^ ids[2], 0, 0)

    sizes = [384] * 6 + [1536]
    return pl.pallas_call(
        unpack_ffn_kernel,
        out_shape=(
            jax.ShapeDtypeStruct((384, FF), jnp.float32),
            jax.ShapeDtypeStruct((384, D), jnp.float32),
            jax.ShapeDtypeStruct((FF // 2, D), jnp.float32),
        )
        + tuple(jax.ShapeDtypeStruct((size,), jnp.float32) for size in sizes),
        grid_spec=pltpu.PrefetchScalarGridSpec(
            num_scalar_prefetch=1,
            grid=(2, 2),
            in_specs=[pl.BlockSpec((4, 448, 384), source_own), pl.BlockSpec((4, 448, 384), source_other)],
            out_specs=(
                pl.BlockSpec((192, 1536), lambda d, j, ids: (d ^ ids[1], j)),
                pl.BlockSpec((192, 384), lambda d, j, ids: (d ^ ids[1], j)),
                pl.BlockSpec((FF // 4, D), lambda d, j, ids: (d ^ ids[1], 0)),
            )
            + tuple(pl.BlockSpec((size,), lambda d, j, ids: (0,)) for size in sizes),
        ),
        compiler_params=PARAMS,
        name="unpack_ffn",
    )(ids, own, other)


def qkv_grad_kernel(ids, t0, t1, t2, t3, *rest):
    kept, given, sent, dq, near, far, both, whole = rest
    x, c = ids[0], ids[1]
    rows = dq.shape[0] // GROUPS
    total = jnp.zeros((1, 576), jnp.float32)
    for flip in range(GROUPS):
        term = (
            kept[0, flip].astype(jnp.float32)
            + given[0, flip].astype(jnp.float32)
            + sent[flip].astype(jnp.float32)
        ).astype(jnp.bfloat16)
        own = slice(rows * flip, rows * flip + rows)
        block = jnp.concatenate([term, dq[own, :]], axis=1)
        both[flip ^ ids[3]] = block
        whole[own, :] = block
        total = total + jnp.sum(block.astype(jnp.float32), axis=0, keepdims=True)
    first = lax.broadcasted_iota(jnp.int32, (16, 576), 0) == 0
    total = jnp.where(first, jnp.broadcast_to(total, (16, 576)), 0.0).astype(jnp.bfloat16)

    @pl.loop(0, 2)
    def _(i):
        lanes = pl.ds(pl.multiple_of(i * 384, 128), 384)
        left = jnp.concatenate([t[:, lanes] for t in (t0, t1, t2, t3)], axis=0)
        part = tn(left, whole[...]).astype(jnp.bfloat16)
        for b in range(2):

            def store(target):
                target[i ^ x, 0:192, :] = part[192 * b : 192 * b + 192]

            pl.when(c == b)(functools.partial(store, near))
            pl.when(c != b)(functools.partial(store, far))
        near[i ^ x, 192:208, :] = total
        far[i ^ x, 192:208, :] = total


def qkv_grads(ids, tokens, kept, given, sent, dq):
    queries = dq.shape[0]
    rows = queries // GROUPS
    return pl.pallas_call(
        qkv_grad_kernel,
        out_shape=(jax.ShapeDtypeStruct((2, 208, 576), jnp.bfloat16),) * 2
        + (jax.ShapeDtypeStruct((GROUPS, rows, 576), jnp.bfloat16),),
        in_specs=[SMEM_SPEC] + [VMEM_SPEC] * 8,
        out_specs=(VMEM_SPEC,) * 3,
        scratch_shapes=[pltpu.VMEM((queries, 576), jnp.bfloat16)],
        compiler_params=PARAMS,
        cost_estimate=pl.CostEstimate(
            flops=2 * queries * D * 576, bytes_accessed=4 << 20, transcendentals=0
        ),
        name="qkv_grads",
    )(ids, *tokens, kept, given, sent, dq)


def unpack_qkv_kernel(ids, own, other, out_q, out_k, out_v, vec):
    c, h = ids[1], ids[3]
    for b in range(2):
        q, k, v = [], [], []
        for g in range(GROUPS):
            block = jnp.where(c == b, own[turn(g ^ h), 0:192, :], other[turn(g ^ h), 0:192, :]).astype(jnp.float32)
            k += [block[:, 0:128], block[:, 192:256]]
            v += [block[:, 256:384], block[:, 128:192]]
            q += [block[:, 384:576]]
        for out, parts in ((out_q, q), (out_k, k), (out_v, v)):
            out[192 * b : 192 * b + 192, :] = jnp.concatenate(parts, axis=1)
    for g in range(GROUPS):
        vec[g] = jnp.where(c == 0, own[turn(g ^ h), 192:208, :], other[turn(g ^ h), 192:208, :]).astype(jnp.float32)


def unpack_qkv(ids, own, other):
    return pl.pallas_call(
        unpack_qkv_kernel,
        out_shape=(jax.ShapeDtypeStruct((384, D), jnp.float32),) * 3
        + (jax.ShapeDtypeStruct((GROUPS, 16, 576), jnp.float32),),
        in_specs=[SMEM_SPEC, VMEM_SPEC, VMEM_SPEC],
        out_specs=(VMEM_SPEC,) * 4,
        compiler_params=PARAMS,
        name="unpack_qkv",
    )(ids, own, other)


def token_grad_kernel(base, both, weight, out):
    total = base[...]
    for g in range(GROUPS):
        w = weight[:, 640 * g : 640 * g + 576]
        total = total + lax.dot_general(both[g], w, NT, preferred_element_type=jnp.float32)
    out[...] = total


def token_grads(base, both, weight):
    return pl.pallas_call(
        token_grad_kernel,
        out_shape=jax.ShapeDtypeStruct(base.shape, jnp.float32),
        in_specs=[VMEM_SPEC] * 3,
        out_specs=VMEM_SPEC,
        compiler_params=PARAMS,
        cost_estimate=pl.CostEstimate(
            flops=2 * base.shape[0] * D * 2304, bytes_accessed=8 << 20, transcendentals=0
        ),
        name="token_grads",
    )(base, both, weight)


def gather_rows(weight, core, *others):
    half = weight.shape[0] // 2
    part = tie(lax.dynamic_slice_in_dim(weight, core * half, half, 0), *others)
    return lax.all_gather(part, ("wa", "c"), axis=0, tiled=True)


def reduce_blocks(grad):
    flat = grad.reshape((-1,) + grad.shape[2:])
    mine = lax.psum_scatter(flat, ("wa", "c"), scatter_dimension=0, tiled=True)
    mine = lax.psum_scatter(mine, "m", scatter_dimension=0, tiled=True)
    mine = lax.psum_scatter(mine, "h", scatter_dimension=0, tiled=True)
    return lax.all_gather(mine, ("c", "m", "h"), axis=0, tiled=True)


def tie(array, *others):
    return lax.optimization_barrier((array,) + others)[0]


def both_sum(near, far, *others):
    near = tie(near, *others)
    return low(widen(near) + widen(far))


def fold(near, far, *others):
    near = tie(near, *others)
    return [low(widen(near[i]) + widen(far[i])) for i in range(2)]


def double(array, axis, bit):
    return jnp.concatenate([array, swap(array, axis, bit)], axis=0)


def pick_columns(weight, group):
    q, k, v = (lax.dynamic_slice_in_dim(w, group * WIDTH, WIDTH, w.ndim - 1) for w in weight)
    return jnp.concatenate(
        [
            k[..., :128],
            v[..., 128:],
            k[..., 128:],
            v[..., :128],
            q[..., :128],
            jnp.zeros_like(q[..., :64]),
            q[..., 128:],
        ],
        axis=-1,
    )


def per_device(
    tokens,
    segment_ids,
    cotangent,
    w_query,
    w_key,
    w_value,
    w_out,
    w_up,
    w_down,
    b_query,
    b_value,
    b_out,
    gain_one,
    shift_one,
    b_up,
    b_down,
    gain_two,
    shift_two,
):
    mid = lax.axis_size("m")
    wide = lax.axis_size("wa")
    paired = mid == 2 and wide == 2
    classes = 2 * mid
    group = lax.axis_index("h")
    core = lax.axis_index("c")
    kind = lax.axis_index("m") * 2 + core
    side = lax.axis_index("wa")
    inputs = tokens[0]
    count = inputs.shape[0]
    chunks = GROUPS * classes
    length = count * chunks
    tiles = length // KTILE
    ids = jnp.stack([group, kind]).astype(jnp.int32)
    place_ids = jnp.stack([side, core, lax.axis_index("m"), group]).astype(jnp.int32)
    order = group ^ jnp.arange(GROUPS)

    second = swap(inputs, "h", 1)
    third = swap(inputs, "h", 2)
    if wide == 2:
        w_own = pick_weights(place_ids, w_query, w_key, w_value)
        w_other = swap(w_own, "wa", 1)
    else:
        w_own = None
        w_other = lax.all_gather(
            pick_columns((w_query, w_key, w_value), group), "wa", axis=0, tiled=True
        )

    smalls = [b_query, b_value, b_out, gain_one, shift_one, b_up, b_down, gain_two, shift_two]
    joined = lax.all_gather(jnp.concatenate(smalls), "wa", axis=0)
    second, third, w_other, joined = lax.optimization_barrier((second, third, w_other, joined))
    fourth = swap(third, "h", 1)
    full, place = [], 0
    for item in smalls:
        size = item.shape[0]
        full.append(widen(joined[:, place : place + size].reshape(-1)))
        place += size
    bias_query, bias_value, bias_out, gain_attn, shift_attn, bias_up, bias_down, gain_ffn, shift_ffn = full
    b_group = pick_columns((bias_query, jnp.zeros_like(bias_query), bias_value), group)[None]

    w_group = (w_own, w_other) if wide == 2 else (w_other,)
    full_out = gather_rows(w_out, core, w_other)
    full_up = gather_rows(w_up, core, w_other)
    full_down = gather_rows(w_down, core, w_other)
    where, pieces = [], []

    def spread(piece, flips):
        have = {0: piece}
        bit = 1
        while bit < mid:
            for mask in list(have):
                have[mask | (bit << 1)] = swap(have[mask], "m", bit)
            bit *= 2
        for mask in list(have):
            have[mask | 1] = swap(have[mask], "c", 1)
        for mask, item in have.items():
            where.append((mask, flips))
            pieces.append(item)

    first_kv, first_q = project(place_ids, b_group, (inputs, second, third), w_group)
    spread(first_kv, (0, 1, 2))

    segs = double(tie(segment_ids, first_kv), "c", 1)
    bit = 1
    while bit < mid:
        segs = double(segs, "m", bit)
        bit *= 2
    segs = double(double(segs, "h", 1), "h", 2)
    own_segs = segs.reshape(GROUPS, classes, count)[:, 0].reshape(-1)
    segs = jnp.take(segs, (group * classes + kind) ^ jnp.arange(chunks), axis=0)

    names = jnp.arange(DOCS)
    begins = jnp.sum((segs.reshape(-1, 1) < names).astype(jnp.int32), axis=0)
    ends = jnp.sum((segs.reshape(-1, 1) <= names).astype(jnp.int32), axis=0)
    chosen = own_segs[None, :] == names[:, None]
    begins = jnp.sum(jnp.where(chosen, begins[:, None], 0), axis=0)
    ends = jnp.sum(jnp.where(chosen, ends[:, None], 0), axis=0)
    spans = jnp.concatenate(
        [begins[None], ends[None], jnp.zeros((6, begins.shape[0]), jnp.int32)], axis=0
    )
    edges = (jnp.arange(tiles) * KTILE)[None, :, None]
    meets = (begins.reshape(-1, 1, QTILE) < edges + KTILE) & (ends.reshape(-1, 1, QTILE) > edges)
    meets = jnp.any(meets, axis=-1).astype(jnp.int32)
    rank = jnp.cumsum(meets, axis=1)
    slots = (rank[:, None, :] == jnp.arange(1, tiles + 1)[None, :, None]) & (meets[:, None, :] > 0)
    listed = jnp.sum(jnp.where(slots, jnp.arange(tiles), 0), axis=-1)
    flags = jnp.concatenate([rank[:, -1:], listed], axis=1).astype(jnp.int32).reshape(-1)

    last_kv, last_q = project(place_ids, b_group, (fourth,), w_group)
    spread(last_kv, (3,))
    where = tuple(where)
    q_rows = jnp.concatenate([first_q, last_q], axis=0)
    group_tokens = [inputs, second, third, fourth]

    o_parts, o_first, o_second, lse = attend_forward(
        ids, flags, q_rows, spans, pieces, where, count, classes
    )

    w_query, w_key, w_value = (tie(item, lse) for item in (w_query, w_key, w_value))
    columns = []
    for g in range(GROUPS):
        low_part, high_part = slice(192 * g, 192 * g + 128), slice(192 * g + 128, 192 * g + 192)
        columns += [w_key[:, low_part], w_value[:, high_part], w_key[:, high_part], w_value[:, low_part]]
        columns += [w_query[:, 192 * g : 192 * g + 192], jnp.zeros_like(w_query[:, :64])]
    by_group = gather_rows(jnp.concatenate(columns, axis=1), core)

    def send_back(parts):
        return lax.all_to_all(parts, "h", 0, 0, tiled=True)

    attn_low = jnp.transpose(send_back(o_parts), (1, 0, 2)).reshape(count, D)
    attended = mm(attn_low, full_out) + bias_out
    hidden, unit_one, scale_one = norm_forward(widen(inputs) + attended, gain_attn, shift_attn)
    hidden_low = low(hidden)
    raised = mm(hidden_low, full_up) + bias_up
    active, slope = gelu_pair(raised)
    active_low = low(active)
    lowered = mm(active_low, full_down) + bias_down
    result, unit_two, scale_two = norm_forward(hidden + lowered, gain_ffn, shift_ffn)
    grad_sum_two, grad_gain_two, grad_shift_two = norm_backward(
        widen(cotangent[0]), unit_two, scale_two, gain_ffn
    )
    grad_lowered = low(grad_sum_two)
    grad_b_down = jnp.sum(widen(grad_lowered), axis=0)
    grad_raised = low(back_product(grad_lowered, full_down) * slope)
    grad_b_up = jnp.sum(widen(grad_raised), axis=0)
    grad_hidden = grad_sum_two + back_product(grad_raised, full_up)
    grad_sum_one, grad_gain_one, grad_shift_one = norm_backward(
        grad_hidden, unit_one, scale_one, gain_attn
    )
    grad_attended = low(grad_sum_one)
    grad_b_out = jnp.sum(widen(grad_attended), axis=0)
    grad_attn = low(back_product(grad_attended, full_out))

    grad_rows = send_back(jnp.transpose(grad_attn.reshape(count, GROUPS, WIDTH), (1, 0, 2)))

    vectors = jnp.concatenate(
        [grad_b_out, grad_gain_one, grad_shift_one, grad_b_down, grad_gain_two, grad_shift_two, grad_b_up]
    )
    blocks = 2 * wide
    if paired:
        vectors = jnp.pad(low(vectors), (0, 9216 - 7680)).reshape(8, 3, 384)
        vectors = jnp.pad(vectors, ((0, 0), (0, 13), (0, 0)))
        near, far = upper_grad(
            place_ids, hidden_low, grad_raised, attn_low, grad_attended, vectors, (by_group,)
        )
        shape = (2, 2, 2, 2, 256, 384)
        near, far = near.reshape(shape), swap(far, "c", 1).reshape(shape)
        grad_rows = tie(grad_rows, near)
        down_sum = down_grad(active_low, grad_lowered, (near,))
        upper, give = fold(near, far, down_sum)
        after = (give,)
        give = swap(give, "m", 1)
        down_sum = tie(down_sum, grad_rows)
        down_sum = lax.psum_scatter(down_sum, ("h", "c"), scatter_dimension=0, tiled=True)
    else:
        grad_w_down = low(outer_sum(active_low, grad_lowered))
        grad_w_up = low(outer_sum(hidden_low, grad_raised))
        grad_w_out = low(outer_sum(attn_low, grad_attended))
        vectors = jnp.pad(low(vectors).reshape(-1, D), ((0, 6), (0, 0)))
        down_rows, out_rows = FF // blocks, D // blocks
        ffn = jnp.concatenate(
            [
                grad_w_down.reshape(blocks, down_rows, D),
                grad_w_up.reshape(blocks, down_rows, D),
                grad_w_out.reshape(blocks, out_rows, D),
                jnp.broadcast_to(vectors[None], (blocks, 16, D)),
            ],
            axis=1,
        )
        after = ()
        ffn_sum = reduce_blocks(ffn).reshape(2, -1, D)
        out_down = widen(ffn_sum[:, :down_rows]).reshape(-1, D)
        out_up = widen(ffn_sum[:, down_rows : 2 * down_rows]).reshape(-1, FF)
        place = 2 * down_rows
        out_out = widen(ffn_sum[:, place : place + out_rows]).reshape(-1, D)
        small = widen(ffn_sum[0, place + out_rows :])

        def share(row, rows):
            vector = small[row : row + rows].reshape(-1)
            size = vector.shape[0] // wide
            return lax.dynamic_slice_in_dim(vector, side * size, size, 0)

        vectors = [share(row, 1) for row in range(6)] + [share(6, 4)]

    stay_masks, leave_masks = tuple(range(0, classes, 2)), tuple(range(1, classes, 2))
    out_where = (stay_masks,) + tuple((mask,) for mask in leave_masks)

    kept, *given, dq = attend_backward(
        ids, flags, q_rows, spans, grad_rows, (o_first, o_second), lse,
        pieces, after, where, count, classes, out_where,
    )

    given = [swap(item, "c", 1) for item in given]
    if paired:
        upper, give = fold(upper, give, dq)
        kept = tie(kept, give)
        sent = low(widen(kept[1]) + widen(given[1][0]))
        down_sum = lax.psum_scatter(tie(down_sum, sent), "wa", scatter_dimension=0, tiled=True)
        give = swap(give, "wa", 1)
        upper = tie(upper, sent)
        sent = swap(sent, "m", 1)
        upper, give = fold(upper, give)
        kept = tie(kept, give)
        give = swap(give, "h", 1)
    else:
        partial = widen(kept) + widen(jnp.concatenate(given, axis=0))
        stay = list(stay_masks)
        bit = mid // 2
        while bit >= 1:
            mask = bit << 1
            near = [i for i, m in enumerate(stay) if not m & mask]
            far = [i for i, m in enumerate(stay) if m & mask]
            sent = swap(low(partial[far[0] : far[-1] + 1]), "m", bit)
            partial = widen(low(partial[near[0] : near[-1] + 1])) + widen(sent)
            stay = [stay[i] for i in near]
            bit //= 2
        dkv = low(partial[0]).reshape(GROUPS * count, 384)

    part = D // wide
    if paired:
        near, far, parts = qkv_grads(place_ids, group_tokens, kept, given[0], sent, dq)
        far = swap(far, "c", 1)
        down_sum = lax.psum_scatter(tie(down_sum, near), "m", scatter_dimension=0, tiled=True)
        upper, give = fold(upper, give, near)
        near = tie(near, give)
        give = swap(give, "h", 2)
        qkv, other = fold(near, far)
        other = swap(other, "wa", 1)
        upper = both_sum(upper, give, qkv)
        joint = jnp.concatenate([upper, down_sum], axis=0)
        joint_other = swap(joint, "h", 2)
        qkv = both_sum(qkv, other, joint)
        other = swap(qkv, "m", 1)
        qkv = both_sum(qkv, other)
        other = swap(qkv, "h", 2)
        joint = jnp.stack([tie(joint, qkv), joint_other])
        joint_other = swap(joint, "h", 1)
        qkv = jnp.stack([tie(qkv, joint), other])
        other = swap(qkv, "h", 1)
        joint = jnp.stack([tie(joint, qkv), joint_other])
        joint_other = swap(joint, "m", 1)
        parts = send_back(tie(parts, joint))
        qkv = jnp.concatenate([tie(qkv, joint), other], axis=0)
        other = swap(qkv, "c", 1)
        grad_inputs = token_grads(tie(grad_sum_one, qkv), parts, by_group)
        joint = jnp.stack([tie(joint, grad_inputs), joint_other])
        joint_other = swap(joint, "c", 1)
        out_query, out_key, out_value, sums = unpack_qkv(place_ids, tie(qkv, joint), other)
        joint = tie(joint, out_query)
        joint, joint_other = (item.reshape(8, 448, 384) for item in (tie(joint, out_query), joint_other))
        out_up, out_out, out_down, *vectors = unpack_ffn(place_ids, joint, joint_other)
        sums = sums[:, 0]
        sums_v = jnp.concatenate([sums[:, 256:384], sums[:, 128:192]], axis=1).reshape(-1)
        sums_q = sums[:, 384:576].reshape(-1)
    else:
        both = jnp.concatenate([dkv, dq], axis=1)
        width = both.shape[1]
        parts = send_back(jnp.take(both.reshape(GROUPS, count, width), order, axis=0))
        w_grad = low(outer_sum(jnp.concatenate(group_tokens, axis=0), both)).reshape(blocks, D // blocks, width)
        b_grad = low(jnp.sum(widen(both), axis=0))
        b_grad = jnp.pad(b_grad[None], ((0, 15), (0, 0)))
        qkv = jnp.concatenate([w_grad, jnp.broadcast_to(b_grad[None], (blocks, 16, width))], axis=1)
        rows = qkv.shape[1]
        mine = lax.psum_scatter(
            qkv.reshape(blocks * rows, width), ("wa", "c"), scatter_dimension=0, tiled=True
        )
        mine = lax.psum(mine, "m")
        every = widen(lax.all_gather(mine, ("c", "h"), axis=0).reshape(2, GROUPS, rows, width))

        def columns(block):
            k = jnp.concatenate([block[..., :128], block[..., 192:256]], axis=-1)
            v = jnp.concatenate([block[..., 256:384], block[..., 128:192]], axis=-1)
            q = block[..., 384:576]
            return [jnp.transpose(item, (0, 2, 1, 3)).reshape(2, -1, D) for item in (q, k, v)]

        out_query, out_key, out_value = (
            item.reshape(-1, D) for item in columns(every[:, :, : rows - 16])
        )
        sums_q, _, sums_v = (item[0, 0] for item in columns(every[:, :, rows - 16 : rows - 15]))
        grad_inputs = token_grads(grad_sum_one, parts, by_group)
    out_b_query = lax.dynamic_slice_in_dim(sums_q, side * part, part, 0)
    out_b_value = lax.dynamic_slice_in_dim(sums_v, side * part, part, 0)

    return (
        low(result)[None],
        grad_inputs[None],
        out_query,
        out_key,
        out_value,
        out_out,
        out_up,
        out_down,
        out_b_query,
        out_b_value,
        vectors[0],
        vectors[1],
        vectors[2],
        vectors[6],
        vectors[3],
        vectors[4],
        vectors[5],
    )


def solution(mesh):
    chunks, wide = mesh.devices.shape
    finer = Mesh(
        mesh.devices.reshape(GROUPS, chunks // (2 * GROUPS), 2, wide), ("h", "m", "c", "wa")
    )
    ctx = ("h", "m", "c")
    seq3, seq2 = P("wa", ctx, None), P("wa", ctx)
    matrix, vector = P("wa", None), P("wa")
    return jax.shard_map(
        per_device,
        mesh=finer,
        in_specs=(seq3, seq2, seq3) + (matrix,) * 6 + (vector,) * 9,
        out_specs=(seq3, seq3) + (matrix,) * 6 + (vector,) * 9,
        check_vma=False,
    )
```

```python
import functools

import jax
import jax.numpy as jnp
from jax import lax
from jax.experimental import pallas as pl
from jax.experimental.pallas import tpu as pltpu
from jax.sharding import Mesh
from jax.sharding import PartitionSpec as P

D = 768
HEADS = 12
HEAD_DIM = 64
FF = 3072
DOCS = 32

GROUPS = 4
OWN = HEADS // GROUPS
WIDTH = OWN * HEAD_DIM
QTILE = 256
KTILE = 512

epsilon = 1e-05
masked_value = -1e30
NT = (((1,), (1,)), ((), ()))
NN = (((1,), (0,)), ((), ()))


def widen(array):
    return array.astype(jnp.float32)


def low(array):
    return array.astype(jnp.bfloat16)


def mm(left, right):
    return jnp.dot(left, right, preferred_element_type=jnp.float32)


def outer_sum(left, right):
    return lax.dot_general(
        left, right, (((0,), (0,)), ((), ())), preferred_element_type=jnp.float32
    )


def back_product(grad, weight):
    return lax.dot_general(grad, weight, NT, preferred_element_type=jnp.float32)


def norm_forward(values, gain, shift):
    centre = values - jnp.mean(values, axis=-1, keepdims=True)
    scale = lax.rsqrt(jnp.mean(centre * centre, axis=-1, keepdims=True) + epsilon)
    unit = centre * scale
    return (unit * gain + shift, unit, scale)


def norm_backward(grad, unit, scale, gain):
    grad_gain = jnp.sum(grad * unit, axis=0)
    grad_shift = jnp.sum(grad, axis=0)
    inner = grad * gain
    grad_in = scale * (
        inner
        - jnp.mean(inner, axis=-1, keepdims=True)
        - unit * jnp.mean(inner * unit, axis=-1, keepdims=True)
    )
    return (grad_in, grad_gain, grad_shift)


def gelu_pair(values):
    cumulative = 0.5 * (1.0 + lax.erf(values * 0.7071067811865476))
    density = jnp.exp(-0.5 * values * values) * 0.3989422804014327
    return (values * cumulative, cumulative + values * density)


def swap(array, axis, bit):
    size = lax.axis_size(axis)
    return lax.ppermute(array, axis, [(i, i ^ bit) for i in range(size)])


K_BLOCK = (0, 0, 1)
V_BLOCK = (2, 2, 1)
K_UPPER = (False, True, True)
V_UPPER = (False, True, False)


def lane_half(array, upper):
    lane = lax.broadcasted_iota(jnp.int32, array.shape, 1)
    keep = (lane >= 64) if upper else (lane < 64)
    return jnp.where(keep, array, jnp.zeros_like(array))


def piece_copies(where, ids, pieces, kv, sem, rows, classes):
    copies = []
    for piece, (mask, flips) in zip(pieces, where):
        for slot, flip in enumerate(flips):
            chunk = (ids[0] ^ flip) * classes + (ids[1] ^ mask)
            start = pl.multiple_of(chunk * rows, 64)
            copies.append(
                pltpu.make_async_copy(
                    piece.at[slot], kv.at[pl.ds(start, rows), :], sem.at[len(copies)]
                )
            )
    return copies


def order_queries(ids, first_q, last_q, q, rows):
    for flip in range(GROUPS):
        part, place = (last_q, 0) if flip == 3 else (first_q, rows * flip)
        start = pl.multiple_of((ids[0] ^ flip) * rows, 64)
        q[pl.ds(start, rows), :] = part[place : place + rows, :]


def allowed(spans, base, start):
    position = lax.broadcasted_iota(jnp.int32, (KTILE, QTILE), 0)
    first = spans[0:1, pl.ds(base, QTILE)] - start
    last = spans[1:2, pl.ds(base, QTILE)] - start
    return (position >= first) & (position < last)


def walk(steps, tiles, j, fetch, work):
    amount = steps[j * (tiles + 1)]

    def tile(i):
        index = steps[j * (tiles + 1) + 1 + jnp.minimum(i, amount - 1)]
        start = pl.multiple_of(index * KTILE, KTILE)
        return start, jnp.where(i < amount, start, -(1 << 24))

    fetch(0, tile(0)[0])

    @pl.loop(0, (amount + 1) // 2)
    def _(i):
        here, there, later = tile(2 * i), tile(2 * i + 1), tile(2 * i + 2)
        fetch(1, there[0])
        work(0, *here)
        fetch(0, later[0])
        work(1, *there)


def forward_kernel(where, rows, classes, ids, flags, first_q, last_q, spans, *rest):
    count = len(where)
    pieces = rest[:count]
    o_parts, o_first, o_second, lse, q, o_low, kv, vt, qm, top, total, accum, first, second, sem = rest[
        count:
    ]
    length = kv.shape[0]
    tiles = length // KTILE
    copies = piece_copies(where, ids, pieces, kv, sem, rows, classes)
    for copy in copies:
        copy.start()
    order_queries(ids, first_q, last_q, q, rows)
    for copy in copies:
        copy.wait()

    @pl.loop(0, tiles)
    def _(t):
        start = pl.multiple_of(t * KTILE, KTILE)
        vt[0:128, pl.ds(start, KTILE)] = kv[pl.ds(start, KTILE), 128:256].T
        vt[128:256, pl.ds(start, KTILE)] = kv[pl.ds(start, KTILE), 256:384].T

    v_row = (128, 192, 0)

    @pl.loop(0, q.shape[0] // QTILE)
    def _(j):
        base = pl.multiple_of(j * QTILE, QTILE)
        for head in range(OWN):
            block = q[pl.ds(base, QTILE), pl.ds(128 * K_BLOCK[head], 128)]
            qm[head] = lane_half(block, K_UPPER[head])
        top[...] = jnp.full_like(top, masked_value)
        total[...] = jnp.zeros_like(total)
        accum[...] = jnp.zeros_like(accum)

        stages = (first, second)

        def fetch(stage, start):
            for head in range(OWN):
                block = 128 * K_BLOCK[head]
                stages[stage][head] = lax.dot_general(
                    kv[pl.ds(start, KTILE), block : block + 128],
                    qm[head],
                    NT,
                    preferred_element_type=jnp.float32,
                )

        def work(stage, start, position):
            same = allowed(spans, base, position)
            for head in range(OWN):
                scores = jnp.where(same, stages[stage][head], masked_value)
                old = top[head : head + 1, :]
                new = jnp.maximum(old, jnp.max(scores, axis=0, keepdims=True))
                weights = jnp.exp(scores - new)
                factor = jnp.exp(old - new)
                top[head : head + 1, :] = new
                total[head : head + 1, :] = total[head : head + 1, :] * factor + jnp.sum(
                    weights, axis=0, keepdims=True
                )
                rows_v = slice(v_row[head], v_row[head] + 64)
                place = slice(64 * head, 64 * head + 64)
                accum[place, :] = accum[place, :] * factor + jnp.dot(
                    vt[rows_v, pl.ds(start, KTILE)],
                    weights.astype(jnp.bfloat16),
                    preferred_element_type=jnp.float32,
                )

        walk(flags, tiles, j, fetch, work)
        outs = [
            accum[64 * head : 64 * head + 64, :] / total[head : head + 1, :] for head in range(OWN)
        ]
        lower = jnp.concatenate(outs[:2], axis=0).T
        upper = jnp.concatenate([outs[2], jnp.zeros_like(outs[2])], axis=0).T
        o_first[pl.ds(base, QTILE), :] = lower
        o_second[pl.ds(base, QTILE), :] = upper
        o_low[pl.ds(base, QTILE), 0:128] = lower.astype(jnp.bfloat16)
        o_low[pl.ds(base, QTILE), 128:192] = upper[:, 0:64].astype(jnp.bfloat16)
        lse[:, pl.ds(base, QTILE)] = top[...] + jnp.log(total[...])

    for chunk in range(GROUPS):
        o_parts[chunk] = o_low[rows * chunk : rows * chunk + rows, :]


def backward_kernel(where, rows, classes, out_where, extra, ids, flags, first_q, last_q, spans, o_first, o_second, lse, *rest):
    count = len(where)
    grads, pieces = rest[0], rest[1 : 1 + count]
    rest = rest[1 + count + extra :]
    outs = rest[: len(out_where)]
    dq, q, grad, kv, kt, qm, dom, stats, dqt, dkv, low_kv, sem = rest[len(out_where) :]
    length = kv.shape[0]
    tiles = length // KTILE
    copies = piece_copies(where, ids, pieces, kv, sem, rows, classes)
    for copy in copies:
        copy.start()

    @pl.loop(0, tiles)
    def _(t):
        start = pl.multiple_of(t * KTILE, KTILE)
        dkv[pl.ds(start, KTILE), :] = jnp.zeros((KTILE, 384), jnp.float32)

    order_queries(ids, first_q, last_q, q, rows)
    for chunk in range(GROUPS):
        grad[rows * chunk : rows * chunk + rows, :] = jnp.concatenate(
            [grads[chunk], jnp.zeros((rows, 64), jnp.bfloat16)], axis=1
        )

    for copy in copies:
        copy.wait()

    @pl.loop(0, tiles)
    def _(t):
        start = pl.multiple_of(t * KTILE, KTILE)
        kt[0:128, pl.ds(start, KTILE)] = kv[pl.ds(start, KTILE), 0:128].T
        kt[128:256, pl.ds(start, KTILE)] = kv[pl.ds(start, KTILE), 128:256].T

    k_row = (0, 64, 192)

    @pl.loop(0, q.shape[0] // QTILE)
    def _(j):
        base = pl.multiple_of(j * QTILE, QTILE)
        for head in range(OWN):
            block = q[pl.ds(base, QTILE), pl.ds(128 * K_BLOCK[head], 128)]
            qm[head] = lane_half(block, K_UPPER[head])
            block = grad[pl.ds(base, QTILE), pl.ds(128 * (2 - V_BLOCK[head]), 128)]
            dom[head] = lane_half(block, V_UPPER[head])
        for part in range(2):
            product = (
                grad[pl.ds(base, QTILE), 128 * part : 128 * part + 128].astype(jnp.float32)
                * (o_first, o_second)[part][pl.ds(base, QTILE), :]
            ).T
            for half in range(2):
                head = 2 * part + half
                if head < OWN:
                    stats[head : head + 1, :] = jnp.sum(
                        product[64 * half : 64 * half + 64], axis=0, keepdims=True
                    )
        dqt[...] = jnp.zeros_like(dqt)

        def product(place, block, right):
            left = kv[place, 128 * block : 128 * block + 128]
            return lax.dot_general(left, right, NT, preferred_element_type=jnp.float32)

        @pl.loop(0, flags[j * (tiles + 1)])
        def _(i):
            start = pl.multiple_of(flags[j * (tiles + 1) + 1 + i] * KTILE, KTILE)
            place = pl.ds(start, KTILE)
            same = allowed(spans, base, start)
            sums = [None, None, None]

            def add(block, left, right):
                term = jnp.dot(left, right, preferred_element_type=jnp.float32)
                sums[block] = term if sums[block] is None else sums[block] + term

            for head in range(OWN):
                scores = product(place, K_BLOCK[head], qm[head])
                grad_probs = product(place, V_BLOCK[head], dom[head])
                probs = jnp.where(
                    same, jnp.exp(scores - lse[head : head + 1, pl.ds(base, QTILE)]), 0.0
                )
                grad_scores = (probs * (grad_probs - stats[head : head + 1, :])).astype(jnp.bfloat16)
                add(V_BLOCK[head], probs.astype(jnp.bfloat16), dom[head])
                add(K_BLOCK[head], grad_scores, qm[head])
                rows_k = slice(k_row[head], k_row[head] + 64)
                dqt[64 * head : 64 * head + 64, :] += jnp.dot(
                    kt[rows_k, place], grad_scores, preferred_element_type=jnp.float32
                )
            for block in range(3):
                dkv[place, 128 * block : 128 * block + 128] += sums[block]

        lower = dqt[0:128, :].T * 0.125
        upper = dqt[64:192, :].T * 0.125
        dq[pl.ds(base, QTILE), 0:128] = lower.astype(jnp.bfloat16)
        dq[pl.ds(base, QTILE), 128:192] = upper[:, 64:128].astype(jnp.bfloat16)

    @pl.loop(0, tiles)
    def _(t):
        start = pl.multiple_of(t * KTILE, KTILE)
        low_kv[pl.ds(start, KTILE), :] = dkv[pl.ds(start, KTILE), :].astype(jnp.bfloat16)

    copies = []
    for out, masks in zip(outs, out_where):
        for slot, mask in enumerate(masks):
            for flip in range(GROUPS):
                chunk = (ids[0] ^ flip) * classes + (ids[1] ^ mask)
                start = pl.multiple_of(chunk * rows, 64)
                copies.append(
                    pltpu.make_async_copy(
                        low_kv.at[pl.ds(start, rows), :], out.at[slot, flip], sem.at[len(copies)]
                    )
                )
    for copy in copies:
        copy.start()
    for copy in copies:
        copy.wait()


VMEM_SPEC = pl.BlockSpec(memory_space=pltpu.VMEM)
SMEM_SPEC = pl.BlockSpec(memory_space=pltpu.SMEM)
ANY_SPEC = pl.BlockSpec(memory_space=pl.ANY)
PARAMS = pltpu.CompilerParams(vmem_limit_bytes=56 * 1024 * 1024)


def attend_forward(ids, flags, first_q, last_q, spans, pieces, where, rows, classes):
    length = rows * classes * GROUPS
    queries = GROUPS * rows
    copies = sum(len(flips) for _, flips in where)
    return pl.pallas_call(
        functools.partial(forward_kernel, where, rows, classes),
        out_shape=(
            jax.ShapeDtypeStruct((GROUPS, rows, WIDTH), jnp.bfloat16),
            jax.ShapeDtypeStruct((queries, 128), jnp.float32),
            jax.ShapeDtypeStruct((queries, 128), jnp.float32),
            jax.ShapeDtypeStruct((8, queries), jnp.float32),
        ),
        in_specs=[SMEM_SPEC, SMEM_SPEC, VMEM_SPEC, VMEM_SPEC, VMEM_SPEC]
        + [ANY_SPEC] * len(pieces),
        out_specs=(VMEM_SPEC,) * 4,
        scratch_shapes=[
            pltpu.VMEM((queries, 256), jnp.bfloat16),
            pltpu.VMEM((queries, WIDTH), jnp.bfloat16),
            pltpu.VMEM((length, 384), jnp.bfloat16),
            pltpu.VMEM((256, length), jnp.bfloat16),
            pltpu.VMEM((OWN, QTILE, 128), jnp.bfloat16),
            pltpu.VMEM((8, QTILE), jnp.float32),
            pltpu.VMEM((8, QTILE), jnp.float32),
            pltpu.VMEM((WIDTH, QTILE), jnp.float32),
            pltpu.VMEM((OWN, KTILE, QTILE), jnp.float32),
            pltpu.VMEM((OWN, KTILE, QTILE), jnp.float32),
            pltpu.SemaphoreType.DMA((copies,)),
        ],
        compiler_params=PARAMS,
        cost_estimate=pl.CostEstimate(
            flops=queries * length * WIDTH * 4, bytes_accessed=8 << 20, transcendentals=0
        ),
        name="attend_forward",
    )(ids, flags, first_q, last_q, spans, *pieces)


def attend_backward(
    ids, flags, first_q, last_q, spans, grads, outputs, lse, pieces, after, where, rows, classes, out_where
):
    length = rows * classes * GROUPS
    queries = GROUPS * rows
    copies = sum(len(flips) for _, flips in where)
    return pl.pallas_call(
        functools.partial(backward_kernel, where, rows, classes, out_where, len(after)),
        out_shape=tuple(
            jax.ShapeDtypeStruct((len(masks), GROUPS, rows, 384), jnp.bfloat16)
            for masks in out_where
        )
        + (jax.ShapeDtypeStruct((queries, WIDTH), jnp.bfloat16),),
        in_specs=[SMEM_SPEC, SMEM_SPEC] + [VMEM_SPEC] * 7 + [ANY_SPEC] * (len(pieces) + len(after)),
        out_specs=(ANY_SPEC,) * len(out_where) + (VMEM_SPEC,),
        scratch_shapes=[
            pltpu.VMEM((queries, 256), jnp.bfloat16),
            pltpu.VMEM((queries, 256), jnp.bfloat16),
            pltpu.VMEM((length, 384), jnp.bfloat16),
            pltpu.VMEM((256, length), jnp.bfloat16),
            pltpu.VMEM((OWN, QTILE, 128), jnp.bfloat16),
            pltpu.VMEM((OWN, QTILE, 128), jnp.bfloat16),
            pltpu.VMEM((8, QTILE), jnp.float32),
            pltpu.VMEM((WIDTH, QTILE), jnp.float32),
            pltpu.VMEM((length, 384), jnp.float32),
            pltpu.VMEM((length, 384), jnp.bfloat16),
            pltpu.SemaphoreType.DMA((copies,)),
        ],
        compiler_params=PARAMS,
        cost_estimate=pl.CostEstimate(
            flops=queries * length * WIDTH * 10, bytes_accessed=16 << 20, transcendentals=0
        ),
        name="attend_backward",
    )(ids, flags, first_q, last_q, spans, *outputs, lse, grads, *pieces, *after)


def pick_kernel(ids, w_q, w_k, w_v, out):
    odd = (ids[3] & 1) == 1
    start = pl.multiple_of((ids[3] // 2) * 384 + (ids[3] & 1) * 128, 128)

    def take(weight):
        both = weight[:, pl.ds(start, 256)]
        return jnp.where(odd, both[:, 64:256], both[:, 0:192])

    q, k, v = take(w_q), take(w_k), take(w_v)
    out[...] = jnp.concatenate(
        [k[:, :128], v[:, 128:], k[:, 128:], v[:, :128], q[:, :128], jnp.zeros_like(q[:, :64]), q[:, 128:]],
        axis=1,
    )


def pick_weights(ids, w_q, w_k, w_v):
    return pl.pallas_call(
        pick_kernel,
        out_shape=jax.ShapeDtypeStruct((w_q.shape[0], 640), jnp.bfloat16),
        in_specs=[SMEM_SPEC] + [VMEM_SPEC] * 3,
        out_specs=VMEM_SPEC,
        compiler_params=PARAMS,
        name="pick_weights",
    )(ids, w_q, w_k, w_v)


def project_kernel(count, parts, ids, bias, *rest):
    tokens, weights, (kv, q) = rest[:count], rest[count : count + parts], rest[count + parts :]
    rows = weights[0].shape[0]
    for i, chunk in enumerate(tokens):
        total = bias[...]
        for part, weight in enumerate(weights):
            lanes = (0 if parts == 1 else ids[0] ^ part) * rows
            left = chunk[:, pl.ds(pl.multiple_of(lanes, 128), rows)]
            total = total + jnp.dot(left, weight[...], preferred_element_type=jnp.float32)
        kv[i] = total[:, :384].astype(jnp.bfloat16)
        q[chunk.shape[0] * i : chunk.shape[0] * (i + 1), :] = (
            total[:, 384:].astype(jnp.bfloat16) * jnp.bfloat16(0.125)
        )


def project(ids, bias, chunks, weights):
    count, rows = len(chunks), chunks[0].shape[0]
    return pl.pallas_call(
        functools.partial(project_kernel, count, len(weights)),
        out_shape=(
            jax.ShapeDtypeStruct((count, rows, 384), jnp.bfloat16),
            jax.ShapeDtypeStruct((count * rows, 256), jnp.bfloat16),
        ),
        in_specs=[SMEM_SPEC] + [VMEM_SPEC] * (1 + count + len(weights)),
        out_specs=(VMEM_SPEC, VMEM_SPEC),
        compiler_params=PARAMS,
        cost_estimate=pl.CostEstimate(
            flops=2 * count * rows * D * 640, bytes_accessed=2 << 20, transcendentals=0
        ),
        name="project",
    )(ids, bias, *chunks, *weights)


def tn(left, right):
    return lax.dot_general(
        left, right, (((0,), (0,)), ((), ())), preferred_element_type=jnp.float32
    )


def down_grad_kernel(active, g_low, after, down):
    part = tn(active[...], g_low[...]).astype(jnp.bfloat16)
    for unit in range(4):
        for half in range(2):
            row = (unit % 2) * 192 + 96 * half
            down[unit // 2, 0, row : row + 96, :] = part[
                96 * unit : 96 * unit + 96, 384 * half : 384 * half + 384
            ]


def down_grad(active, g_low, after):
    rows = active.shape[0]
    return pl.pallas_call(
        down_grad_kernel,
        out_shape=jax.ShapeDtypeStruct((4, 4, 384, 384), jnp.bfloat16),
        grid=(8,),
        in_specs=[
            pl.BlockSpec((rows, 384), lambda i: (0, i)),
            pl.BlockSpec((rows, D), lambda i: (0, 0)),
            ANY_SPEC,
        ],
        out_specs=pl.BlockSpec((2, 1, 384, 384), lambda i: (i % 2, (i // 2) % 2 * 2 + i // 4, 0, 0)),
        compiler_params=PARAMS,
        cost_estimate=pl.CostEstimate(
            flops=2 * rows * D * FF, bytes_accessed=8 << 20, transcendentals=0
        ),
        name="down_grad",
    )(active, g_low, after).reshape(2 * FF, D // 2)


def turn(index):
    return (index & 1) * 2 + index // 2


def upper_grad_kernel(ids, hid, g_raised, attn, g_att, vec, after, near, far):
    core, group = ids[1], ids[3]
    outer = tn(attn[...], g_att[...]).astype(jnp.bfloat16)
    left = hid[...].T
    for k in range(GROUPS):
        lanes = slice(384 * k, 384 * k + 384)
        part = jnp.dot(left, g_raised[:, lanes], preferred_element_type=jnp.float32)
        part = part.astype(jnp.bfloat16)
        place = turn(k ^ group)
        for target, own in ((near, core == 0), (far, core != 0)):
            target[place, 0:192, :] = jnp.where(own, part[:192], part[192:])
            first, second = (outer[192 * b + 48 * k : 192 * b + 48 * k + 48] for b in range(2))
            target[place, 192:240, :] = jnp.where(own, first, second)
            target[place, 240:256, :] = vec[k]


def upper_grad(ids, hid, g_raised, attn, g_att, vec, after):
    rows = hid.shape[0]

    def place(i, j, ids):
        return ((j ^ ids[2]) * 2 + (i ^ ids[0]), 0, 0)

    return pl.pallas_call(
        upper_grad_kernel,
        out_shape=(jax.ShapeDtypeStruct((16, 256, 384), jnp.bfloat16),) * 2,
        grid_spec=pltpu.PrefetchScalarGridSpec(
            num_scalar_prefetch=1,
            grid=(2, 2),
            in_specs=[
                pl.BlockSpec((rows, 384), lambda i, j, ids: (0, i)),
                pl.BlockSpec((rows, 1536), lambda i, j, ids: (0, j)),
                pl.BlockSpec((rows, 384), lambda i, j, ids: (0, i)),
                pl.BlockSpec((rows, 384), lambda i, j, ids: (0, j)),
                pl.BlockSpec((4, 16, 384), lambda i, j, ids: (j, 0, 0)),
                ANY_SPEC,
            ],
            out_specs=(pl.BlockSpec((4, 256, 384), place),) * 2,
        ),
        compiler_params=PARAMS,
        cost_estimate=pl.CostEstimate(
            flops=2 * rows * D * (FF + D), bytes_accessed=12 << 20, transcendentals=0
        ),
        name="upper_grad",
    )(ids, hid, g_raised, attn, g_att, vec, after)


def unpack_ffn_kernel(ids, block_own, block_other, up, out, down, *vecs):
    side, core, mid, group = ids[0], ids[1], ids[2], ids[3]
    b, j = pl.program_id(0) ^ core, pl.program_id(1)
    own = pl.program_id(0) == 0
    for k in range(GROUPS):
        place = turn(k ^ group)
        part = jnp.where(own, block_own[place], block_other[place]).astype(jnp.float32)
        up[:, 384 * k : 384 * k + 384] = part[0:192]
        out[48 * k : 48 * k + 48, :] = part[192:240]
        rows = pl.ds(pl.multiple_of(96 * j, 32) + 192 * k, 96)
        down[rows, 0:384] = part[256:352]
        down[rows, 384:768] = part[352:448]

    @pl.when(b == 0)
    def _():
        for u in range(8):
            place = turn((u % 4) ^ group)
            rows = jnp.where(own, block_own[place, 240:256, :], block_other[place, 240:256, :])
            rows = rows.astype(jnp.float32)
            for r in range(3):
                row = 3 * u + r
                if row < 12:
                    target, where, half = vecs[row // 2], 0, row % 2
                elif row < 20:
                    target, where, half = vecs[6], (row - 12) % 4, (row - 12) // 4
                else:
                    continue

                @pl.when((j == u // 4) & (side == half))
                def _():
                    target[384 * where : 384 * where + 384] = rows[r]


def unpack_ffn(ids, own, other):
    def source_own(d, j, ids):
        return (jnp.where(d == 0, j, 1) ^ ids[2], 0, 0)

    def source_other(d, j, ids):
        return (jnp.where(d == 0, 0, j) ^ ids[2], 0, 0)

    sizes = [384] * 6 + [1536]
    return pl.pallas_call(
        unpack_ffn_kernel,
        out_shape=(
            jax.ShapeDtypeStruct((384, FF), jnp.float32),
            jax.ShapeDtypeStruct((384, D), jnp.float32),
            jax.ShapeDtypeStruct((FF // 2, D), jnp.float32),
        )
        + tuple(jax.ShapeDtypeStruct((size,), jnp.float32) for size in sizes),
        grid_spec=pltpu.PrefetchScalarGridSpec(
            num_scalar_prefetch=1,
            grid=(2, 2),
            in_specs=[pl.BlockSpec((4, 448, 384), source_own), pl.BlockSpec((4, 448, 384), source_other)],
            out_specs=(
                pl.BlockSpec((192, 1536), lambda d, j, ids: (d ^ ids[1], j)),
                pl.BlockSpec((192, 384), lambda d, j, ids: (d ^ ids[1], j)),
                pl.BlockSpec((FF // 4, D), lambda d, j, ids: (d ^ ids[1], 0)),
            )
            + tuple(pl.BlockSpec((size,), lambda d, j, ids: (0,)) for size in sizes),
        ),
        compiler_params=PARAMS,
        name="unpack_ffn",
    )(ids, own, other)


def qkv_grad_kernel(ids, t0, t1, t2, t3, *rest):
    kept, given, sent, dq, near, far, both, whole = rest
    x, c = ids[0], ids[1]
    rows = dq.shape[0] // GROUPS
    total = jnp.zeros((1, 576), jnp.float32)
    for flip in range(GROUPS):
        term = (
            kept[0, flip].astype(jnp.float32)
            + given[0, flip].astype(jnp.float32)
            + sent[flip].astype(jnp.float32)
        ).astype(jnp.bfloat16)
        own = slice(rows * flip, rows * flip + rows)
        start = pl.multiple_of((flip ^ ids[3]) * rows, 64)
        block = jnp.concatenate([term, dq[pl.ds(start, rows), :]], axis=1)
        both[flip ^ ids[3]] = block
        whole[own, :] = block
        total = total + jnp.sum(block.astype(jnp.float32), axis=0, keepdims=True)
    first = lax.broadcasted_iota(jnp.int32, (16, 576), 0) == 0
    total = jnp.where(first, jnp.broadcast_to(total, (16, 576)), 0.0).astype(jnp.bfloat16)

    @pl.loop(0, 2)
    def _(i):
        lanes = pl.ds(pl.multiple_of(i * 384, 128), 384)
        left = jnp.concatenate([t[:, lanes] for t in (t0, t1, t2, t3)], axis=0)
        part = tn(left, whole[...]).astype(jnp.bfloat16)
        for b in range(2):

            def store(target):
                target[i ^ x, 0:192, :] = part[192 * b : 192 * b + 192]

            pl.when(c == b)(functools.partial(store, near))
            pl.when(c != b)(functools.partial(store, far))
        near[i ^ x, 192:208, :] = total
        far[i ^ x, 192:208, :] = total


def qkv_grads(ids, tokens, kept, given, sent, dq):
    queries = dq.shape[0]
    rows = queries // GROUPS
    return pl.pallas_call(
        qkv_grad_kernel,
        out_shape=(jax.ShapeDtypeStruct((2, 208, 576), jnp.bfloat16),) * 2
        + (jax.ShapeDtypeStruct((GROUPS, rows, 576), jnp.bfloat16),),
        in_specs=[SMEM_SPEC] + [VMEM_SPEC] * 8,
        out_specs=(VMEM_SPEC,) * 3,
        scratch_shapes=[pltpu.VMEM((queries, 576), jnp.bfloat16)],
        compiler_params=PARAMS,
        cost_estimate=pl.CostEstimate(
            flops=2 * queries * D * 576, bytes_accessed=4 << 20, transcendentals=0
        ),
        name="qkv_grads",
    )(ids, *tokens, kept, given, sent, dq)


def unpack_qkv_kernel(ids, own, other, out_q, out_k, out_v, vec):
    c, h = ids[1], ids[3]
    for b in range(2):
        q, k, v = [], [], []
        for g in range(GROUPS):
            block = jnp.where(c == b, own[turn(g ^ h), 0:192, :], other[turn(g ^ h), 0:192, :]).astype(jnp.float32)
            k += [block[:, 0:128], block[:, 192:256]]
            v += [block[:, 256:384], block[:, 128:192]]
            q += [block[:, 384:576]]
        for out, parts in ((out_q, q), (out_k, k), (out_v, v)):
            out[192 * b : 192 * b + 192, :] = jnp.concatenate(parts, axis=1)
    for g in range(GROUPS):
        vec[g] = jnp.where(c == 0, own[turn(g ^ h), 192:208, :], other[turn(g ^ h), 192:208, :]).astype(jnp.float32)


def unpack_qkv(ids, own, other):
    return pl.pallas_call(
        unpack_qkv_kernel,
        out_shape=(jax.ShapeDtypeStruct((384, D), jnp.float32),) * 3
        + (jax.ShapeDtypeStruct((GROUPS, 16, 576), jnp.float32),),
        in_specs=[SMEM_SPEC, VMEM_SPEC, VMEM_SPEC],
        out_specs=(VMEM_SPEC,) * 4,
        compiler_params=PARAMS,
        name="unpack_qkv",
    )(ids, own, other)


def token_grad_kernel(base, both, weight, out):
    total = base[...]
    for g in range(GROUPS):
        w = weight[:, 640 * g : 640 * g + 576]
        total = total + lax.dot_general(both[g], w, NT, preferred_element_type=jnp.float32)
    out[...] = total


def token_grads(base, both, weight):
    return pl.pallas_call(
        token_grad_kernel,
        out_shape=jax.ShapeDtypeStruct(base.shape, jnp.float32),
        in_specs=[VMEM_SPEC] * 3,
        out_specs=VMEM_SPEC,
        compiler_params=PARAMS,
        cost_estimate=pl.CostEstimate(
            flops=2 * base.shape[0] * D * 2304, bytes_accessed=8 << 20, transcendentals=0
        ),
        name="token_grads",
    )(base, both, weight)


def gather_rows(weight, core, *others):
    half = weight.shape[0] // 2
    part = tie(lax.dynamic_slice_in_dim(weight, core * half, half, 0), *others)
    return lax.all_gather(part, ("wa", "c"), axis=0, tiled=True)


def reduce_blocks(grad):
    flat = grad.reshape((-1,) + grad.shape[2:])
    mine = lax.psum_scatter(flat, ("wa", "c"), scatter_dimension=0, tiled=True)
    mine = lax.psum_scatter(mine, "m", scatter_dimension=0, tiled=True)
    mine = lax.psum_scatter(mine, "h", scatter_dimension=0, tiled=True)
    return lax.all_gather(mine, ("c", "m", "h"), axis=0, tiled=True)


def tie(array, *others):
    return lax.optimization_barrier((array,) + others)[0]


def both_sum(near, far, *others):
    near = tie(near, *others)
    return low(widen(near) + widen(far))


def fold(near, far, *others):
    near = tie(near, *others)
    return [low(widen(near[i]) + widen(far[i])) for i in range(2)]


def double(array, axis, bit):
    return jnp.concatenate([array, swap(array, axis, bit)], axis=0)


def pick_columns(weight, group):
    q, k, v = (lax.dynamic_slice_in_dim(w, group * WIDTH, WIDTH, w.ndim - 1) for w in weight)
    return jnp.concatenate(
        [
            k[..., :128],
            v[..., 128:],
            k[..., 128:],
            v[..., :128],
            q[..., :128],
            jnp.zeros_like(q[..., :64]),
            q[..., 128:],
        ],
        axis=-1,
    )


def per_device(
    tokens,
    segment_ids,
    cotangent,
    w_query,
    w_key,
    w_value,
    w_out,
    w_up,
    w_down,
    b_query,
    b_value,
    b_out,
    gain_one,
    shift_one,
    b_up,
    b_down,
    gain_two,
    shift_two,
):
    mid = lax.axis_size("m")
    wide = lax.axis_size("wa")
    paired = mid == 2 and wide == 2
    classes = 2 * mid
    group = lax.axis_index("h")
    core = lax.axis_index("c")
    kind = lax.axis_index("m") * 2 + core
    side = lax.axis_index("wa")
    inputs = tokens[0]
    count = inputs.shape[0]
    chunks = GROUPS * classes
    length = count * chunks
    tiles = length // KTILE
    ids = jnp.stack([group, kind]).astype(jnp.int32)
    place_ids = jnp.stack([side, core, lax.axis_index("m"), group]).astype(jnp.int32)
    order = group ^ jnp.arange(GROUPS)

    second = swap(inputs, "h", 1)
    third = swap(inputs, "h", 2)
    if wide == 2:
        w_own = pick_weights(place_ids, w_query, w_key, w_value)
        w_other = swap(w_own, "wa", 1)
    else:
        w_own = None
        w_other = lax.all_gather(
            pick_columns((w_query, w_key, w_value), group), "wa", axis=0, tiled=True
        )

    smalls = [b_query, b_value, b_out, gain_one, shift_one, b_up, b_down, gain_two, shift_two]
    joined = lax.all_gather(jnp.concatenate(smalls), "wa", axis=0)
    second, third, w_other, joined = lax.optimization_barrier((second, third, w_other, joined))
    fourth = swap(third, "h", 1)
    full, place = [], 0
    for item in smalls:
        size = item.shape[0]
        full.append(widen(joined[:, place : place + size].reshape(-1)))
        place += size
    bias_query, bias_value, bias_out, gain_attn, shift_attn, bias_up, bias_down, gain_ffn, shift_ffn = full
    b_group = pick_columns((bias_query, jnp.zeros_like(bias_query), bias_value), group)[None]

    w_group = (w_own, w_other) if wide == 2 else (w_other,)
    full_out = gather_rows(w_out, core, w_other)
    full_up = gather_rows(w_up, core, w_other)
    full_down = gather_rows(w_down, core, w_other)
    where, pieces = [], []

    def spread(piece, flips):
        have = {0: piece}
        bit = 1
        while bit < mid:
            for mask in list(have):
                have[mask | (bit << 1)] = swap(have[mask], "m", bit)
            bit *= 2
        for mask in list(have):
            have[mask | 1] = swap(have[mask], "c", 1)
        for mask, item in have.items():
            where.append((mask, flips))
            pieces.append(item)

    first_kv, first_q = project(place_ids, b_group, (inputs, second, third), w_group)
    spread(first_kv, (0, 1, 2))

    segs = double(tie(segment_ids, first_kv), "c", 1)
    bit = 1
    while bit < mid:
        segs = double(segs, "m", bit)
        bit *= 2
    segs = double(double(segs, "h", 1), "h", 2)
    segs = jnp.take(segs, (group * classes + kind) ^ jnp.arange(chunks), axis=0)

    own_segs = lax.dynamic_index_in_dim(
        segs.reshape(GROUPS, classes, count), kind, 1, keepdims=False
    ).reshape(-1)

    names = jnp.arange(DOCS)
    begins = jnp.sum((segs.reshape(-1, 1) < names).astype(jnp.int32), axis=0)
    ends = jnp.sum((segs.reshape(-1, 1) <= names).astype(jnp.int32), axis=0)
    chosen = own_segs[None, :] == names[:, None]
    begins = jnp.sum(jnp.where(chosen, begins[:, None], 0), axis=0)
    ends = jnp.sum(jnp.where(chosen, ends[:, None], 0), axis=0)
    spans = jnp.concatenate(
        [begins[None], ends[None], jnp.zeros((6, begins.shape[0]), jnp.int32)], axis=0
    )
    edges = (jnp.arange(tiles) * KTILE)[None, :, None]
    meets = (begins.reshape(-1, 1, QTILE) < edges + KTILE) & (ends.reshape(-1, 1, QTILE) > edges)
    meets = jnp.any(meets, axis=-1).astype(jnp.int32)
    rank = jnp.cumsum(meets, axis=1)
    slots = (rank[:, None, :] == jnp.arange(1, tiles + 1)[None, :, None]) & (meets[:, None, :] > 0)
    listed = jnp.sum(jnp.where(slots, jnp.arange(tiles), 0), axis=-1)
    flags = jnp.concatenate([rank[:, -1:], listed], axis=1).astype(jnp.int32).reshape(-1)

    last_kv, last_q = project(place_ids, b_group, (fourth,), w_group)
    spread(last_kv, (3,))
    where = tuple(where)
    group_tokens = [inputs, second, third, fourth]

    o_parts, o_first, o_second, lse = attend_forward(
        ids, flags, first_q, last_q, spans, pieces, where, count, classes
    )

    w_query, w_key, w_value = (tie(item, lse) for item in (w_query, w_key, w_value))
    columns = []
    for g in range(GROUPS):
        low_part, high_part = slice(192 * g, 192 * g + 128), slice(192 * g + 128, 192 * g + 192)
        columns += [w_key[:, low_part], w_value[:, high_part], w_key[:, high_part], w_value[:, low_part]]
        columns += [w_query[:, 192 * g : 192 * g + 192], jnp.zeros_like(w_query[:, :64])]
    by_group = gather_rows(jnp.concatenate(columns, axis=1), core)

    def send_back(parts):
        return lax.all_to_all(parts, "h", 0, 0, tiled=True)

    attn_low = jnp.transpose(send_back(o_parts), (1, 0, 2)).reshape(count, D)
    attended = mm(attn_low, full_out) + bias_out
    hidden, unit_one, scale_one = norm_forward(widen(inputs) + attended, gain_attn, shift_attn)
    hidden_low = low(hidden)
    raised = mm(hidden_low, full_up) + bias_up
    active, slope = gelu_pair(raised)
    active_low = low(active)
    lowered = mm(active_low, full_down) + bias_down
    result, unit_two, scale_two = norm_forward(hidden + lowered, gain_ffn, shift_ffn)
    grad_sum_two, grad_gain_two, grad_shift_two = norm_backward(
        widen(cotangent[0]), unit_two, scale_two, gain_ffn
    )
    grad_lowered = low(grad_sum_two)
    grad_b_down = jnp.sum(widen(grad_lowered), axis=0)
    grad_raised = low(back_product(grad_lowered, full_down) * slope)
    grad_b_up = jnp.sum(widen(grad_raised), axis=0)
    grad_hidden = grad_sum_two + back_product(grad_raised, full_up)
    grad_sum_one, grad_gain_one, grad_shift_one = norm_backward(
        grad_hidden, unit_one, scale_one, gain_attn
    )
    grad_attended = low(grad_sum_one)
    grad_b_out = jnp.sum(widen(grad_attended), axis=0)
    grad_attn = low(back_product(grad_attended, full_out))

    grad_rows = send_back(jnp.transpose(grad_attn.reshape(count, GROUPS, WIDTH), (1, 0, 2)))

    vectors = jnp.concatenate(
        [grad_b_out, grad_gain_one, grad_shift_one, grad_b_down, grad_gain_two, grad_shift_two, grad_b_up]
    )
    blocks = 2 * wide
    if paired:
        vectors = jnp.pad(low(vectors), (0, 9216 - 7680)).reshape(8, 3, 384)
        vectors = jnp.pad(vectors, ((0, 0), (0, 13), (0, 0)))
        near, far = upper_grad(
            place_ids, hidden_low, grad_raised, attn_low, grad_attended, vectors, by_group
        )
        shape = (2, 2, 2, 2, 256, 384)
        near, far = near.reshape(shape), swap(far, "c", 1).reshape(shape)
        grad_rows = tie(grad_rows, near)
        down_sum = down_grad(active_low, grad_lowered, near)
        upper, give = fold(near, far, down_sum)
        after = (give,)
        give = swap(give, "m", 1)
        down_sum = tie(down_sum, grad_rows)
        down_sum = lax.psum_scatter(down_sum, ("h", "c"), scatter_dimension=0, tiled=True)
    else:
        grad_w_down = low(outer_sum(active_low, grad_lowered))
        grad_w_up = low(outer_sum(hidden_low, grad_raised))
        grad_w_out = low(outer_sum(attn_low, grad_attended))
        vectors = jnp.pad(low(vectors).reshape(-1, D), ((0, 6), (0, 0)))
        down_rows, out_rows = FF // blocks, D // blocks
        ffn = jnp.concatenate(
            [
                grad_w_down.reshape(blocks, down_rows, D),
                grad_w_up.reshape(blocks, down_rows, D),
                grad_w_out.reshape(blocks, out_rows, D),
                jnp.broadcast_to(vectors[None], (blocks, 16, D)),
            ],
            axis=1,
        )
        after = ()
        ffn_sum = reduce_blocks(ffn).reshape(2, -1, D)
        out_down = widen(ffn_sum[:, :down_rows]).reshape(-1, D)
        out_up = widen(ffn_sum[:, down_rows : 2 * down_rows]).reshape(-1, FF)
        place = 2 * down_rows
        out_out = widen(ffn_sum[:, place : place + out_rows]).reshape(-1, D)
        small = widen(ffn_sum[0, place + out_rows :])

        def share(row, rows):
            vector = small[row : row + rows].reshape(-1)
            size = vector.shape[0] // wide
            return lax.dynamic_slice_in_dim(vector, side * size, size, 0)

        vectors = [share(row, 1) for row in range(6)] + [share(6, 4)]

    stay_masks, leave_masks = tuple(range(0, classes, 2)), tuple(range(1, classes, 2))
    out_where = (stay_masks,) + tuple((mask,) for mask in leave_masks)

    kept, *given, dq = attend_backward(
        ids, flags, first_q, last_q, spans, grad_rows, (o_first, o_second), lse,
        pieces, after, where, count, classes, out_where,
    )

    given = [swap(item, "c", 1) for item in given]
    if paired:
        upper, give = fold(upper, give, dq)
        kept = tie(kept, give)
        sent = low(widen(kept[1]) + widen(given[1][0]))
        down_sum = lax.psum_scatter(tie(down_sum, sent), "wa", scatter_dimension=0, tiled=True)
        give = swap(give, "wa", 1)
        upper = tie(upper, sent)
        sent = swap(sent, "m", 1)
        upper, give = fold(upper, give)
        kept = tie(kept, give)
        give = swap(give, "h", 1)
    else:
        partial = widen(kept) + widen(jnp.concatenate(given, axis=0))
        stay = list(stay_masks)
        bit = mid // 2
        while bit >= 1:
            mask = bit << 1
            near = [i for i, m in enumerate(stay) if not m & mask]
            far = [i for i, m in enumerate(stay) if m & mask]
            sent = swap(low(partial[far[0] : far[-1] + 1]), "m", bit)
            partial = widen(low(partial[near[0] : near[-1] + 1])) + widen(sent)
            stay = [stay[i] for i in near]
            bit //= 2
        dkv = low(partial[0]).reshape(GROUPS * count, 384)

    part = D // wide
    if paired:
        near, far, parts = qkv_grads(place_ids, group_tokens, kept, given[0], sent, dq)
        far = swap(far, "c", 1)
        down_sum = lax.psum_scatter(tie(down_sum, near), "m", scatter_dimension=0, tiled=True)
        upper, give = fold(upper, give, near)
        near = tie(near, give)
        give = swap(give, "h", 2)
        qkv, other = fold(near, far)
        other = swap(other, "wa", 1)
        upper = both_sum(upper, give, qkv)
        joint = jnp.concatenate([upper, down_sum], axis=0)
        joint_other = swap(joint, "h", 2)
        qkv = both_sum(qkv, other, joint)
        other = swap(qkv, "m", 1)
        qkv = both_sum(qkv, other)
        other = swap(qkv, "h", 2)
        joint = jnp.stack([tie(joint, qkv), joint_other])
        joint_other = swap(joint, "h", 1)
        qkv = jnp.stack([tie(qkv, joint), other])
        other = swap(qkv, "h", 1)
        joint = jnp.stack([tie(joint, qkv), joint_other])
        joint_other = swap(joint, "m", 1)
        parts = send_back(tie(parts, joint))
        qkv = jnp.concatenate([tie(qkv, joint), other], axis=0)
        other = swap(qkv, "c", 1)
        grad_inputs = token_grads(tie(grad_sum_one, qkv), parts, by_group)
        joint = jnp.stack([tie(joint, grad_inputs), joint_other])
        joint_other = swap(joint, "c", 1)
        out_query, out_key, out_value, sums = unpack_qkv(place_ids, tie(qkv, joint), other)
        joint = tie(joint, out_query)
        joint, joint_other = (item.reshape(8, 448, 384) for item in (tie(joint, out_query), joint_other))
        out_up, out_out, out_down, *vectors = unpack_ffn(place_ids, joint, joint_other)
        sums = sums[:, 0]
        sums_v = jnp.concatenate([sums[:, 256:384], sums[:, 128:192]], axis=1).reshape(-1)
        sums_q = sums[:, 384:576].reshape(-1)
    else:
        dq = jnp.take(dq.reshape(GROUPS, count, WIDTH), order, axis=0).reshape(-1, WIDTH)
        both = jnp.concatenate([dkv, dq], axis=1)
        width = both.shape[1]
        parts = send_back(jnp.take(both.reshape(GROUPS, count, width), order, axis=0))
        w_grad = low(outer_sum(jnp.concatenate(group_tokens, axis=0), both)).reshape(blocks, D // blocks, width)
        b_grad = low(jnp.sum(widen(both), axis=0))
        b_grad = jnp.pad(b_grad[None], ((0, 15), (0, 0)))
        qkv = jnp.concatenate([w_grad, jnp.broadcast_to(b_grad[None], (blocks, 16, width))], axis=1)
        rows = qkv.shape[1]
        mine = lax.psum_scatter(
            qkv.reshape(blocks * rows, width), ("wa", "c"), scatter_dimension=0, tiled=True
        )
        mine = lax.psum(mine, "m")
        every = widen(lax.all_gather(mine, ("c", "h"), axis=0).reshape(2, GROUPS, rows, width))

        def columns(block):
            k = jnp.concatenate([block[..., :128], block[..., 192:256]], axis=-1)
            v = jnp.concatenate([block[..., 256:384], block[..., 128:192]], axis=-1)
            q = block[..., 384:576]
            return [jnp.transpose(item, (0, 2, 1, 3)).reshape(2, -1, D) for item in (q, k, v)]

        out_query, out_key, out_value = (
            item.reshape(-1, D) for item in columns(every[:, :, : rows - 16])
        )
        sums_q, _, sums_v = (item[0, 0] for item in columns(every[:, :, rows - 16 : rows - 15]))
        grad_inputs = token_grads(grad_sum_one, parts, by_group)
    out_b_query = lax.dynamic_slice_in_dim(sums_q, side * part, part, 0)
    out_b_value = lax.dynamic_slice_in_dim(sums_v, side * part, part, 0)

    return (
        low(result)[None],
        grad_inputs[None],
        out_query,
        out_key,
        out_value,
        out_out,
        out_up,
        out_down,
        out_b_query,
        out_b_value,
        vectors[0],
        vectors[1],
        vectors[2],
        vectors[6],
        vectors[3],
        vectors[4],
        vectors[5],
    )


def solution(mesh):
    chunks, wide = mesh.devices.shape
    finer = Mesh(
        mesh.devices.reshape(GROUPS, chunks // (2 * GROUPS), 2, wide), ("h", "m", "c", "wa")
    )
    ctx = ("h", "m", "c")
    seq3, seq2 = P("wa", ctx, None), P("wa", ctx)
    matrix, vector = P("wa", None), P("wa")
    return jax.shard_map(
        per_device,
        mesh=finer,
        in_specs=(seq3, seq2, seq3) + (matrix,) * 6 + (vector,) * 9,
        out_specs=(seq3, seq3) + (matrix,) * 6 + (vector,) * 9,
        check_vma=False,
    )
```

```python
import functools

import jax
import jax.numpy as jnp
from jax import lax
from jax.experimental import pallas as pl
from jax.experimental.pallas import tpu as pltpu
from jax.sharding import Mesh
from jax.sharding import PartitionSpec as P

D = 768
HEADS = 12
HEAD_DIM = 64
FF = 3072
DOCS = 32

GROUPS = 4
OWN = HEADS // GROUPS
WIDTH = OWN * HEAD_DIM
QTILE = 256
KTILE = 512

epsilon = 1e-05
masked_value = -1e30
NT = (((1,), (1,)), ((), ()))
NN = (((1,), (0,)), ((), ()))


def widen(array):
    return array.astype(jnp.float32)


def low(array):
    return array.astype(jnp.bfloat16)


def mm(left, right):
    return jnp.dot(left, right, preferred_element_type=jnp.float32)


def outer_sum(left, right):
    return lax.dot_general(
        left, right, (((0,), (0,)), ((), ())), preferred_element_type=jnp.float32
    )


def back_product(grad, weight):
    return lax.dot_general(grad, weight, NT, preferred_element_type=jnp.float32)


def norm_forward(values, gain, shift):
    centre = values - jnp.mean(values, axis=-1, keepdims=True)
    scale = lax.rsqrt(jnp.mean(centre * centre, axis=-1, keepdims=True) + epsilon)
    unit = centre * scale
    return (unit * gain + shift, unit, scale)


def norm_backward(grad, unit, scale, gain):
    grad_gain = jnp.sum(grad * unit, axis=0)
    grad_shift = jnp.sum(grad, axis=0)
    inner = grad * gain
    grad_in = scale * (
        inner
        - jnp.mean(inner, axis=-1, keepdims=True)
        - unit * jnp.mean(inner * unit, axis=-1, keepdims=True)
    )
    return (grad_in, grad_gain, grad_shift)


def gelu_pair(values):
    cumulative = 0.5 * (1.0 + lax.erf(values * 0.7071067811865476))
    density = jnp.exp(-0.5 * values * values) * 0.3989422804014327
    return (values * cumulative, cumulative + values * density)


def swap(array, axis, bit):
    size = lax.axis_size(axis)
    return lax.ppermute(array, axis, [(i, i ^ bit) for i in range(size)])


K_BLOCK = (0, 0, 1)
V_BLOCK = (2, 2, 1)
K_UPPER = (False, True, True)
V_UPPER = (False, True, False)


def lane_half(array, upper):
    lane = lax.broadcasted_iota(jnp.int32, array.shape, 1)
    keep = (lane >= 64) if upper else (lane < 64)
    return jnp.where(keep, array, jnp.zeros_like(array))


def piece_copies(where, ids, pieces, kv, sem, rows, classes):
    copies = []
    for piece, (mask, flips) in zip(pieces, where):
        for slot, flip in enumerate(flips):
            chunk = (ids[0] ^ flip) * classes + (ids[1] ^ mask)
            start = pl.multiple_of(chunk * rows, 64)
            copies.append(
                pltpu.make_async_copy(
                    piece.at[slot], kv.at[pl.ds(start, rows), :], sem.at[len(copies)]
                )
            )
    return copies


def order_queries(ids, first_q, last_q, q, rows):
    for flip in range(GROUPS):
        part, place = (last_q, 0) if flip == 3 else (first_q, rows * flip)
        start = pl.multiple_of((ids[0] ^ flip) * rows, 64)
        q[pl.ds(start, rows), :] = part[place : place + rows, :]


def allowed(spans, base, start):
    position = lax.broadcasted_iota(jnp.int32, (KTILE, QTILE), 0)
    first = spans[0:1, pl.ds(base, QTILE)] - start
    last = spans[1:2, pl.ds(base, QTILE)] - start
    return (position >= first) & (position < last)


def walk(steps, tiles, j, fetch, work):
    amount = steps[j * (tiles + 1)]

    def tile(i):
        index = steps[j * (tiles + 1) + 1 + jnp.minimum(i, amount - 1)]
        start = pl.multiple_of(index * KTILE, KTILE)
        return start, jnp.where(i < amount, start, -(1 << 24))

    fetch(0, tile(0)[0])

    @pl.loop(0, (amount + 1) // 2)
    def _(i):
        here, there, later = tile(2 * i), tile(2 * i + 1), tile(2 * i + 2)
        fetch(1, there[0])
        work(0, *here)
        fetch(0, later[0])
        work(1, *there)


def forward_kernel(where, rows, classes, ids, flags, first_q, last_q, spans, *rest):
    count = len(where)
    pieces = rest[:count]
    o_parts, o_first, o_second, lse, q, o_low, kv, vt, qm, top, total, accum, first, second, sem = rest[
        count:
    ]
    length = kv.shape[0]
    tiles = length // KTILE
    copies = piece_copies(where, ids, pieces, kv, sem, rows, classes)
    for copy in copies:
        copy.start()
    order_queries(ids, first_q, last_q, q, rows)
    for copy in copies:
        copy.wait()

    @pl.loop(0, tiles)
    def _(t):
        start = pl.multiple_of(t * KTILE, KTILE)
        vt[0:128, pl.ds(start, KTILE)] = kv[pl.ds(start, KTILE), 128:256].T
        vt[128:256, pl.ds(start, KTILE)] = kv[pl.ds(start, KTILE), 256:384].T

    v_row = (128, 192, 0)

    @pl.loop(0, q.shape[0] // QTILE)
    def _(j):
        base = pl.multiple_of(j * QTILE, QTILE)
        for head in range(OWN):
            block = q[pl.ds(base, QTILE), pl.ds(128 * K_BLOCK[head], 128)]
            qm[head] = lane_half(block, K_UPPER[head])
        top[...] = jnp.full_like(top, masked_value)
        total[...] = jnp.zeros_like(total)
        accum[...] = jnp.zeros_like(accum)

        stages = (first, second)

        def fetch(stage, start):
            for head in range(OWN):
                block = 128 * K_BLOCK[head]
                stages[stage][head] = lax.dot_general(
                    kv[pl.ds(start, KTILE), block : block + 128],
                    qm[head],
                    NT,
                    preferred_element_type=jnp.float32,
                )

        def work(stage, start, position):
            same = allowed(spans, base, position)
            for head in range(OWN):
                scores = jnp.where(same, stages[stage][head], masked_value)
                old = top[head : head + 1, :]
                new = jnp.maximum(old, jnp.max(scores, axis=0, keepdims=True))
                weights = jnp.exp(scores - new)
                factor = jnp.exp(old - new)
                top[head : head + 1, :] = new
                total[head : head + 1, :] = total[head : head + 1, :] * factor + jnp.sum(
                    weights, axis=0, keepdims=True
                )
                rows_v = slice(v_row[head], v_row[head] + 64)
                place = slice(64 * head, 64 * head + 64)
                accum[place, :] = accum[place, :] * factor + jnp.dot(
                    vt[rows_v, pl.ds(start, KTILE)],
                    weights.astype(jnp.bfloat16),
                    preferred_element_type=jnp.float32,
                )

        walk(flags, tiles, j, fetch, work)
        outs = [
            accum[64 * head : 64 * head + 64, :] / total[head : head + 1, :] for head in range(OWN)
        ]
        lower = jnp.concatenate(outs[:2], axis=0).T
        upper = jnp.concatenate([outs[2], jnp.zeros_like(outs[2])], axis=0).T
        o_first[pl.ds(base, QTILE), :] = lower
        o_second[pl.ds(base, QTILE), :] = upper
        o_low[pl.ds(base, QTILE), 0:128] = lower.astype(jnp.bfloat16)
        o_low[pl.ds(base, QTILE), 128:192] = upper[:, 0:64].astype(jnp.bfloat16)
        lse[:, pl.ds(base, QTILE)] = top[...] + jnp.log(total[...])

    for chunk in range(GROUPS):
        o_parts[chunk] = o_low[rows * chunk : rows * chunk + rows, :]


def backward_kernel(where, rows, classes, out_where, extra, ids, flags, first_q, last_q, spans, o_first, o_second, lse, *rest):
    count = len(where)
    grads, pieces = rest[0], rest[1 : 1 + count]
    rest = rest[1 + count + extra :]
    outs = rest[: len(out_where)]
    dq, q, grad, kv, kt, qm, dom, stats, dqt, dkv, low_kv, sem = rest[len(out_where) :]
    length = kv.shape[0]
    tiles = length // KTILE
    copies = piece_copies(where, ids, pieces, kv, sem, rows, classes)
    for copy in copies:
        copy.start()

    @pl.loop(0, tiles)
    def _(t):
        start = pl.multiple_of(t * KTILE, KTILE)
        dkv[pl.ds(start, KTILE), :] = jnp.zeros((KTILE, 384), jnp.float32)

    order_queries(ids, first_q, last_q, q, rows)
    for chunk in range(GROUPS):
        grad[rows * chunk : rows * chunk + rows, :] = jnp.concatenate(
            [grads[chunk], jnp.zeros((rows, 64), jnp.bfloat16)], axis=1
        )

    for copy in copies:
        copy.wait()

    @pl.loop(0, tiles)
    def _(t):
        start = pl.multiple_of(t * KTILE, KTILE)
        kt[0:128, pl.ds(start, KTILE)] = kv[pl.ds(start, KTILE), 0:128].T
        kt[128:256, pl.ds(start, KTILE)] = kv[pl.ds(start, KTILE), 128:256].T

    k_row = (0, 64, 192)

    @pl.loop(0, q.shape[0] // QTILE)
    def _(j):
        base = pl.multiple_of(j * QTILE, QTILE)
        for head in range(OWN):
            block = q[pl.ds(base, QTILE), pl.ds(128 * K_BLOCK[head], 128)]
            qm[head] = lane_half(block, K_UPPER[head])
            block = grad[pl.ds(base, QTILE), pl.ds(128 * (2 - V_BLOCK[head]), 128)]
            dom[head] = lane_half(block, V_UPPER[head])
        for part in range(2):
            product = (
                grad[pl.ds(base, QTILE), 128 * part : 128 * part + 128].astype(jnp.float32)
                * (o_first, o_second)[part][pl.ds(base, QTILE), :]
            ).T
            for half in range(2):
                head = 2 * part + half
                if head < OWN:
                    stats[head : head + 1, :] = jnp.sum(
                        product[64 * half : 64 * half + 64], axis=0, keepdims=True
                    )
        dqt[...] = jnp.zeros_like(dqt)

        def product(place, block, right):
            left = kv[place, 128 * block : 128 * block + 128]
            return lax.dot_general(left, right, NT, preferred_element_type=jnp.float32)

        @pl.loop(0, flags[j * (tiles + 1)])
        def _(i):
            start = pl.multiple_of(flags[j * (tiles + 1) + 1 + i] * KTILE, KTILE)
            place = pl.ds(start, KTILE)
            same = allowed(spans, base, start)
            sums = [None, None, None]

            def add(block, left, right):
                term = jnp.dot(left, right, preferred_element_type=jnp.float32)
                sums[block] = term if sums[block] is None else sums[block] + term

            for head in range(OWN):
                scores = product(place, K_BLOCK[head], qm[head])
                grad_probs = product(place, V_BLOCK[head], dom[head])
                probs = jnp.where(
                    same, jnp.exp(scores - lse[head : head + 1, pl.ds(base, QTILE)]), 0.0
                )
                grad_scores = (probs * (grad_probs - stats[head : head + 1, :])).astype(jnp.bfloat16)
                add(V_BLOCK[head], probs.astype(jnp.bfloat16), dom[head])
                add(K_BLOCK[head], grad_scores, qm[head])
                rows_k = slice(k_row[head], k_row[head] + 64)
                dqt[64 * head : 64 * head + 64, :] += jnp.dot(
                    kt[rows_k, place], grad_scores, preferred_element_type=jnp.float32
                )
            for block in range(3):
                dkv[place, 128 * block : 128 * block + 128] += sums[block]

        lower = dqt[0:128, :].T * 0.125
        upper = dqt[64:192, :].T * 0.125
        dq[pl.ds(base, QTILE), 0:128] = lower.astype(jnp.bfloat16)
        dq[pl.ds(base, QTILE), 128:192] = upper[:, 64:128].astype(jnp.bfloat16)

    @pl.loop(0, tiles)
    def _(t):
        start = pl.multiple_of(t * KTILE, KTILE)
        low_kv[pl.ds(start, KTILE), :] = dkv[pl.ds(start, KTILE), :].astype(jnp.bfloat16)

    copies = []
    for out, masks in zip(outs, out_where):
        for slot, mask in enumerate(masks):
            for flip in range(GROUPS):
                chunk = (ids[0] ^ flip) * classes + (ids[1] ^ mask)
                start = pl.multiple_of(chunk * rows, 64)
                copies.append(
                    pltpu.make_async_copy(
                        low_kv.at[pl.ds(start, rows), :], out.at[slot, flip], sem.at[len(copies)]
                    )
                )
    for copy in copies:
        copy.start()
    for copy in copies:
        copy.wait()


VMEM_SPEC = pl.BlockSpec(memory_space=pltpu.VMEM)
SMEM_SPEC = pl.BlockSpec(memory_space=pltpu.SMEM)
ANY_SPEC = pl.BlockSpec(memory_space=pl.ANY)
PARAMS = pltpu.CompilerParams(vmem_limit_bytes=56 * 1024 * 1024)


def attend_forward(ids, flags, first_q, last_q, spans, pieces, where, rows, classes):
    length = rows * classes * GROUPS
    queries = GROUPS * rows
    copies = sum(len(flips) for _, flips in where)
    return pl.pallas_call(
        functools.partial(forward_kernel, where, rows, classes),
        out_shape=(
            jax.ShapeDtypeStruct((GROUPS, rows, WIDTH), jnp.bfloat16),
            jax.ShapeDtypeStruct((queries, 128), jnp.float32),
            jax.ShapeDtypeStruct((queries, 128), jnp.float32),
            jax.ShapeDtypeStruct((8, queries), jnp.float32),
        ),
        in_specs=[SMEM_SPEC, SMEM_SPEC, VMEM_SPEC, VMEM_SPEC, VMEM_SPEC]
        + [ANY_SPEC] * len(pieces),
        out_specs=(VMEM_SPEC,) * 4,
        scratch_shapes=[
            pltpu.VMEM((queries, 256), jnp.bfloat16),
            pltpu.VMEM((queries, WIDTH), jnp.bfloat16),
            pltpu.VMEM((length, 384), jnp.bfloat16),
            pltpu.VMEM((256, length), jnp.bfloat16),
            pltpu.VMEM((OWN, QTILE, 128), jnp.bfloat16),
            pltpu.VMEM((8, QTILE), jnp.float32),
            pltpu.VMEM((8, QTILE), jnp.float32),
            pltpu.VMEM((WIDTH, QTILE), jnp.float32),
            pltpu.VMEM((OWN, KTILE, QTILE), jnp.float32),
            pltpu.VMEM((OWN, KTILE, QTILE), jnp.float32),
            pltpu.SemaphoreType.DMA((copies,)),
        ],
        compiler_params=PARAMS,
        cost_estimate=pl.CostEstimate(
            flops=queries * length * WIDTH * 4, bytes_accessed=8 << 20, transcendentals=0
        ),
        name="attend_forward",
    )(ids, flags, first_q, last_q, spans, *pieces)


def attend_backward(
    ids, flags, first_q, last_q, spans, grads, outputs, lse, pieces, after, where, rows, classes, out_where
):
    length = rows * classes * GROUPS
    queries = GROUPS * rows
    copies = sum(len(flips) for _, flips in where)
    return pl.pallas_call(
        functools.partial(backward_kernel, where, rows, classes, out_where, len(after)),
        out_shape=tuple(
            jax.ShapeDtypeStruct((len(masks), GROUPS, rows, 384), jnp.bfloat16)
            for masks in out_where
        )
        + (jax.ShapeDtypeStruct((queries, WIDTH), jnp.bfloat16),),
        in_specs=[SMEM_SPEC, SMEM_SPEC] + [VMEM_SPEC] * 7 + [ANY_SPEC] * (len(pieces) + len(after)),
        out_specs=(ANY_SPEC,) * len(out_where) + (VMEM_SPEC,),
        scratch_shapes=[
            pltpu.VMEM((queries, 256), jnp.bfloat16),
            pltpu.VMEM((queries, 256), jnp.bfloat16),
            pltpu.VMEM((length, 384), jnp.bfloat16),
            pltpu.VMEM((256, length), jnp.bfloat16),
            pltpu.VMEM((OWN, QTILE, 128), jnp.bfloat16),
            pltpu.VMEM((OWN, QTILE, 128), jnp.bfloat16),
            pltpu.VMEM((8, QTILE), jnp.float32),
            pltpu.VMEM((WIDTH, QTILE), jnp.float32),
            pltpu.VMEM((length, 384), jnp.float32),
            pltpu.VMEM((length, 384), jnp.bfloat16),
            pltpu.SemaphoreType.DMA((copies,)),
        ],
        compiler_params=PARAMS,
        cost_estimate=pl.CostEstimate(
            flops=queries * length * WIDTH * 10, bytes_accessed=16 << 20, transcendentals=0
        ),
        name="attend_backward",
    )(ids, flags, first_q, last_q, spans, *outputs, lse, grads, *pieces, *after)


def pick_kernel(ids, w_q, w_k, w_v, out):
    odd = (ids[3] & 1) == 1
    start = pl.multiple_of((ids[3] // 2) * 384 + (ids[3] & 1) * 128, 128)

    def take(weight):
        both = weight[:, pl.ds(start, 256)]
        return jnp.where(odd, both[:, 64:256], both[:, 0:192])

    q, k, v = take(w_q), take(w_k), take(w_v)
    out[...] = jnp.concatenate(
        [k[:, :128], v[:, 128:], k[:, 128:], v[:, :128], q[:, :128], jnp.zeros_like(q[:, :64]), q[:, 128:]],
        axis=1,
    )


def pick_weights(ids, w_q, w_k, w_v):
    return pl.pallas_call(
        pick_kernel,
        out_shape=jax.ShapeDtypeStruct((w_q.shape[0], 640), jnp.bfloat16),
        in_specs=[SMEM_SPEC] + [VMEM_SPEC] * 3,
        out_specs=VMEM_SPEC,
        compiler_params=PARAMS,
        name="pick_weights",
    )(ids, w_q, w_k, w_v)


def project_kernel(count, parts, ids, bias, *rest):
    tokens, weights, (kv, q) = rest[:count], rest[count : count + parts], rest[count + parts :]
    rows = weights[0].shape[0]
    for i, chunk in enumerate(tokens):
        total = bias[...]
        for part, weight in enumerate(weights):
            lanes = (0 if parts == 1 else ids[0] ^ part) * rows
            left = chunk[:, pl.ds(pl.multiple_of(lanes, 128), rows)]
            total = total + jnp.dot(left, weight[...], preferred_element_type=jnp.float32)
        kv[i] = total[:, :384].astype(jnp.bfloat16)
        q[chunk.shape[0] * i : chunk.shape[0] * (i + 1), :] = (
            total[:, 384:].astype(jnp.bfloat16) * jnp.bfloat16(0.125)
        )


def project(ids, bias, chunks, weights):
    count, rows = len(chunks), chunks[0].shape[0]
    return pl.pallas_call(
        functools.partial(project_kernel, count, len(weights)),
        out_shape=(
            jax.ShapeDtypeStruct((count, rows, 384), jnp.bfloat16),
            jax.ShapeDtypeStruct((count * rows, 256), jnp.bfloat16),
        ),
        in_specs=[SMEM_SPEC] + [VMEM_SPEC] * (1 + count + len(weights)),
        out_specs=(VMEM_SPEC, VMEM_SPEC),
        compiler_params=PARAMS,
        cost_estimate=pl.CostEstimate(
            flops=2 * count * rows * D * 640, bytes_accessed=2 << 20, transcendentals=0
        ),
        name="project",
    )(ids, bias, *chunks, *weights)


def tn(left, right):
    return lax.dot_general(
        left, right, (((0,), (0,)), ((), ())), preferred_element_type=jnp.float32
    )


def down_grad_kernel(active, g_low, after, down):
    part = tn(active[...], g_low[...]).astype(jnp.bfloat16)
    for unit in range(4):
        for half in range(2):
            row = (unit % 2) * 192 + 96 * half
            down[unit // 2, 0, row : row + 96, :] = part[
                96 * unit : 96 * unit + 96, 384 * half : 384 * half + 384
            ]


def down_grad(active, g_low, after):
    rows = active.shape[0]
    return pl.pallas_call(
        down_grad_kernel,
        out_shape=jax.ShapeDtypeStruct((4, 4, 384, 384), jnp.bfloat16),
        grid=(8,),
        in_specs=[
            pl.BlockSpec((rows, 384), lambda i: (0, i)),
            pl.BlockSpec((rows, D), lambda i: (0, 0)),
            ANY_SPEC,
        ],
        out_specs=pl.BlockSpec((2, 1, 384, 384), lambda i: (i % 2, (i // 2) % 2 * 2 + i // 4, 0, 0)),
        compiler_params=PARAMS,
        cost_estimate=pl.CostEstimate(
            flops=2 * rows * D * FF, bytes_accessed=8 << 20, transcendentals=0
        ),
        name="down_grad",
    )(active, g_low, after).reshape(2 * FF, D // 2)


def turn(index):
    return (index & 1) * 2 + index // 2


def upper_grad_kernel(ids, hid, g_raised, attn, g_att, vec, after, near, far):
    core, group = ids[1], ids[3]
    outer = tn(attn[...], g_att[...]).astype(jnp.bfloat16)
    left = hid[...].T
    for k in range(GROUPS):
        lanes = slice(384 * k, 384 * k + 384)
        part = jnp.dot(left, g_raised[:, lanes], preferred_element_type=jnp.float32)
        part = part.astype(jnp.bfloat16)
        place = turn(k ^ group)
        for target, own in ((near, core == 0), (far, core != 0)):
            target[place, 0:192, :] = jnp.where(own, part[:192], part[192:])
            first, second = (outer[192 * b + 48 * k : 192 * b + 48 * k + 48] for b in range(2))
            target[place, 192:240, :] = jnp.where(own, first, second)
            target[place, 240:256, :] = vec[k]


def upper_grad(ids, hid, g_raised, attn, g_att, vec, after):
    rows = hid.shape[0]

    def place(i, j, ids):
        return ((j ^ ids[2]) * 2 + (i ^ ids[0]), 0, 0)

    return pl.pallas_call(
        upper_grad_kernel,
        out_shape=(jax.ShapeDtypeStruct((16, 256, 384), jnp.bfloat16),) * 2,
        grid_spec=pltpu.PrefetchScalarGridSpec(
            num_scalar_prefetch=1,
            grid=(2, 2),
            in_specs=[
                pl.BlockSpec((rows, 384), lambda i, j, ids: (0, i)),
                pl.BlockSpec((rows, 1536), lambda i, j, ids: (0, j)),
                pl.BlockSpec((rows, 384), lambda i, j, ids: (0, i)),
                pl.BlockSpec((rows, 384), lambda i, j, ids: (0, j)),
                pl.BlockSpec((4, 16, 384), lambda i, j, ids: (j, 0, 0)),
                ANY_SPEC,
            ],
            out_specs=(pl.BlockSpec((4, 256, 384), place),) * 2,
        ),
        compiler_params=PARAMS,
        cost_estimate=pl.CostEstimate(
            flops=2 * rows * D * (FF + D), bytes_accessed=12 << 20, transcendentals=0
        ),
        name="upper_grad",
    )(ids, hid, g_raised, attn, g_att, vec, after)


def own_source(d, j, ids):
    return (jnp.where(d == 0, j, 1) ^ ids[2], 0, 0)


def other_source(d, j, ids):
    return (jnp.where(d == 0, 0, j) ^ ids[2], 0, 0)


def unpack_upper_kernel(ids, block_own, block_other, up, out, *vecs):
    side, core, mid, group = ids[0], ids[1], ids[2], ids[3]
    b, j = pl.program_id(0) ^ core, pl.program_id(1)
    own = pl.program_id(0) == 0
    for k in range(GROUPS):
        place = turn(k ^ group)
        part = jnp.where(own, block_own[place], block_other[place]).astype(jnp.float32)
        up[:, 384 * k : 384 * k + 384] = part[0:192]
        out[48 * k : 48 * k + 48, :] = part[192:240]

    @pl.when(b == 0)
    def _():
        for u in range(8):
            place = turn((u % 4) ^ group)
            rows = jnp.where(own, block_own[place, 240:256, :], block_other[place, 240:256, :])
            rows = rows.astype(jnp.float32)
            for r in range(3):
                row = 3 * u + r
                if row < 12:
                    target, where, half = vecs[row // 2], 0, row % 2
                elif row < 20:
                    target, where, half = vecs[6], (row - 12) % 4, (row - 12) // 4
                else:
                    continue

                @pl.when((j == u // 4) & (side == half))
                def _():
                    target[384 * where : 384 * where + 384] = rows[r]


def unpack_upper(ids, own, other):
    sizes = [384] * 6 + [1536]
    return pl.pallas_call(
        unpack_upper_kernel,
        out_shape=(
            jax.ShapeDtypeStruct((384, FF), jnp.float32),
            jax.ShapeDtypeStruct((384, D), jnp.float32),
        )
        + tuple(jax.ShapeDtypeStruct((size,), jnp.float32) for size in sizes),
        grid_spec=pltpu.PrefetchScalarGridSpec(
            num_scalar_prefetch=1,
            grid=(2, 2),
            in_specs=[
                pl.BlockSpec((4, 256, 384), own_source),
                pl.BlockSpec((4, 256, 384), other_source),
            ],
            out_specs=(
                pl.BlockSpec((192, 1536), lambda d, j, ids: (d ^ ids[1], j)),
                pl.BlockSpec((192, 384), lambda d, j, ids: (d ^ ids[1], j)),
            )
            + tuple(pl.BlockSpec((size,), lambda d, j, ids: (0,)) for size in sizes),
        ),
        compiler_params=PARAMS,
        name="unpack_upper",
    )(ids, own, other)


def unpack_down_kernel(ids, block_own, block_other, down):
    own, j = pl.program_id(0) == 0, pl.program_id(1)
    for k in range(GROUPS):
        place = turn(k ^ ids[3])
        part = jnp.where(own, block_own[place], block_other[place]).astype(jnp.float32)
        rows = pl.ds(pl.multiple_of(96 * j, 32) + 192 * k, 96)
        down[rows, 0:384] = part[0:96]
        down[rows, 384:768] = part[96:192]


def unpack_down(ids, own, other):
    return pl.pallas_call(
        unpack_down_kernel,
        out_shape=jax.ShapeDtypeStruct((FF // 2, D), jnp.float32),
        grid_spec=pltpu.PrefetchScalarGridSpec(
            num_scalar_prefetch=1,
            grid=(2, 2),
            in_specs=[
                pl.BlockSpec((4, 192, 384), own_source),
                pl.BlockSpec((4, 192, 384), other_source),
            ],
            out_specs=pl.BlockSpec((FF // 4, D), lambda d, j, ids: (d ^ ids[1], 0)),
        ),
        compiler_params=PARAMS,
        name="unpack_down",
    )(ids, own, other)


def qkv_grad_kernel(ids, t0, t1, t2, t3, *rest):
    kept, given, sent, dq, near, far, both, whole = rest
    x, c = ids[0], ids[1]
    rows = dq.shape[0] // GROUPS
    total = jnp.zeros((1, 576), jnp.float32)
    for flip in range(GROUPS):
        term = (
            kept[0, flip].astype(jnp.float32)
            + given[0, flip].astype(jnp.float32)
            + sent[flip].astype(jnp.float32)
        ).astype(jnp.bfloat16)
        own = slice(rows * flip, rows * flip + rows)
        start = pl.multiple_of((flip ^ ids[3]) * rows, 64)
        block = jnp.concatenate([term, dq[pl.ds(start, rows), :]], axis=1)
        both[flip ^ ids[3]] = block
        whole[own, :] = block
        total = total + jnp.sum(block.astype(jnp.float32), axis=0, keepdims=True)
    first = lax.broadcasted_iota(jnp.int32, (16, 576), 0) == 0
    total = jnp.where(first, jnp.broadcast_to(total, (16, 576)), 0.0).astype(jnp.bfloat16)

    @pl.loop(0, 2)
    def _(i):
        lanes = pl.ds(pl.multiple_of(i * 384, 128), 384)
        left = jnp.concatenate([t[:, lanes] for t in (t0, t1, t2, t3)], axis=0)
        part = tn(left, whole[...]).astype(jnp.bfloat16)
        for b in range(2):

            def store(target):
                target[i ^ x, 0:192, :] = part[192 * b : 192 * b + 192]

            pl.when(c == b)(functools.partial(store, near))
            pl.when(c != b)(functools.partial(store, far))
        near[i ^ x, 192:208, :] = total
        far[i ^ x, 192:208, :] = total


def qkv_grads(ids, tokens, kept, given, sent, dq):
    queries = dq.shape[0]
    rows = queries // GROUPS
    return pl.pallas_call(
        qkv_grad_kernel,
        out_shape=(jax.ShapeDtypeStruct((2, 208, 576), jnp.bfloat16),) * 2
        + (jax.ShapeDtypeStruct((GROUPS, rows, 576), jnp.bfloat16),),
        in_specs=[SMEM_SPEC] + [VMEM_SPEC] * 8,
        out_specs=(VMEM_SPEC,) * 3,
        scratch_shapes=[pltpu.VMEM((queries, 576), jnp.bfloat16)],
        compiler_params=PARAMS,
        cost_estimate=pl.CostEstimate(
            flops=2 * queries * D * 576, bytes_accessed=4 << 20, transcendentals=0
        ),
        name="qkv_grads",
    )(ids, *tokens, kept, given, sent, dq)


def unpack_qkv_kernel(ids, own, other, out_q, out_k, out_v, vec):
    c, h = ids[1], ids[3]
    for b in range(2):
        q, k, v = [], [], []
        for g in range(GROUPS):
            block = jnp.where(c == b, own[turn(g ^ h), 0:192, :], other[turn(g ^ h), 0:192, :]).astype(jnp.float32)
            k += [block[:, 0:128], block[:, 192:256]]
            v += [block[:, 256:384], block[:, 128:192]]
            q += [block[:, 384:576]]
        for out, parts in ((out_q, q), (out_k, k), (out_v, v)):
            out[192 * b : 192 * b + 192, :] = jnp.concatenate(parts, axis=1)
    for g in range(GROUPS):
        vec[g] = jnp.where(c == 0, own[turn(g ^ h), 192:208, :], other[turn(g ^ h), 192:208, :]).astype(jnp.float32)


def unpack_qkv(ids, own, other):
    return pl.pallas_call(
        unpack_qkv_kernel,
        out_shape=(jax.ShapeDtypeStruct((384, D), jnp.float32),) * 3
        + (jax.ShapeDtypeStruct((GROUPS, 16, 576), jnp.float32),),
        in_specs=[SMEM_SPEC, VMEM_SPEC, VMEM_SPEC],
        out_specs=(VMEM_SPEC,) * 4,
        compiler_params=PARAMS,
        name="unpack_qkv",
    )(ids, own, other)


def token_grad_kernel(base, both, weight, out):
    total = base[...]
    for g in range(GROUPS):
        w = weight[:, 640 * g : 640 * g + 576]
        total = total + lax.dot_general(both[g], w, NT, preferred_element_type=jnp.float32)
    out[...] = total


def token_grads(base, both, weight):
    return pl.pallas_call(
        token_grad_kernel,
        out_shape=jax.ShapeDtypeStruct(base.shape, jnp.float32),
        in_specs=[VMEM_SPEC] * 3,
        out_specs=VMEM_SPEC,
        compiler_params=PARAMS,
        cost_estimate=pl.CostEstimate(
            flops=2 * base.shape[0] * D * 2304, bytes_accessed=8 << 20, transcendentals=0
        ),
        name="token_grads",
    )(base, both, weight)


def own_part(weight, core):
    half = weight.shape[0] // 2
    return lax.dynamic_slice_in_dim(weight, core * half, half, 0)


def reduce_blocks(grad):
    flat = grad.reshape((-1,) + grad.shape[2:])
    mine = lax.psum_scatter(flat, ("wa", "c"), scatter_dimension=0, tiled=True)
    mine = lax.psum_scatter(mine, "m", scatter_dimension=0, tiled=True)
    mine = lax.psum_scatter(mine, "h", scatter_dimension=0, tiled=True)
    return lax.all_gather(mine, ("c", "m", "h"), axis=0, tiled=True)


def tie(array, *others):
    return lax.optimization_barrier((array,) + others)[0]


def both_sum(near, far, *others):
    near = tie(near, *others)
    return low(widen(near) + widen(far))


def fold(near, far, *others):
    near = tie(near, *others)
    return [low(widen(near[i]) + widen(far[i])) for i in range(2)]


def double(array, axis, bit):
    return jnp.concatenate([array, swap(array, axis, bit)], axis=0)


def pick_columns(weight, group):
    q, k, v = (lax.dynamic_slice_in_dim(w, group * WIDTH, WIDTH, w.ndim - 1) for w in weight)
    return jnp.concatenate(
        [
            k[..., :128],
            v[..., 128:],
            k[..., 128:],
            v[..., :128],
            q[..., :128],
            jnp.zeros_like(q[..., :64]),
            q[..., 128:],
        ],
        axis=-1,
    )


def per_device(
    tokens,
    segment_ids,
    cotangent,
    w_query,
    w_key,
    w_value,
    w_out,
    w_up,
    w_down,
    b_query,
    b_value,
    b_out,
    gain_one,
    shift_one,
    b_up,
    b_down,
    gain_two,
    shift_two,
):
    mid = lax.axis_size("m")
    wide = lax.axis_size("wa")
    paired = mid == 2 and wide == 2
    classes = 2 * mid
    group = lax.axis_index("h")
    core = lax.axis_index("c")
    kind = lax.axis_index("m") * 2 + core
    side = lax.axis_index("wa")
    inputs = tokens[0]
    count = inputs.shape[0]
    chunks = GROUPS * classes
    length = count * chunks
    tiles = length // KTILE
    ids = jnp.stack([group, kind]).astype(jnp.int32)
    place_ids = jnp.stack([side, core, lax.axis_index("m"), group]).astype(jnp.int32)
    order = group ^ jnp.arange(GROUPS)

    second = swap(inputs, "h", 1)
    third = swap(inputs, "h", 2)
    if wide == 2:
        w_own = pick_weights(place_ids, w_query, w_key, w_value)
        w_other = swap(w_own, "wa", 1)
    else:
        w_own = None
        w_other = lax.all_gather(
            pick_columns((w_query, w_key, w_value), group), "wa", axis=0, tiled=True
        )

    smalls = [b_query, b_value, b_out, gain_one, shift_one, b_up, b_down, gain_two, shift_two]
    w_parts = [own_part(item, core) for item in (w_out, w_up, w_down)]
    joined = lax.all_gather(tie(jnp.concatenate(smalls), *w_parts), "wa", axis=0)
    second, third, w_other, joined = lax.optimization_barrier((second, third, w_other, joined))
    fourth = swap(third, "h", 1)
    full, place = [], 0
    for item in smalls:
        size = item.shape[0]
        full.append(widen(joined[:, place : place + size].reshape(-1)))
        place += size
    bias_query, bias_value, bias_out, gain_attn, shift_attn, bias_up, bias_down, gain_ffn, shift_ffn = full
    b_group = pick_columns((bias_query, jnp.zeros_like(bias_query), bias_value), group)[None]

    w_group = (w_own, w_other) if wide == 2 else (w_other,)
    full_out, full_up, full_down = (
        lax.all_gather(tie(part, w_other), ("wa", "c"), axis=0, tiled=True) for part in w_parts
    )
    where, pieces = [], []

    def spread(piece, flips):
        have = {0: piece}
        bit = 1
        while bit < mid:
            for mask in list(have):
                have[mask | (bit << 1)] = swap(have[mask], "m", bit)
            bit *= 2
        for mask in list(have):
            have[mask | 1] = swap(have[mask], "c", 1)
        for mask, item in have.items():
            where.append((mask, flips))
            pieces.append(item)

    first_kv, first_q = project(place_ids, b_group, (inputs, second, third), w_group)
    spread(first_kv, (0, 1, 2))

    segs = double(tie(segment_ids, first_kv), "c", 1)
    bit = 1
    while bit < mid:
        segs = double(segs, "m", bit)
        bit *= 2
    segs = double(double(segs, "h", 1), "h", 2)
    segs = jnp.take(segs, (group * classes + kind) ^ jnp.arange(chunks), axis=0)

    own_segs = lax.dynamic_index_in_dim(
        segs.reshape(GROUPS, classes, count), kind, 1, keepdims=False
    ).reshape(-1)

    names = jnp.arange(DOCS)
    begins = jnp.sum((segs.reshape(-1, 1) < names).astype(jnp.int32), axis=0)
    ends = jnp.sum((segs.reshape(-1, 1) <= names).astype(jnp.int32), axis=0)
    chosen = own_segs[None, :] == names[:, None]
    begins = jnp.sum(jnp.where(chosen, begins[:, None], 0), axis=0)
    ends = jnp.sum(jnp.where(chosen, ends[:, None], 0), axis=0)
    spans = jnp.concatenate(
        [begins[None], ends[None], jnp.zeros((6, begins.shape[0]), jnp.int32)], axis=0
    )
    edges = (jnp.arange(tiles) * KTILE)[None, :, None]
    meets = (begins.reshape(-1, 1, QTILE) < edges + KTILE) & (ends.reshape(-1, 1, QTILE) > edges)
    meets = jnp.any(meets, axis=-1).astype(jnp.int32)
    rank = jnp.cumsum(meets, axis=1)
    slots = (rank[:, None, :] == jnp.arange(1, tiles + 1)[None, :, None]) & (meets[:, None, :] > 0)
    listed = jnp.sum(jnp.where(slots, jnp.arange(tiles), 0), axis=-1)
    flags = jnp.concatenate([rank[:, -1:], listed], axis=1).astype(jnp.int32).reshape(-1)

    last_kv, last_q = project(place_ids, b_group, (fourth,), w_group)
    spread(last_kv, (3,))
    where = tuple(where)
    group_tokens = [inputs, second, third, fourth]

    o_parts, o_first, o_second, lse = attend_forward(
        ids, flags, first_q, last_q, spans, pieces, where, count, classes
    )

    w_query, w_key, w_value = (tie(item, lse) for item in (w_query, w_key, w_value))
    columns = []
    for g in range(GROUPS):
        low_part, high_part = slice(192 * g, 192 * g + 128), slice(192 * g + 128, 192 * g + 192)
        columns += [w_key[:, low_part], w_value[:, high_part], w_key[:, high_part], w_value[:, low_part]]
        columns += [w_query[:, 192 * g : 192 * g + 192], jnp.zeros_like(w_query[:, :64])]
    by_group = own_part(jnp.concatenate(columns, axis=1), core)
    by_group = lax.all_gather(by_group, ("wa", "c"), axis=0, tiled=True)

    def send_back(parts):
        return lax.all_to_all(parts, "h", 0, 0, tiled=True)

    attn_low = jnp.transpose(send_back(o_parts), (1, 0, 2)).reshape(count, D)
    attended = mm(attn_low, full_out) + bias_out
    hidden, unit_one, scale_one = norm_forward(widen(inputs) + attended, gain_attn, shift_attn)
    hidden_low = low(hidden)
    raised = mm(hidden_low, full_up) + bias_up
    active, slope = gelu_pair(raised)
    active_low = low(active)
    lowered = mm(active_low, full_down) + bias_down
    result, unit_two, scale_two = norm_forward(hidden + lowered, gain_ffn, shift_ffn)
    grad_sum_two, grad_gain_two, grad_shift_two = norm_backward(
        widen(cotangent[0]), unit_two, scale_two, gain_ffn
    )
    grad_lowered = low(grad_sum_two)
    grad_b_down = jnp.sum(widen(grad_lowered), axis=0)
    grad_raised = low(back_product(grad_lowered, full_down) * slope)
    grad_b_up = jnp.sum(widen(grad_raised), axis=0)
    grad_hidden = grad_sum_two + back_product(grad_raised, full_up)
    grad_sum_one, grad_gain_one, grad_shift_one = norm_backward(
        grad_hidden, unit_one, scale_one, gain_attn
    )
    grad_attended = low(grad_sum_one)
    grad_b_out = jnp.sum(widen(grad_attended), axis=0)
    grad_attn = low(back_product(grad_attended, full_out))

    grad_rows = send_back(jnp.transpose(grad_attn.reshape(count, GROUPS, WIDTH), (1, 0, 2)))

    vectors = jnp.concatenate(
        [grad_b_out, grad_gain_one, grad_shift_one, grad_b_down, grad_gain_two, grad_shift_two, grad_b_up]
    )
    blocks = 2 * wide
    if paired:
        vectors = jnp.pad(low(vectors), (0, 9216 - 7680)).reshape(8, 3, 384)
        vectors = jnp.pad(vectors, ((0, 0), (0, 13), (0, 0)))
        near, far = upper_grad(
            place_ids, hidden_low, grad_raised, attn_low, grad_attended, vectors, by_group
        )
        shape = (2, 2, 2, 2, 256, 384)
        near, far = near.reshape(shape), swap(far, "c", 1).reshape(shape)
        grad_rows = tie(grad_rows, near)
        down_sum = down_grad(active_low, grad_lowered, near)
        upper, give = fold(near, far, down_sum)
        after = (give,)
        give = swap(give, "m", 1)
        down_sum = tie(down_sum, grad_rows)
        down_sum = lax.psum_scatter(down_sum, ("h", "c"), scatter_dimension=0, tiled=True)
    else:
        grad_w_down = low(outer_sum(active_low, grad_lowered))
        grad_w_up = low(outer_sum(hidden_low, grad_raised))
        grad_w_out = low(outer_sum(attn_low, grad_attended))
        vectors = jnp.pad(low(vectors).reshape(-1, D), ((0, 6), (0, 0)))
        down_rows, out_rows = FF // blocks, D // blocks
        ffn = jnp.concatenate(
            [
                grad_w_down.reshape(blocks, down_rows, D),
                grad_w_up.reshape(blocks, down_rows, D),
                grad_w_out.reshape(blocks, out_rows, D),
                jnp.broadcast_to(vectors[None], (blocks, 16, D)),
            ],
            axis=1,
        )
        after = ()
        ffn_sum = reduce_blocks(ffn).reshape(2, -1, D)
        out_down = widen(ffn_sum[:, :down_rows]).reshape(-1, D)
        out_up = widen(ffn_sum[:, down_rows : 2 * down_rows]).reshape(-1, FF)
        place = 2 * down_rows
        out_out = widen(ffn_sum[:, place : place + out_rows]).reshape(-1, D)
        small = widen(ffn_sum[0, place + out_rows :])

        def share(row, rows):
            vector = small[row : row + rows].reshape(-1)
            size = vector.shape[0] // wide
            return lax.dynamic_slice_in_dim(vector, side * size, size, 0)

        vectors = [share(row, 1) for row in range(6)] + [share(6, 4)]

    stay_masks, leave_masks = tuple(range(0, classes, 2)), tuple(range(1, classes, 2))
    out_where = (stay_masks,) + tuple((mask,) for mask in leave_masks)

    kept, *given, dq = attend_backward(
        ids, flags, first_q, last_q, spans, grad_rows, (o_first, o_second), lse,
        pieces, after, where, count, classes, out_where,
    )

    given = [swap(item, "c", 1) for item in given]
    if paired:
        upper, give = fold(upper, give, dq)
        kept = tie(kept, give)
        sent = low(widen(kept[1]) + widen(given[1][0]))
        down_sum = lax.psum_scatter(tie(down_sum, sent), "wa", scatter_dimension=0, tiled=True)
        give = swap(give, "wa", 1)
        upper = tie(upper, sent)
        sent = swap(sent, "m", 1)
        upper, give = fold(upper, give)
        kept = tie(kept, give)
        give = swap(give, "h", 1)
    else:
        partial = widen(kept) + widen(jnp.concatenate(given, axis=0))
        stay = list(stay_masks)
        bit = mid // 2
        while bit >= 1:
            mask = bit << 1
            near = [i for i, m in enumerate(stay) if not m & mask]
            far = [i for i, m in enumerate(stay) if m & mask]
            sent = swap(low(partial[far[0] : far[-1] + 1]), "m", bit)
            partial = widen(low(partial[near[0] : near[-1] + 1])) + widen(sent)
            stay = [stay[i] for i in near]
            bit //= 2
        dkv = low(partial[0]).reshape(GROUPS * count, 384)

    part = D // wide
    if paired:
        near, far, parts = qkv_grads(place_ids, group_tokens, kept, given[0], sent, dq)
        far = swap(far, "c", 1)
        down_sum = lax.psum_scatter(tie(down_sum, near), "m", scatter_dimension=0, tiled=True)
        upper, give = fold(upper, give, near)
        near = tie(near, give)
        give = swap(give, "h", 2)
        qkv, other = fold(near, far)
        other = swap(other, "wa", 1)
        down_other = swap(down_sum, "h", 2)
        upper = both_sum(upper, give, qkv)
        upper_other = swap(upper, "h", 2)
        qkv = both_sum(qkv, other, upper)
        other = swap(qkv, "m", 1)
        down_sum = jnp.stack([tie(down_sum, qkv), down_other])
        down_other = swap(down_sum, "h", 1)
        upper = jnp.stack([tie(upper, down_sum), upper_other])
        upper_other = swap(upper, "h", 1)
        qkv = both_sum(qkv, other, upper)
        other = swap(qkv, "h", 2)
        down_sum = jnp.stack([tie(down_sum, qkv), down_other])
        down_other = swap(down_sum, "m", 1)
        upper = jnp.stack([tie(upper, down_sum), upper_other])
        upper_other = swap(upper, "m", 1)
        parts = send_back(tie(parts, upper))
        qkv = jnp.stack([tie(qkv, upper), other])
        other = swap(qkv, "h", 1)
        down_sum = jnp.stack([tie(down_sum, qkv), down_other])
        down_other = swap(down_sum, "c", 1)
        qkv = jnp.concatenate([tie(qkv, down_sum), other], axis=0)
        other = swap(qkv, "c", 1)
        down_sum, down_other = (item.reshape(8, 192, 384) for item in (tie(down_sum, qkv), down_other))
        out_down = unpack_down(place_ids, down_sum, down_other)
        upper = jnp.stack([tie(upper, out_down), upper_other])
        upper_other = swap(upper, "c", 1)
        out_query, out_key, out_value, sums = unpack_qkv(place_ids, tie(qkv, upper), other)
        upper, upper_other = (item.reshape(8, 256, 384) for item in (tie(upper, out_query), upper_other))
        out_up, out_out, *vectors = unpack_upper(place_ids, upper, upper_other)
        grad_inputs = token_grads(tie(grad_sum_one, out_up), parts, by_group)
        sums = sums[:, 0]
        sums_v = jnp.concatenate([sums[:, 256:384], sums[:, 128:192]], axis=1).reshape(-1)
        sums_q = sums[:, 384:576].reshape(-1)
    else:
        dq = jnp.take(dq.reshape(GROUPS, count, WIDTH), order, axis=0).reshape(-1, WIDTH)
        both = jnp.concatenate([dkv, dq], axis=1)
        width = both.shape[1]
        parts = send_back(jnp.take(both.reshape(GROUPS, count, width), order, axis=0))
        w_grad = low(outer_sum(jnp.concatenate(group_tokens, axis=0), both)).reshape(blocks, D // blocks, width)
        b_grad = low(jnp.sum(widen(both), axis=0))
        b_grad = jnp.pad(b_grad[None], ((0, 15), (0, 0)))
        qkv = jnp.concatenate([w_grad, jnp.broadcast_to(b_grad[None], (blocks, 16, width))], axis=1)
        rows = qkv.shape[1]
        mine = lax.psum_scatter(
            qkv.reshape(blocks * rows, width), ("wa", "c"), scatter_dimension=0, tiled=True
        )
        mine = lax.psum(mine, "m")
        every = widen(lax.all_gather(mine, ("c", "h"), axis=0).reshape(2, GROUPS, rows, width))

        def columns(block):
            k = jnp.concatenate([block[..., :128], block[..., 192:256]], axis=-1)
            v = jnp.concatenate([block[..., 256:384], block[..., 128:192]], axis=-1)
            q = block[..., 384:576]
            return [jnp.transpose(item, (0, 2, 1, 3)).reshape(2, -1, D) for item in (q, k, v)]

        out_query, out_key, out_value = (
            item.reshape(-1, D) for item in columns(every[:, :, : rows - 16])
        )
        sums_q, _, sums_v = (item[0, 0] for item in columns(every[:, :, rows - 16 : rows - 15]))
        grad_inputs = token_grads(grad_sum_one, parts, by_group)
    out_b_query = lax.dynamic_slice_in_dim(sums_q, side * part, part, 0)
    out_b_value = lax.dynamic_slice_in_dim(sums_v, side * part, part, 0)

    return (
        low(result)[None],
        grad_inputs[None],
        out_query,
        out_key,
        out_value,
        out_out,
        out_up,
        out_down,
        out_b_query,
        out_b_value,
        vectors[0],
        vectors[1],
        vectors[2],
        vectors[6],
        vectors[3],
        vectors[4],
        vectors[5],
    )


def solution(mesh):
    chunks, wide = mesh.devices.shape
    finer = Mesh(
        mesh.devices.reshape(GROUPS, chunks // (2 * GROUPS), 2, wide), ("h", "m", "c", "wa")
    )
    ctx = ("h", "m", "c")
    seq3, seq2 = P("wa", ctx, None), P("wa", ctx)
    matrix, vector = P("wa", None), P("wa")
    return jax.shard_map(
        per_device,
        mesh=finer,
        in_specs=(seq3, seq2, seq3) + (matrix,) * 6 + (vector,) * 9,
        out_specs=(seq3, seq3) + (matrix,) * 6 + (vector,) * 9,
        check_vma=False,
    )
```

```python
import functools

import jax
import jax.numpy as jnp
from jax import lax
from jax.experimental import pallas as pl
from jax.experimental.pallas import tpu as pltpu
from jax.sharding import Mesh
from jax.sharding import PartitionSpec as P

D = 768
HEADS = 12
HEAD_DIM = 64
FF = 3072
DOCS = 32

GROUPS = 4
OWN = HEADS // GROUPS
WIDTH = OWN * HEAD_DIM
QTILE = 256
KTILE = 512
KSTEP = 128

epsilon = 1e-05
masked_value = -1e30
NT = (((1,), (1,)), ((), ()))
NN = (((1,), (0,)), ((), ()))


def widen(array):
    return array.astype(jnp.float32)


def low(array):
    return array.astype(jnp.bfloat16)


def mm(left, right):
    return jnp.dot(left, right, preferred_element_type=jnp.float32)


def outer_sum(left, right):
    return lax.dot_general(
        left, right, (((0,), (0,)), ((), ())), preferred_element_type=jnp.float32
    )


def back_product(grad, weight):
    return lax.dot_general(grad, weight, NT, preferred_element_type=jnp.float32)


def norm_forward(values, gain, shift):
    centre = values - jnp.mean(values, axis=-1, keepdims=True)
    scale = lax.rsqrt(jnp.mean(centre * centre, axis=-1, keepdims=True) + epsilon)
    unit = centre * scale
    return (unit * gain + shift, unit, scale)


def norm_backward(grad, unit, scale, gain):
    grad_gain = jnp.sum(grad * unit, axis=0)
    grad_shift = jnp.sum(grad, axis=0)
    inner = grad * gain
    grad_in = scale * (
        inner
        - jnp.mean(inner, axis=-1, keepdims=True)
        - unit * jnp.mean(inner * unit, axis=-1, keepdims=True)
    )
    return (grad_in, grad_gain, grad_shift)


def gelu_pair(values):
    cumulative = 0.5 * (1.0 + lax.erf(values * 0.7071067811865476))
    density = jnp.exp(-0.5 * values * values) * 0.3989422804014327
    return (values * cumulative, cumulative + values * density)


def swap(array, axis, bit):
    size = lax.axis_size(axis)
    return lax.ppermute(array, axis, [(i, i ^ bit) for i in range(size)])


K_BLOCK = (0, 0, 1)
V_BLOCK = (2, 2, 1)
K_UPPER = (False, True, True)
V_UPPER = (False, True, False)


def lane_half(array, upper):
    lane = lax.broadcasted_iota(jnp.int32, array.shape, 1)
    keep = (lane >= 64) if upper else (lane < 64)
    return jnp.where(keep, array, jnp.zeros_like(array))


def start_pieces(where, ids, pieces, kv, sem, rows, classes):
    for piece, (mask, flips) in zip(pieces, where):
        for slot, flip in enumerate(flips):
            chunk = (ids[0] ^ flip) * classes + (ids[1] ^ mask)
            start = pl.multiple_of(chunk * rows, 64)
            pltpu.make_async_copy(
                piece.at[slot], kv.at[pl.ds(start, rows), :], sem.at[chunk]
            ).start()


def turn_pieces(pieces, kv, turned, blocks, sem, rows):
    @pl.loop(0, kv.shape[0] // (2 * rows))
    def _(t):
        for half in range(2):
            start = pl.multiple_of((2 * t + half) * rows, 64)
            pltpu.make_async_copy(
                pieces[0].at[0], kv.at[pl.ds(start, rows), :], sem.at[2 * t + half]
            ).wait()
        both = pl.ds(pl.multiple_of(t * 2 * rows, 128), 2 * rows)
        for n, block in enumerate(blocks):
            turned[128 * n : 128 * n + 128, both] = kv[both, 128 * block : 128 * block + 128].T


def pack(part):
    half = part.shape[0] // 2
    return jnp.concatenate(
        [part[:, :128], jnp.concatenate([part[:half, 128:], part[half:, 128:]], axis=1)], axis=0
    )


def unpack(packed):
    rows = packed.shape[0] // 3 * 2
    rest = packed[rows:]
    return packed[:rows], jnp.concatenate([rest[:, :64], rest[:, 64:]], axis=0)


def order_queries(ids, first_q, last_q, q, rows):
    for flip in range(GROUPS):
        part, place = (last_q, 0) if flip == 3 else (first_q, rows * flip)
        start = pl.multiple_of((ids[0] ^ flip) * rows, 64)
        q[pl.ds(start, rows), :] = part[place : place + rows, :]


def allowed(spans, base, start, floor):
    position = lax.broadcasted_iota(jnp.int32, (KTILE, QTILE), 0)
    first = jnp.maximum(spans[0:1, pl.ds(base, QTILE)] - start, floor)
    last = spans[1:2, pl.ds(base, QTILE)] - start
    return (position >= first) & (position < last)


class Tiles:
    def __init__(self, steps, length, j):
        self.end = length // KSTEP
        self.span = KTILE // KSTEP
        self.steps, self.row = steps, j * (self.end + self.span + 1)

    def after(self, step):
        return self.steps[self.row + step]

    def following(self, step):
        return self.after(step + self.span)

    def place(self, step):
        return pl.multiple_of(jnp.minimum(step, self.end - self.span) * KSTEP, KSTEP)

    def floor(self, step):
        floor = jnp.maximum(step - (self.end - self.span), 0) * KSTEP
        return jnp.where(step < self.end, floor, KTILE)


def walk(tiles, fetch, work):
    begin = tiles.after(0)
    fetch(0, tiles.place(begin))

    def body(here):
        there = tiles.following(here)
        later = tiles.following(there)
        fetch(1, tiles.place(there))
        work(0, tiles.place(here), tiles.floor(here))
        fetch(0, tiles.place(later))
        work(1, tiles.place(there), tiles.floor(there))
        return later

    lax.while_loop(lambda here: here < tiles.end, body, begin)


def forward_kernel(where, rows, classes, ids, flags, first_q, last_q, spans, *rest):
    count = len(where)
    pieces = rest[:count]
    o_parts, o_first, o_second, lse, q, o_low, kv, vt, qm, top, total, accum, first, second, sem = rest[
        count:
    ]
    length = kv.shape[0]
    tiles = length // KTILE
    start_pieces(where, ids, pieces, kv, sem, rows, classes)
    order_queries(ids, first_q, last_q, q, rows)
    turn_pieces(pieces, kv, vt, (1, 2), sem, rows)

    v_row = (128, 192, 0)

    @pl.loop(0, q.shape[0] // QTILE)
    def _(j):
        base = pl.multiple_of(j * QTILE, QTILE)
        for head in range(OWN):
            block = q[pl.ds(base, QTILE), pl.ds(128 * K_BLOCK[head], 128)]
            qm[head] = lane_half(block, K_UPPER[head])
        top[...] = jnp.full_like(top, masked_value)
        total[...] = jnp.zeros_like(total)
        accum[...] = jnp.zeros_like(accum)

        stages = (first, second)

        def fetch(stage, start):
            for head in range(OWN):
                block = 128 * K_BLOCK[head]
                stages[stage][head] = lax.dot_general(
                    kv[pl.ds(start, KTILE), block : block + 128],
                    qm[head],
                    NT,
                    preferred_element_type=jnp.float32,
                )

        def work(stage, start, floor):
            same = allowed(spans, base, start, floor)
            for head in range(OWN):
                scores = jnp.where(same, stages[stage][head], masked_value)
                old = top[head : head + 1, :]
                new = jnp.maximum(old, jnp.max(scores, axis=0, keepdims=True))
                weights = jnp.exp(scores - new)
                factor = jnp.exp(old - new)
                top[head : head + 1, :] = new
                total[head : head + 1, :] = total[head : head + 1, :] * factor + jnp.sum(
                    weights, axis=0, keepdims=True
                )
                rows_v = slice(v_row[head], v_row[head] + 64)
                place = slice(64 * head, 64 * head + 64)
                accum[place, :] = accum[place, :] * factor + jnp.dot(
                    vt[rows_v, pl.ds(start, KTILE)],
                    weights.astype(jnp.bfloat16),
                    preferred_element_type=jnp.float32,
                )

        walk(Tiles(flags, length, j), fetch, work)
        outs = [
            accum[64 * head : 64 * head + 64, :] / total[head : head + 1, :] for head in range(OWN)
        ]
        lower = jnp.concatenate(outs[:2], axis=0).T
        upper = jnp.concatenate([outs[2], jnp.zeros_like(outs[2])], axis=0).T
        o_first[pl.ds(base, QTILE), :] = lower
        o_second[pl.ds(base, QTILE), :] = upper
        o_low[pl.ds(base, QTILE), 0:128] = lower.astype(jnp.bfloat16)
        o_low[pl.ds(base, QTILE), 128:192] = upper[:, 0:64].astype(jnp.bfloat16)
        lse[:, pl.ds(base, QTILE)] = top[...] + jnp.log(total[...])

    for chunk in range(GROUPS):
        o_parts[chunk] = pack(o_low[rows * chunk : rows * chunk + rows, :])


def backward_kernel(where, rows, classes, out_where, extra, ids, flags, first_q, last_q, spans, o_first, o_second, lse, *rest):
    count = len(where)
    grads, pieces = rest[0], rest[1 : 1 + count]
    rest = rest[1 + count + extra :]
    outs = rest[: len(out_where)]
    dq, q, grad, kv, kt, qm, dom, stats, dqt, dkv, low_kv, sem = rest[len(out_where) :]
    length = kv.shape[0]
    tiles = length // KTILE
    start_pieces(where, ids, pieces, kv, sem, rows, classes)

    @pl.loop(0, tiles)
    def _(t):
        start = pl.multiple_of(t * KTILE, KTILE)
        dkv[pl.ds(start, KTILE), :] = jnp.zeros((KTILE, 384), jnp.float32)

    order_queries(ids, first_q, last_q, q, rows)
    for chunk in range(GROUPS):
        first, last = unpack(grads[chunk])
        grad[rows * chunk : rows * chunk + rows, :] = jnp.concatenate(
            [first, last, jnp.zeros((rows, 64), jnp.bfloat16)], axis=1
        )

    turn_pieces(pieces, kv, kt, (0, 1), sem, rows)

    k_row = (0, 64, 192)

    @pl.loop(0, q.shape[0] // QTILE)
    def _(j):
        base = pl.multiple_of(j * QTILE, QTILE)
        for head in range(OWN):
            block = q[pl.ds(base, QTILE), pl.ds(128 * K_BLOCK[head], 128)]
            qm[head] = lane_half(block, K_UPPER[head])
            block = grad[pl.ds(base, QTILE), pl.ds(128 * (2 - V_BLOCK[head]), 128)]
            dom[head] = lane_half(block, V_UPPER[head])
        for part in range(2):
            product = (
                grad[pl.ds(base, QTILE), 128 * part : 128 * part + 128].astype(jnp.float32)
                * (o_first, o_second)[part][pl.ds(base, QTILE), :]
            ).T
            for half in range(2):
                head = 2 * part + half
                if head < OWN:
                    stats[head : head + 1, :] = jnp.sum(
                        product[64 * half : 64 * half + 64], axis=0, keepdims=True
                    )
        dqt[...] = jnp.zeros_like(dqt)

        def product(place, block, right):
            left = kv[place, 128 * block : 128 * block + 128]
            return lax.dot_general(left, right, NT, preferred_element_type=jnp.float32)

        meets = Tiles(flags, length, j)

        def work(step):
            start = meets.place(step)
            place = pl.ds(start, KTILE)
            same = allowed(spans, base, start, meets.floor(step))
            sums = [None, None, None]

            def add(block, left, right):
                term = jnp.dot(left, right, preferred_element_type=jnp.float32)
                sums[block] = term if sums[block] is None else sums[block] + term

            for head in range(OWN):
                scores = product(place, K_BLOCK[head], qm[head])
                grad_probs = product(place, V_BLOCK[head], dom[head])
                probs = jnp.where(
                    same, jnp.exp(scores - lse[head : head + 1, pl.ds(base, QTILE)]), 0.0
                )
                grad_scores = (probs * (grad_probs - stats[head : head + 1, :])).astype(jnp.bfloat16)
                add(V_BLOCK[head], probs.astype(jnp.bfloat16), dom[head])
                add(K_BLOCK[head], grad_scores, qm[head])
                rows_k = slice(k_row[head], k_row[head] + 64)
                dqt[64 * head : 64 * head + 64, :] += jnp.dot(
                    kt[rows_k, place], grad_scores, preferred_element_type=jnp.float32
                )
            for block in range(3):
                dkv[place, 128 * block : 128 * block + 128] += sums[block]
            return meets.following(step)

        lax.while_loop(lambda step: step < meets.end, work, meets.after(0))
        lower = dqt[0:128, :].T * 0.125
        upper = dqt[64:192, :].T * 0.125
        dq[pl.ds(base, QTILE), 0:128] = lower.astype(jnp.bfloat16)
        dq[pl.ds(base, QTILE), 128:192] = upper[:, 64:128].astype(jnp.bfloat16)

    @pl.loop(0, tiles)
    def _(t):
        start = pl.multiple_of(t * KTILE, KTILE)
        low_kv[pl.ds(start, KTILE), :] = dkv[pl.ds(start, KTILE), :].astype(jnp.bfloat16)

    copies = []
    for out, masks in zip(outs, out_where):
        for slot, mask in enumerate(masks):
            for flip in range(GROUPS):
                chunk = (ids[0] ^ flip) * classes + (ids[1] ^ mask)
                start = pl.multiple_of(chunk * rows, 64)
                copies.append(
                    pltpu.make_async_copy(
                        low_kv.at[pl.ds(start, rows), :], out.at[slot, flip], sem.at[len(copies)]
                    )
                )
    for copy in copies:
        copy.start()
    for copy in copies:
        copy.wait()


VMEM_SPEC = pl.BlockSpec(memory_space=pltpu.VMEM)
SMEM_SPEC = pl.BlockSpec(memory_space=pltpu.SMEM)
ANY_SPEC = pl.BlockSpec(memory_space=pl.ANY)
PARAMS = pltpu.CompilerParams(vmem_limit_bytes=56 * 1024 * 1024)


def attend_forward(ids, flags, first_q, last_q, spans, pieces, where, rows, classes):
    length = rows * classes * GROUPS
    queries = GROUPS * rows
    copies = sum(len(flips) for _, flips in where)
    return pl.pallas_call(
        functools.partial(forward_kernel, where, rows, classes),
        out_shape=(
            jax.ShapeDtypeStruct((GROUPS, rows * 3 // 2, 128), jnp.bfloat16),
            jax.ShapeDtypeStruct((queries, 128), jnp.float32),
            jax.ShapeDtypeStruct((queries, 128), jnp.float32),
            jax.ShapeDtypeStruct((8, queries), jnp.float32),
        ),
        in_specs=[SMEM_SPEC, SMEM_SPEC, VMEM_SPEC, VMEM_SPEC, VMEM_SPEC]
        + [ANY_SPEC] * len(pieces),
        out_specs=(VMEM_SPEC,) * 4,
        scratch_shapes=[
            pltpu.VMEM((queries, 256), jnp.bfloat16),
            pltpu.VMEM((queries, WIDTH), jnp.bfloat16),
            pltpu.VMEM((length, 384), jnp.bfloat16),
            pltpu.VMEM((256, length), jnp.bfloat16),
            pltpu.VMEM((OWN, QTILE, 128), jnp.bfloat16),
            pltpu.VMEM((8, QTILE), jnp.float32),
            pltpu.VMEM((8, QTILE), jnp.float32),
            pltpu.VMEM((WIDTH, QTILE), jnp.float32),
            pltpu.VMEM((OWN, KTILE, QTILE), jnp.float32),
            pltpu.VMEM((OWN, KTILE, QTILE), jnp.float32),
            pltpu.SemaphoreType.DMA((copies,)),
        ],
        compiler_params=PARAMS,
        cost_estimate=pl.CostEstimate(
            flops=queries * length * WIDTH * 4, bytes_accessed=8 << 20, transcendentals=0
        ),
        name="attend_forward",
    )(ids, flags, first_q, last_q, spans, *pieces)


def attend_backward(
    ids, flags, first_q, last_q, spans, grads, outputs, lse, pieces, after, where, rows, classes, out_where
):
    length = rows * classes * GROUPS
    queries = GROUPS * rows
    copies = sum(len(flips) for _, flips in where)
    return pl.pallas_call(
        functools.partial(backward_kernel, where, rows, classes, out_where, len(after)),
        out_shape=tuple(
            jax.ShapeDtypeStruct((len(masks), GROUPS, rows, 384), jnp.bfloat16)
            for masks in out_where
        )
        + (jax.ShapeDtypeStruct((queries, WIDTH), jnp.bfloat16),),
        in_specs=[SMEM_SPEC, SMEM_SPEC] + [VMEM_SPEC] * 7 + [ANY_SPEC] * (len(pieces) + len(after)),
        out_specs=(ANY_SPEC,) * len(out_where) + (VMEM_SPEC,),
        scratch_shapes=[
            pltpu.VMEM((queries, 256), jnp.bfloat16),
            pltpu.VMEM((queries, 256), jnp.bfloat16),
            pltpu.VMEM((length, 384), jnp.bfloat16),
            pltpu.VMEM((256, length), jnp.bfloat16),
            pltpu.VMEM((OWN, QTILE, 128), jnp.bfloat16),
            pltpu.VMEM((OWN, QTILE, 128), jnp.bfloat16),
            pltpu.VMEM((8, QTILE), jnp.float32),
            pltpu.VMEM((WIDTH, QTILE), jnp.float32),
            pltpu.VMEM((length, 384), jnp.float32),
            pltpu.VMEM((length, 384), jnp.bfloat16),
            pltpu.SemaphoreType.DMA((copies,)),
        ],
        compiler_params=PARAMS,
        cost_estimate=pl.CostEstimate(
            flops=queries * length * WIDTH * 10, bytes_accessed=16 << 20, transcendentals=0
        ),
        name="attend_backward",
    )(ids, flags, first_q, last_q, spans, *outputs, lse, grads, *pieces, *after)


def pick_kernel(ids, w_q, w_k, w_v, out):
    odd = (ids[3] & 1) == 1
    start = pl.multiple_of((ids[3] // 2) * 384 + (ids[3] & 1) * 128, 128)

    def take(weight):
        both = weight[:, pl.ds(start, 256)]
        return jnp.where(odd, both[:, 64:256], both[:, 0:192])

    q, k, v = take(w_q), take(w_k), take(w_v)
    out[...] = jnp.concatenate(
        [k[:, :128], v[:, 128:], k[:, 128:], v[:, :128], q[:, :128], jnp.zeros_like(q[:, :64]), q[:, 128:]],
        axis=1,
    )


def pick_weights(ids, w_q, w_k, w_v):
    return pl.pallas_call(
        pick_kernel,
        out_shape=jax.ShapeDtypeStruct((w_q.shape[0], 640), jnp.bfloat16),
        in_specs=[SMEM_SPEC] + [VMEM_SPEC] * 3,
        out_specs=VMEM_SPEC,
        compiler_params=PARAMS,
        name="pick_weights",
    )(ids, w_q, w_k, w_v)


def project_kernel(count, parts, ids, bias, *rest):
    tokens, weights, (kv, q) = rest[:count], rest[count : count + parts], rest[count + parts :]
    rows = weights[0].shape[0]
    for i, chunk in enumerate(tokens):
        total = bias[...]
        for part, weight in enumerate(weights):
            lanes = (0 if parts == 1 else ids[0] ^ part) * rows
            left = chunk[:, pl.ds(pl.multiple_of(lanes, 128), rows)]
            total = total + jnp.dot(left, weight[...], preferred_element_type=jnp.float32)
        kv[i] = total[:, :384].astype(jnp.bfloat16)
        q[chunk.shape[0] * i : chunk.shape[0] * (i + 1), :] = (
            total[:, 384:].astype(jnp.bfloat16) * jnp.bfloat16(0.125)
        )


def project(ids, bias, chunks, weights):
    count, rows = len(chunks), chunks[0].shape[0]
    return pl.pallas_call(
        functools.partial(project_kernel, count, len(weights)),
        out_shape=(
            jax.ShapeDtypeStruct((count, rows, 384), jnp.bfloat16),
            jax.ShapeDtypeStruct((count * rows, 256), jnp.bfloat16),
        ),
        in_specs=[SMEM_SPEC] + [VMEM_SPEC] * (1 + count + len(weights)),
        out_specs=(VMEM_SPEC, VMEM_SPEC),
        compiler_params=PARAMS,
        cost_estimate=pl.CostEstimate(
            flops=2 * count * rows * D * 640, bytes_accessed=2 << 20, transcendentals=0
        ),
        name="project",
    )(ids, bias, *chunks, *weights)


def out_kernel(parts, weight, vectors, tokens, attn, hidden, hidden_low, unit, scale):
    for g in range(GROUPS):
        attn[:, WIDTH * g : WIDTH * g + WIDTH] = jnp.concatenate(unpack(parts[g]), axis=1)
    total = jnp.dot(attn[...], weight[...], preferred_element_type=jnp.float32) + vectors[0:1, :]
    total = tokens[...].astype(jnp.float32) + total
    value, normal, spread = norm_forward(total, vectors[1:2, :], vectors[2:3, :])
    hidden[...] = value
    hidden_low[...] = value.astype(jnp.bfloat16)
    unit[...] = normal
    scale[...] = jnp.broadcast_to(spread, scale.shape)


def out_project(parts, weight, vectors, tokens):
    shape = tokens.shape
    return pl.pallas_call(
        out_kernel,
        out_shape=(
            jax.ShapeDtypeStruct(shape, jnp.bfloat16),
            jax.ShapeDtypeStruct(shape, jnp.float32),
            jax.ShapeDtypeStruct(shape, jnp.bfloat16),
            jax.ShapeDtypeStruct(shape, jnp.float32),
            jax.ShapeDtypeStruct((shape[0], 128), jnp.float32),
        ),
        in_specs=[VMEM_SPEC] * 4,
        out_specs=(VMEM_SPEC,) * 5,
        compiler_params=PARAMS,
        cost_estimate=pl.CostEstimate(
            flops=2 * shape[0] * D * D, bytes_accessed=5 << 20, transcendentals=0
        ),
        name="out_project",
    )(parts, weight, vectors, tokens)


def out_back_kernel(grad, weight, parts):
    for g in range(GROUPS):
        part = lax.dot_general(
            grad[...], weight[WIDTH * g : WIDTH * g + WIDTH, :], NT, preferred_element_type=jnp.float32
        )
        parts[g] = pack(part.astype(jnp.bfloat16))


def out_back(grad, weight):
    return pl.pallas_call(
        out_back_kernel,
        out_shape=jax.ShapeDtypeStruct((GROUPS, grad.shape[0] * 3 // 2, 128), jnp.bfloat16),
        in_specs=[VMEM_SPEC] * 2,
        out_specs=VMEM_SPEC,
        compiler_params=PARAMS,
        cost_estimate=pl.CostEstimate(
            flops=2 * grad.shape[0] * D * D, bytes_accessed=3 << 20, transcendentals=0
        ),
        name="out_back",
    )(grad, weight)


def tn(left, right):
    return lax.dot_general(
        left, right, (((0,), (0,)), ((), ())), preferred_element_type=jnp.float32
    )


def down_grad_kernel(active, g_low, after, down):
    part = tn(active[...], g_low[...]).astype(jnp.bfloat16)
    for unit in range(4):
        for half in range(2):
            row = (unit % 2) * 192 + 96 * half
            down[unit // 2, 0, row : row + 96, :] = part[
                96 * unit : 96 * unit + 96, 384 * half : 384 * half + 384
            ]


def down_grad(active, g_low, after):
    rows = active.shape[0]
    return pl.pallas_call(
        down_grad_kernel,
        out_shape=jax.ShapeDtypeStruct((4, 4, 384, 384), jnp.bfloat16),
        grid=(8,),
        in_specs=[
            pl.BlockSpec((rows, 384), lambda i: (0, i)),
            pl.BlockSpec((rows, D), lambda i: (0, 0)),
            ANY_SPEC,
        ],
        out_specs=pl.BlockSpec((2, 1, 384, 384), lambda i: (i % 2, (i // 2) % 2 * 2 + i // 4, 0, 0)),
        compiler_params=PARAMS,
        cost_estimate=pl.CostEstimate(
            flops=2 * rows * D * FF, bytes_accessed=8 << 20, transcendentals=0
        ),
        name="down_grad",
    )(active, g_low, after).reshape(2 * FF, D // 2)


def turn(index):
    return (index & 1) * 2 + index // 2


def upper_grad_kernel(ids, hid, g_raised, attn, g_att, vec, after, near, far):
    core, group = ids[1], ids[3]
    outer = tn(attn[...], g_att[...]).astype(jnp.bfloat16)
    left = hid[...].T
    for k in range(GROUPS):
        lanes = slice(384 * k, 384 * k + 384)
        part = jnp.dot(left, g_raised[:, lanes], preferred_element_type=jnp.float32)
        part = part.astype(jnp.bfloat16)
        place = turn(k ^ group)
        for target, own in ((near, core == 0), (far, core != 0)):
            target[place, 0:192, :] = jnp.where(own, part[:192], part[192:])
            first, second = (outer[192 * b + 48 * k : 192 * b + 48 * k + 48] for b in range(2))
            target[place, 192:240, :] = jnp.where(own, first, second)
            target[place, 240:256, :] = vec[k]


def upper_grad(ids, hid, g_raised, attn, g_att, vec, after):
    rows = hid.shape[0]

    def place(i, j, ids):
        return ((j ^ ids[2]) * 2 + (i ^ ids[0]), 0, 0)

    return pl.pallas_call(
        upper_grad_kernel,
        out_shape=(jax.ShapeDtypeStruct((16, 256, 384), jnp.bfloat16),) * 2,
        grid_spec=pltpu.PrefetchScalarGridSpec(
            num_scalar_prefetch=1,
            grid=(2, 2),
            in_specs=[
                pl.BlockSpec((rows, 384), lambda i, j, ids: (0, i)),
                pl.BlockSpec((rows, 1536), lambda i, j, ids: (0, j)),
                pl.BlockSpec((rows, 384), lambda i, j, ids: (0, i)),
                pl.BlockSpec((rows, 384), lambda i, j, ids: (0, j)),
                pl.BlockSpec((4, 16, 384), lambda i, j, ids: (j, 0, 0)),
                ANY_SPEC,
            ],
            out_specs=(pl.BlockSpec((4, 256, 384), place),) * 2,
        ),
        compiler_params=PARAMS,
        cost_estimate=pl.CostEstimate(
            flops=2 * rows * D * (FF + D), bytes_accessed=12 << 20, transcendentals=0
        ),
        name="upper_grad",
    )(ids, hid, g_raised, attn, g_att, vec, after)


def own_source(d, j, ids):
    return (jnp.where(d == 0, j, 1) ^ ids[2], 0, 0)


def other_source(d, j, ids):
    return (jnp.where(d == 0, 0, j) ^ ids[2], 0, 0)


def unpack_upper_kernel(ids, block_own, block_other, up, out, *vecs):
    side, core, mid, group = ids[0], ids[1], ids[2], ids[3]
    b, j = pl.program_id(0) ^ core, pl.program_id(1)
    own = pl.program_id(0) == 0
    for k in range(GROUPS):
        place = turn(k ^ group)
        part = jnp.where(own, block_own[place], block_other[place]).astype(jnp.float32)
        up[:, 384 * k : 384 * k + 384] = part[0:192]
        out[48 * k : 48 * k + 48, :] = part[192:240]

    @pl.when(b == 0)
    def _():
        for u in range(8):
            place = turn((u % 4) ^ group)
            rows = jnp.where(own, block_own[place, 240:256, :], block_other[place, 240:256, :])
            rows = rows.astype(jnp.float32)
            for r in range(3):
                row = 3 * u + r
                if row < 12:
                    target, where, half = vecs[row // 2], 0, row % 2
                elif row < 20:
                    target, where, half = vecs[6], (row - 12) % 4, (row - 12) // 4
                else:
                    continue

                @pl.when((j == u // 4) & (side == half))
                def _():
                    target[384 * where : 384 * where + 384] = rows[r]


def unpack_upper(ids, own, other):
    sizes = [384] * 6 + [1536]
    return pl.pallas_call(
        unpack_upper_kernel,
        out_shape=(
            jax.ShapeDtypeStruct((384, FF), jnp.float32),
            jax.ShapeDtypeStruct((384, D), jnp.float32),
        )
        + tuple(jax.ShapeDtypeStruct((size,), jnp.float32) for size in sizes),
        grid_spec=pltpu.PrefetchScalarGridSpec(
            num_scalar_prefetch=1,
            grid=(2, 2),
            in_specs=[
                pl.BlockSpec((4, 256, 384), own_source),
                pl.BlockSpec((4, 256, 384), other_source),
            ],
            out_specs=(
                pl.BlockSpec((192, 1536), lambda d, j, ids: (d ^ ids[1], j)),
                pl.BlockSpec((192, 384), lambda d, j, ids: (d ^ ids[1], j)),
            )
            + tuple(pl.BlockSpec((size,), lambda d, j, ids: (0,)) for size in sizes),
        ),
        compiler_params=PARAMS,
        name="unpack_upper",
    )(ids, own, other)


def unpack_down_kernel(ids, block_own, block_other, down):
    own, j = pl.program_id(0) == 0, pl.program_id(1)
    for k in range(GROUPS):
        place = turn(k ^ ids[3])
        part = jnp.where(own, block_own[place], block_other[place]).astype(jnp.float32)
        rows = pl.ds(pl.multiple_of(96 * j, 32) + 192 * k, 96)
        down[rows, 0:384] = part[0:96]
        down[rows, 384:768] = part[96:192]


def unpack_down(ids, own, other):
    return pl.pallas_call(
        unpack_down_kernel,
        out_shape=jax.ShapeDtypeStruct((FF // 2, D), jnp.float32),
        grid_spec=pltpu.PrefetchScalarGridSpec(
            num_scalar_prefetch=1,
            grid=(2, 2),
            in_specs=[
                pl.BlockSpec((4, 192, 384), own_source),
                pl.BlockSpec((4, 192, 384), other_source),
            ],
            out_specs=pl.BlockSpec((FF // 4, D), lambda d, j, ids: (d ^ ids[1], 0)),
        ),
        compiler_params=PARAMS,
        name="unpack_down",
    )(ids, own, other)


def qkv_grad_kernel(ids, t0, t1, t2, t3, *rest):
    kept, given, sent, dq, near, far, both, whole = rest
    x, c = ids[0], ids[1]
    rows = dq.shape[0] // GROUPS
    total = jnp.zeros((1, 576), jnp.float32)
    for flip in range(GROUPS):
        term = (
            kept[0, flip].astype(jnp.float32)
            + given[0, flip].astype(jnp.float32)
            + sent[flip].astype(jnp.float32)
        ).astype(jnp.bfloat16)
        own = slice(rows * flip, rows * flip + rows)
        start = pl.multiple_of((flip ^ ids[3]) * rows, 64)
        block = jnp.concatenate([term, dq[pl.ds(start, rows), :]], axis=1)
        both[flip ^ ids[3]] = block
        whole[own, :] = block
        total = total + jnp.sum(block.astype(jnp.float32), axis=0, keepdims=True)
    first = lax.broadcasted_iota(jnp.int32, (16, 576), 0) == 0
    total = jnp.where(first, jnp.broadcast_to(total, (16, 576)), 0.0).astype(jnp.bfloat16)

    @pl.loop(0, 2)
    def _(i):
        lanes = pl.ds(pl.multiple_of(i * 384, 128), 384)
        left = jnp.concatenate([t[:, lanes] for t in (t0, t1, t2, t3)], axis=0)
        part = tn(left, whole[...]).astype(jnp.bfloat16)
        for b in range(2):

            def store(target):
                target[i ^ x, 0:192, :] = part[192 * b : 192 * b + 192]

            pl.when(c == b)(functools.partial(store, near))
            pl.when(c != b)(functools.partial(store, far))
        near[i ^ x, 192:208, :] = total
        far[i ^ x, 192:208, :] = total


def qkv_grads(ids, tokens, kept, given, sent, dq):
    queries = dq.shape[0]
    rows = queries // GROUPS
    return pl.pallas_call(
        qkv_grad_kernel,
        out_shape=(jax.ShapeDtypeStruct((2, 208, 576), jnp.bfloat16),) * 2
        + (jax.ShapeDtypeStruct((GROUPS, rows, 576), jnp.bfloat16),),
        in_specs=[SMEM_SPEC] + [VMEM_SPEC] * 8,
        out_specs=(VMEM_SPEC,) * 3,
        scratch_shapes=[pltpu.VMEM((queries, 576), jnp.bfloat16)],
        compiler_params=PARAMS,
        cost_estimate=pl.CostEstimate(
            flops=2 * queries * D * 576, bytes_accessed=4 << 20, transcendentals=0
        ),
        name="qkv_grads",
    )(ids, *tokens, kept, given, sent, dq)


def unpack_qkv_kernel(ids, own, other, out_q, out_k, out_v, vec):
    c, h = ids[1], ids[3]
    for b in range(2):
        q, k, v = [], [], []
        for g in range(GROUPS):
            block = jnp.where(c == b, own[turn(g ^ h), 0:192, :], other[turn(g ^ h), 0:192, :]).astype(jnp.float32)
            k += [block[:, 0:128], block[:, 192:256]]
            v += [block[:, 256:384], block[:, 128:192]]
            q += [block[:, 384:576]]
        for out, parts in ((out_q, q), (out_k, k), (out_v, v)):
            out[192 * b : 192 * b + 192, :] = jnp.concatenate(parts, axis=1)
    for g in range(GROUPS):
        vec[g] = jnp.where(c == 0, own[turn(g ^ h), 192:208, :], other[turn(g ^ h), 192:208, :]).astype(jnp.float32)


def unpack_qkv(ids, own, other):
    return pl.pallas_call(
        unpack_qkv_kernel,
        out_shape=(jax.ShapeDtypeStruct((384, D), jnp.float32),) * 3
        + (jax.ShapeDtypeStruct((GROUPS, 16, 576), jnp.float32),),
        in_specs=[SMEM_SPEC, VMEM_SPEC, VMEM_SPEC],
        out_specs=(VMEM_SPEC,) * 4,
        compiler_params=PARAMS,
        name="unpack_qkv",
    )(ids, own, other)


def token_grad_kernel(base, both, weight, out):
    total = base[...]
    for g in range(GROUPS):
        w = weight[:, 640 * g : 640 * g + 576]
        total = total + lax.dot_general(both[g], w, NT, preferred_element_type=jnp.float32)
    out[...] = total


def token_grads(base, both, weight):
    return pl.pallas_call(
        token_grad_kernel,
        out_shape=jax.ShapeDtypeStruct(base.shape, jnp.float32),
        in_specs=[VMEM_SPEC] * 3,
        out_specs=VMEM_SPEC,
        compiler_params=PARAMS,
        cost_estimate=pl.CostEstimate(
            flops=2 * base.shape[0] * D * 2304, bytes_accessed=8 << 20, transcendentals=0
        ),
        name="token_grads",
    )(base, both, weight)


def own_part(weight, core):
    half = weight.shape[0] // 2
    return lax.dynamic_slice_in_dim(weight, core * half, half, 0)


def reduce_blocks(grad):
    flat = grad.reshape((-1,) + grad.shape[2:])
    mine = lax.psum_scatter(flat, ("wa", "c"), scatter_dimension=0, tiled=True)
    mine = lax.psum_scatter(mine, "m", scatter_dimension=0, tiled=True)
    mine = lax.psum_scatter(mine, "h", scatter_dimension=0, tiled=True)
    return lax.all_gather(mine, ("c", "m", "h"), axis=0, tiled=True)


def tie(array, *others):
    return lax.optimization_barrier((array,) + others)[0]


def both_sum(near, far, *others):
    near = tie(near, *others)
    return low(widen(near) + widen(far))


def fold(near, far, *others):
    near = tie(near, *others)
    return [low(widen(near[i]) + widen(far[i])) for i in range(2)]


def double(array, axis, bit):
    return jnp.concatenate([array, swap(array, axis, bit)], axis=0)


def pick_columns(weight, group):
    q, k, v = (lax.dynamic_slice_in_dim(w, group * WIDTH, WIDTH, w.ndim - 1) for w in weight)
    return jnp.concatenate(
        [
            k[..., :128],
            v[..., 128:],
            k[..., 128:],
            v[..., :128],
            q[..., :128],
            jnp.zeros_like(q[..., :64]),
            q[..., 128:],
        ],
        axis=-1,
    )


def per_device(
    tokens,
    segment_ids,
    cotangent,
    w_query,
    w_key,
    w_value,
    w_out,
    w_up,
    w_down,
    b_query,
    b_value,
    b_out,
    gain_one,
    shift_one,
    b_up,
    b_down,
    gain_two,
    shift_two,
):
    mid = lax.axis_size("m")
    wide = lax.axis_size("wa")
    paired = mid == 2 and wide == 2
    classes = 2 * mid
    group = lax.axis_index("h")
    core = lax.axis_index("c")
    kind = lax.axis_index("m") * 2 + core
    side = lax.axis_index("wa")
    inputs = tokens[0]
    count = inputs.shape[0]
    chunks = GROUPS * classes
    length = count * chunks
    tiles = length // KTILE
    ids = jnp.stack([group, kind]).astype(jnp.int32)
    place_ids = jnp.stack([side, core, lax.axis_index("m"), group]).astype(jnp.int32)
    order = group ^ jnp.arange(GROUPS)

    second = swap(inputs, "h", 1)
    third = swap(inputs, "h", 2)
    if wide == 2:
        w_own = pick_weights(place_ids, w_query, w_key, w_value)
        w_other = swap(w_own, "wa", 1)
    else:
        w_own = None
        w_other = lax.all_gather(
            pick_columns((w_query, w_key, w_value), group), "wa", axis=0, tiled=True
        )

    smalls = [b_query, b_value, b_out, gain_one, shift_one, b_up, b_down, gain_two, shift_two]
    w_parts = [own_part(item, core) for item in (w_out, w_up, w_down)]
    joined = lax.all_gather(tie(jnp.concatenate(smalls), *w_parts), "wa", axis=0)
    second, third, w_other, joined = lax.optimization_barrier((second, third, w_other, joined))
    fourth = swap(third, "h", 1)
    full, place = [], 0
    for item in smalls:
        size = item.shape[0]
        full.append(widen(joined[:, place : place + size].reshape(-1)))
        place += size
    bias_query, bias_value, bias_out, gain_attn, shift_attn, bias_up, bias_down, gain_ffn, shift_ffn = full
    b_group = pick_columns((bias_query, jnp.zeros_like(bias_query), bias_value), group)[None]

    w_group = (w_own, w_other) if wide == 2 else (w_other,)
    full_out, full_up, full_down = (
        lax.all_gather(tie(part, w_other), ("wa", "c"), axis=0, tiled=True) for part in w_parts
    )
    where, pieces = [], []

    def spread(piece, flips):
        have = {0: piece}
        bit = 1
        while bit < mid:
            for mask in list(have):
                have[mask | (bit << 1)] = swap(have[mask], "m", bit)
            bit *= 2
        for mask in list(have):
            have[mask | 1] = swap(have[mask], "c", 1)
        for mask, item in have.items():
            where.append((mask, flips))
            pieces.append(item)

    first_kv, first_q = project(place_ids, b_group, (inputs, second, third), w_group)
    spread(first_kv, (0, 1, 2))

    segs = double(tie(segment_ids, first_kv), "c", 1)
    bit = 1
    while bit < mid:
        segs = double(segs, "m", bit)
        bit *= 2
    segs = double(double(segs, "h", 1), "h", 2)
    segs = jnp.take(segs, (group * classes + kind) ^ jnp.arange(chunks), axis=0)

    own_segs = lax.dynamic_index_in_dim(
        segs.reshape(GROUPS, classes, count), kind, 1, keepdims=False
    ).reshape(-1)

    names = jnp.arange(DOCS)
    begins = jnp.sum((segs.reshape(-1, 1) < names).astype(jnp.int32), axis=0)
    ends = jnp.sum((segs.reshape(-1, 1) <= names).astype(jnp.int32), axis=0)
    chosen = own_segs[None, :] == names[:, None]
    begins = jnp.sum(jnp.where(chosen, begins[:, None], 0), axis=0)
    ends = jnp.sum(jnp.where(chosen, ends[:, None], 0), axis=0)
    spans = jnp.concatenate(
        [begins[None], ends[None], jnp.zeros((6, begins.shape[0]), jnp.int32)], axis=0
    )
    ends_at = length // KSTEP
    edges = (jnp.arange(ends_at) * KSTEP)[None, :, None]
    meets = (begins.reshape(-1, 1, QTILE) < edges + KSTEP) & (ends.reshape(-1, 1, QTILE) > edges)
    meets = jnp.any(meets, axis=-1)
    steps = jnp.arange(ends_at)
    starts = jnp.arange(ends_at + KTILE // KSTEP + 1)
    later = meets[:, None, :] & (steps[None, None, :] >= starts[None, :, None])
    flags = jnp.min(jnp.where(later, steps, ends_at), axis=-1).astype(jnp.int32).reshape(-1)

    last_kv, last_q = project(place_ids, b_group, (fourth,), w_group)
    spread(last_kv, (3,))
    where = tuple(where)
    group_tokens = [inputs, second, third, fourth]

    o_parts, o_first, o_second, lse = attend_forward(
        ids, flags, first_q, last_q, spans, pieces, where, count, classes
    )

    w_query, w_key, w_value = (tie(item, lse) for item in (w_query, w_key, w_value))
    columns = []
    for g in range(GROUPS):
        low_part, high_part = slice(192 * g, 192 * g + 128), slice(192 * g + 128, 192 * g + 192)
        columns += [w_key[:, low_part], w_value[:, high_part], w_key[:, high_part], w_value[:, low_part]]
        columns += [w_query[:, 192 * g : 192 * g + 192], jnp.zeros_like(w_query[:, :64])]
    by_group = own_part(jnp.concatenate(columns, axis=1), core)
    by_group = lax.all_gather(by_group, ("wa", "c"), axis=0, tiled=True)

    def send_back(parts):
        return lax.all_to_all(parts, "h", 0, 0, tiled=True)

    zeros = jnp.zeros_like(bias_out)
    attn_low, hidden, hidden_low, unit_one, scale_one = out_project(
        send_back(o_parts),
        full_out,
        jnp.stack([bias_out, gain_attn, shift_attn] + [zeros] * 5),
        inputs,
    )
    scale_one = scale_one[:, :1]
    raised = mm(hidden_low, full_up) + bias_up
    active, slope = gelu_pair(raised)
    active_low = low(active)
    lowered = mm(active_low, full_down) + bias_down
    result, unit_two, scale_two = norm_forward(hidden + lowered, gain_ffn, shift_ffn)
    grad_sum_two, grad_gain_two, grad_shift_two = norm_backward(
        widen(cotangent[0]), unit_two, scale_two, gain_ffn
    )
    grad_lowered = low(grad_sum_two)
    grad_b_down = jnp.sum(widen(grad_lowered), axis=0)
    grad_raised = low(back_product(grad_lowered, full_down) * slope)
    grad_b_up = jnp.sum(widen(grad_raised), axis=0)
    grad_hidden = grad_sum_two + back_product(grad_raised, full_up)
    grad_sum_one, grad_gain_one, grad_shift_one = norm_backward(
        grad_hidden, unit_one, scale_one, gain_attn
    )
    grad_attended = low(grad_sum_one)
    grad_b_out = jnp.sum(widen(grad_attended), axis=0)

    grad_rows = send_back(out_back(grad_attended, full_out))

    vectors = jnp.concatenate(
        [grad_b_out, grad_gain_one, grad_shift_one, grad_b_down, grad_gain_two, grad_shift_two, grad_b_up]
    )
    blocks = 2 * wide
    if paired:
        vectors = jnp.pad(low(vectors), (0, 9216 - 7680)).reshape(8, 3, 384)
        vectors = jnp.pad(vectors, ((0, 0), (0, 13), (0, 0)))
        near, far = upper_grad(
            place_ids, hidden_low, grad_raised, attn_low, grad_attended, vectors, grad_attended
        )
        shape = (2, 2, 2, 2, 256, 384)
        near, far = near.reshape(shape), swap(far, "c", 1).reshape(shape)
        grad_rows = tie(grad_rows, near)
        down_sum = down_grad(active_low, grad_lowered, near)
        upper, give = fold(near, far, down_sum)
        after = (give,)
        give = swap(give, "m", 1)
        down_sum = tie(down_sum, grad_rows, by_group)
        down_sum = lax.psum_scatter(down_sum, ("h", "c"), scatter_dimension=0, tiled=True)
    else:
        grad_w_down = low(outer_sum(active_low, grad_lowered))
        grad_w_up = low(outer_sum(hidden_low, grad_raised))
        grad_w_out = low(outer_sum(attn_low, grad_attended))
        vectors = jnp.pad(low(vectors).reshape(-1, D), ((0, 6), (0, 0)))
        down_rows, out_rows = FF // blocks, D // blocks
        ffn = jnp.concatenate(
            [
                grad_w_down.reshape(blocks, down_rows, D),
                grad_w_up.reshape(blocks, down_rows, D),
                grad_w_out.reshape(blocks, out_rows, D),
                jnp.broadcast_to(vectors[None], (blocks, 16, D)),
            ],
            axis=1,
        )
        after = ()
        ffn_sum = reduce_blocks(ffn).reshape(2, -1, D)
        out_down = widen(ffn_sum[:, :down_rows]).reshape(-1, D)
        out_up = widen(ffn_sum[:, down_rows : 2 * down_rows]).reshape(-1, FF)
        place = 2 * down_rows
        out_out = widen(ffn_sum[:, place : place + out_rows]).reshape(-1, D)
        small = widen(ffn_sum[0, place + out_rows :])

        def share(row, rows):
            vector = small[row : row + rows].reshape(-1)
            size = vector.shape[0] // wide
            return lax.dynamic_slice_in_dim(vector, side * size, size, 0)

        vectors = [share(row, 1) for row in range(6)] + [share(6, 4)]

    stay_masks, leave_masks = tuple(range(0, classes, 2)), tuple(range(1, classes, 2))
    out_where = (stay_masks,) + tuple((mask,) for mask in leave_masks)

    kept, *given, dq = attend_backward(
        ids, flags, first_q, last_q, spans, grad_rows, (o_first, o_second), lse,
        pieces, after, where, count, classes, out_where,
    )

    given = [swap(item, "c", 1) for item in given]
    if paired:
        upper, give = fold(upper, give, dq)
        kept = tie(kept, give)
        sent = low(widen(kept[1]) + widen(given[1][0]))
        down_sum = lax.psum_scatter(tie(down_sum, sent), "wa", scatter_dimension=0, tiled=True)
        give = swap(give, "wa", 1)
        upper = tie(upper, sent)
        sent = swap(sent, "m", 1)
        upper, give = fold(upper, give)
        kept = tie(kept, give)
        give = swap(give, "h", 1)
    else:
        partial = widen(kept) + widen(jnp.concatenate(given, axis=0))
        stay = list(stay_masks)
        bit = mid // 2
        while bit >= 1:
            mask = bit << 1
            near = [i for i, m in enumerate(stay) if not m & mask]
            far = [i for i, m in enumerate(stay) if m & mask]
            sent = swap(low(partial[far[0] : far[-1] + 1]), "m", bit)
            partial = widen(low(partial[near[0] : near[-1] + 1])) + widen(sent)
            stay = [stay[i] for i in near]
            bit //= 2
        dkv = low(partial[0]).reshape(GROUPS * count, 384)

    part = D // wide
    if paired:
        near, far, parts = qkv_grads(place_ids, group_tokens, kept, given[0], sent, dq)
        far = swap(far, "c", 1)
        down_sum = lax.psum_scatter(tie(down_sum, near), "m", scatter_dimension=0, tiled=True)
        upper, give = fold(upper, give, near)
        near = tie(near, give)
        give = swap(give, "h", 2)
        qkv, other = fold(near, far)
        other = swap(other, "wa", 1)
        down_other = swap(down_sum, "h", 2)
        upper = both_sum(upper, give, qkv)
        upper_other = swap(upper, "h", 2)
        qkv = both_sum(qkv, other, upper)
        other = swap(qkv, "m", 1)
        down_sum = jnp.stack([tie(down_sum, qkv), down_other])
        down_other = swap(down_sum, "h", 1)
        upper = jnp.stack([tie(upper, down_sum), upper_other])
        upper_other = swap(upper, "h", 1)
        qkv = both_sum(qkv, other, upper)
        other = swap(qkv, "h", 2)
        down_sum = jnp.stack([tie(down_sum, qkv), down_other])
        down_other = swap(down_sum, "m", 1)
        upper = jnp.stack([tie(upper, down_sum), upper_other])
        upper_other = swap(upper, "m", 1)
        parts = send_back(tie(parts, upper))
        qkv = jnp.stack([tie(qkv, upper), other])
        other = swap(qkv, "h", 1)
        down_sum = jnp.stack([tie(down_sum, qkv), down_other])
        down_other = swap(down_sum, "c", 1)
        qkv = jnp.concatenate([tie(qkv, down_sum), other], axis=0)
        other = swap(qkv, "c", 1)
        down_sum, down_other = (item.reshape(8, 192, 384) for item in (tie(down_sum, qkv), down_other))
        out_down = unpack_down(place_ids, down_sum, down_other)
        upper = jnp.stack([tie(upper, out_down), upper_other])
        upper_other = swap(upper, "c", 1)
        out_query, out_key, out_value, sums = unpack_qkv(place_ids, tie(qkv, upper), other)
        upper, upper_other = (item.reshape(8, 256, 384) for item in (tie(upper, out_query), upper_other))
        out_up, out_out, *vectors = unpack_upper(place_ids, upper, upper_other)
        grad_inputs = token_grads(tie(grad_sum_one, out_up), parts, by_group)
        sums = sums[:, 0]
        sums_v = jnp.concatenate([sums[:, 256:384], sums[:, 128:192]], axis=1).reshape(-1)
        sums_q = sums[:, 384:576].reshape(-1)
    else:
        dq = jnp.take(dq.reshape(GROUPS, count, WIDTH), order, axis=0).reshape(-1, WIDTH)
        both = jnp.concatenate([dkv, dq], axis=1)
        width = both.shape[1]
        parts = send_back(jnp.take(both.reshape(GROUPS, count, width), order, axis=0))
        w_grad = low(outer_sum(jnp.concatenate(group_tokens, axis=0), both)).reshape(blocks, D // blocks, width)
        b_grad = low(jnp.sum(widen(both), axis=0))
        b_grad = jnp.pad(b_grad[None], ((0, 15), (0, 0)))
        qkv = jnp.concatenate([w_grad, jnp.broadcast_to(b_grad[None], (blocks, 16, width))], axis=1)
        rows = qkv.shape[1]
        mine = lax.psum_scatter(
            qkv.reshape(blocks * rows, width), ("wa", "c"), scatter_dimension=0, tiled=True
        )
        mine = lax.psum(mine, "m")
        every = widen(lax.all_gather(mine, ("c", "h"), axis=0).reshape(2, GROUPS, rows, width))

        def columns(block):
            k = jnp.concatenate([block[..., :128], block[..., 192:256]], axis=-1)
            v = jnp.concatenate([block[..., 256:384], block[..., 128:192]], axis=-1)
            q = block[..., 384:576]
            return [jnp.transpose(item, (0, 2, 1, 3)).reshape(2, -1, D) for item in (q, k, v)]

        out_query, out_key, out_value = (
            item.reshape(-1, D) for item in columns(every[:, :, : rows - 16])
        )
        sums_q, _, sums_v = (item[0, 0] for item in columns(every[:, :, rows - 16 : rows - 15]))
        grad_inputs = token_grads(grad_sum_one, parts, by_group)
    out_b_query = lax.dynamic_slice_in_dim(sums_q, side * part, part, 0)
    out_b_value = lax.dynamic_slice_in_dim(sums_v, side * part, part, 0)

    return (
        low(result)[None],
        grad_inputs[None],
        out_query,
        out_key,
        out_value,
        out_out,
        out_up,
        out_down,
        out_b_query,
        out_b_value,
        vectors[0],
        vectors[1],
        vectors[2],
        vectors[6],
        vectors[3],
        vectors[4],
        vectors[5],
    )


def solution(mesh):
    chunks, wide = mesh.devices.shape
    finer = Mesh(
        mesh.devices.reshape(GROUPS, chunks // (2 * GROUPS), 2, wide), ("h", "m", "c", "wa")
    )
    ctx = ("h", "m", "c")
    seq3, seq2 = P("wa", ctx, None), P("wa", ctx)
    matrix, vector = P("wa", None), P("wa")
    return jax.shard_map(
        per_device,
        mesh=finer,
        in_specs=(seq3, seq2, seq3) + (matrix,) * 6 + (vector,) * 9,
        out_specs=(seq3, seq3) + (matrix,) * 6 + (vector,) * 9,
        check_vma=False,
    )
```

```python
import functools

import jax
import jax.numpy as jnp
from jax import lax
from jax.experimental import pallas as pl
from jax.experimental.pallas import tpu as pltpu
from jax.sharding import Mesh
from jax.sharding import PartitionSpec as P

D = 768
HEADS = 12
HEAD_DIM = 64
FF = 3072
DOCS = 32

GROUPS = 4
OWN = HEADS // GROUPS
WIDTH = OWN * HEAD_DIM
QTILE = 256
KTILE = 512
KSTEP = 128

epsilon = 1e-05
masked_value = -1e30
NT = (((1,), (1,)), ((), ()))
NN = (((1,), (0,)), ((), ()))


def widen(array):
    return array.astype(jnp.float32)


def low(array):
    return array.astype(jnp.bfloat16)


def mm(left, right):
    return jnp.dot(left, right, preferred_element_type=jnp.float32)


def outer_sum(left, right):
    return lax.dot_general(
        left, right, (((0,), (0,)), ((), ())), preferred_element_type=jnp.float32
    )


def back_product(grad, weight):
    return lax.dot_general(grad, weight, NT, preferred_element_type=jnp.float32)


def norm_forward(values, gain, shift):
    centre = values - jnp.mean(values, axis=-1, keepdims=True)
    scale = lax.rsqrt(jnp.mean(centre * centre, axis=-1, keepdims=True) + epsilon)
    unit = centre * scale
    return (unit * gain + shift, unit, scale)


def norm_backward(grad, unit, scale, gain):
    grad_gain = jnp.sum(grad * unit, axis=0)
    grad_shift = jnp.sum(grad, axis=0)
    inner = grad * gain
    grad_in = scale * (
        inner
        - jnp.mean(inner, axis=-1, keepdims=True)
        - unit * jnp.mean(inner * unit, axis=-1, keepdims=True)
    )
    return (grad_in, grad_gain, grad_shift)


def gelu_pair(values):
    cumulative = 0.5 * (1.0 + lax.erf(values * 0.7071067811865476))
    density = jnp.exp(-0.5 * values * values) * 0.3989422804014327
    return (values * cumulative, cumulative + values * density)


def swap(array, axis, bit):
    size = lax.axis_size(axis)
    return lax.ppermute(array, axis, [(i, i ^ bit) for i in range(size)])


K_BLOCK = (0, 0, 1)
V_BLOCK = (2, 2, 1)
K_UPPER = (False, True, True)
V_UPPER = (False, True, False)


def lane_half(array, upper):
    lane = lax.broadcasted_iota(jnp.int32, array.shape, 1)
    keep = (lane >= 64) if upper else (lane < 64)
    return jnp.where(keep, array, jnp.zeros_like(array))


def start_pieces(where, ids, pieces, kv, sem, rows, classes):
    for piece, (mask, flips) in zip(pieces, where):
        for slot, flip in enumerate(flips):
            chunk = (ids[0] ^ flip) * classes + (ids[1] ^ mask)
            start = pl.multiple_of(chunk * rows, 64)
            pltpu.make_async_copy(
                piece.at[slot], kv.at[pl.ds(start, rows), :], sem.at[chunk]
            ).start()


def turn_pieces(pieces, kv, turned, blocks, sem, rows):
    @pl.loop(0, kv.shape[0] // (2 * rows))
    def _(t):
        for half in range(2):
            start = pl.multiple_of((2 * t + half) * rows, 64)
            pltpu.make_async_copy(
                pieces[0].at[0], kv.at[pl.ds(start, rows), :], sem.at[2 * t + half]
            ).wait()
        both = pl.ds(pl.multiple_of(t * 2 * rows, 128), 2 * rows)
        for n, block in enumerate(blocks):
            turned[128 * n : 128 * n + 128, both] = kv[both, 128 * block : 128 * block + 128].T


def pack(part):
    half = part.shape[0] // 2
    return jnp.concatenate(
        [part[:, :128], jnp.concatenate([part[:half, 128:], part[half:, 128:]], axis=1)], axis=0
    )


def unpack(packed):
    rows = packed.shape[0] // 3 * 2
    rest = packed[rows:]
    return packed[:rows], jnp.concatenate([rest[:, :64], rest[:, 64:]], axis=0)


def order_queries(ids, first_q, last_q, q, rows):
    for flip in range(GROUPS):
        part, place = (last_q, 0) if flip == 3 else (first_q, rows * flip)
        start = pl.multiple_of((ids[0] ^ flip) * rows, 64)
        q[pl.ds(start, rows), :] = part[place : place + rows, :]


def allowed(spans, base, start, floor):
    position = lax.broadcasted_iota(jnp.int32, (KTILE, QTILE), 0)
    first = jnp.maximum(spans[0:1, pl.ds(base, QTILE)] - start, floor)
    last = spans[1:2, pl.ds(base, QTILE)] - start
    return (position >= first) & (position < last)


class Tiles:
    def __init__(self, steps, length, j):
        self.end = length // KSTEP
        self.span = KTILE // KSTEP
        self.steps, self.row = steps, j * (self.end + self.span + 1)

    def after(self, step):
        return self.steps[self.row + step]

    def following(self, step):
        return self.after(step + self.span)

    def place(self, step):
        return pl.multiple_of(jnp.minimum(step, self.end - self.span) * KSTEP, KSTEP)

    def floor(self, step):
        floor = jnp.maximum(step - (self.end - self.span), 0) * KSTEP
        return jnp.where(step < self.end, floor, KTILE)


def walk(tiles, fetch, work):
    begin = tiles.after(0)
    fetch(0, tiles.place(begin))

    def body(here):
        there = tiles.following(here)
        later = tiles.following(there)
        fetch(1, tiles.place(there))
        work(0, tiles.place(here), tiles.floor(here))
        fetch(0, tiles.place(later))
        work(1, tiles.place(there), tiles.floor(there))
        return later

    lax.while_loop(lambda here: here < tiles.end, body, begin)


def forward_kernel(where, rows, classes, ids, flags, first_q, last_q, spans, *rest):
    count = len(where)
    pieces = rest[:count]
    o_parts, o_first, o_second, lse, q, o_low, kv, vt, qm, top, total, accum, first, second, sem = rest[
        count:
    ]
    length = kv.shape[0]
    tiles = length // KTILE
    start_pieces(where, ids, pieces, kv, sem, rows, classes)
    order_queries(ids, first_q, last_q, q, rows)
    turn_pieces(pieces, kv, vt, (1, 2), sem, rows)

    v_row = (128, 192, 0)

    @pl.loop(0, q.shape[0] // QTILE)
    def _(j):
        base = pl.multiple_of(j * QTILE, QTILE)
        for head in range(OWN):
            block = q[pl.ds(base, QTILE), pl.ds(128 * K_BLOCK[head], 128)]
            qm[head] = lane_half(block, K_UPPER[head])
        top[...] = jnp.full_like(top, masked_value)
        total[...] = jnp.zeros_like(total)
        accum[...] = jnp.zeros_like(accum)

        stages = (first, second)

        def fetch(stage, start):
            for head in range(OWN):
                block = 128 * K_BLOCK[head]
                stages[stage][head] = lax.dot_general(
                    kv[pl.ds(start, KTILE), block : block + 128],
                    qm[head],
                    NT,
                    preferred_element_type=jnp.float32,
                )

        def work(stage, start, floor):
            same = allowed(spans, base, start, floor)
            for head in range(OWN):
                scores = jnp.where(same, stages[stage][head], masked_value)
                old = top[head : head + 1, :]
                new = jnp.maximum(old, jnp.max(scores, axis=0, keepdims=True))
                weights = jnp.exp(scores - new)
                factor = jnp.exp(old - new)
                top[head : head + 1, :] = new
                total[head : head + 1, :] = total[head : head + 1, :] * factor + jnp.sum(
                    weights, axis=0, keepdims=True
                )
                rows_v = slice(v_row[head], v_row[head] + 64)
                place = slice(64 * head, 64 * head + 64)
                accum[place, :] = accum[place, :] * factor + jnp.dot(
                    vt[rows_v, pl.ds(start, KTILE)],
                    weights.astype(jnp.bfloat16),
                    preferred_element_type=jnp.float32,
                )

        walk(Tiles(flags, length, j), fetch, work)
        outs = [
            accum[64 * head : 64 * head + 64, :] / total[head : head + 1, :] for head in range(OWN)
        ]
        lower = jnp.concatenate(outs[:2], axis=0).T
        upper = jnp.concatenate([outs[2], jnp.zeros_like(outs[2])], axis=0).T
        o_first[pl.ds(base, QTILE), :] = lower
        o_second[pl.ds(base, QTILE), :] = upper
        o_low[pl.ds(base, QTILE), 0:128] = lower.astype(jnp.bfloat16)
        o_low[pl.ds(base, QTILE), 128:192] = upper[:, 0:64].astype(jnp.bfloat16)
        lse[:, pl.ds(base, QTILE)] = top[...] + jnp.log(total[...])

    for chunk in range(GROUPS):
        o_parts[chunk] = pack(o_low[rows * chunk : rows * chunk + rows, :])


def backward_kernel(where, rows, classes, out_where, extra, ids, flags, first_q, last_q, spans, o_first, o_second, lse, *rest):
    count = len(where)
    grads, pieces = rest[0], rest[1 : 1 + count]
    rest = rest[1 + count + extra :]
    outs = rest[: len(out_where)]
    dq, q, grad, kv, kt, qm, dom, stats, dqt, dkv, low_kv, sem = rest[len(out_where) :]
    length = kv.shape[0]
    tiles = length // KTILE
    start_pieces(where, ids, pieces, kv, sem, rows, classes)

    @pl.loop(0, tiles)
    def _(t):
        start = pl.multiple_of(t * KTILE, KTILE)
        dkv[pl.ds(start, KTILE), :] = jnp.zeros((KTILE, 384), jnp.float32)

    order_queries(ids, first_q, last_q, q, rows)
    for chunk in range(GROUPS):
        first, last = unpack(grads[chunk])
        grad[rows * chunk : rows * chunk + rows, :] = jnp.concatenate(
            [first, last, jnp.zeros((rows, 64), jnp.bfloat16)], axis=1
        )

    turn_pieces(pieces, kv, kt, (0, 1), sem, rows)

    k_row = (0, 64, 192)

    @pl.loop(0, q.shape[0] // QTILE)
    def _(j):
        base = pl.multiple_of(j * QTILE, QTILE)
        for head in range(OWN):
            block = q[pl.ds(base, QTILE), pl.ds(128 * K_BLOCK[head], 128)]
            qm[head] = lane_half(block, K_UPPER[head])
            block = grad[pl.ds(base, QTILE), pl.ds(128 * (2 - V_BLOCK[head]), 128)]
            dom[head] = lane_half(block, V_UPPER[head])
        for part in range(2):
            product = (
                grad[pl.ds(base, QTILE), 128 * part : 128 * part + 128].astype(jnp.float32)
                * (o_first, o_second)[part][pl.ds(base, QTILE), :]
            ).T
            for half in range(2):
                head = 2 * part + half
                if head < OWN:
                    stats[head : head + 1, :] = jnp.sum(
                        product[64 * half : 64 * half + 64], axis=0, keepdims=True
                    )
        dqt[...] = jnp.zeros_like(dqt)

        def product(place, block, right):
            left = kv[place, 128 * block : 128 * block + 128]
            return lax.dot_general(left, right, NT, preferred_element_type=jnp.float32)

        meets = Tiles(flags, length, j)

        def work(step):
            start = meets.place(step)
            place = pl.ds(start, KTILE)
            same = allowed(spans, base, start, meets.floor(step))
            sums = [None, None, None]

            def add(block, left, right):
                term = jnp.dot(left, right, preferred_element_type=jnp.float32)
                sums[block] = term if sums[block] is None else sums[block] + term

            for head in range(OWN):
                scores = product(place, K_BLOCK[head], qm[head])
                grad_probs = product(place, V_BLOCK[head], dom[head])
                probs = jnp.where(
                    same, jnp.exp(scores - lse[head : head + 1, pl.ds(base, QTILE)]), 0.0
                )
                grad_scores = (probs * (grad_probs - stats[head : head + 1, :])).astype(jnp.bfloat16)
                add(V_BLOCK[head], probs.astype(jnp.bfloat16), dom[head])
                add(K_BLOCK[head], grad_scores, qm[head])
                rows_k = slice(k_row[head], k_row[head] + 64)
                dqt[64 * head : 64 * head + 64, :] += jnp.dot(
                    kt[rows_k, place], grad_scores, preferred_element_type=jnp.float32
                )
            for block in range(3):
                dkv[place, 128 * block : 128 * block + 128] += sums[block]
            return meets.following(step)

        lax.while_loop(lambda step: step < meets.end, work, meets.after(0))
        lower = dqt[0:128, :].T * 0.125
        upper = dqt[64:192, :].T * 0.125
        dq[pl.ds(base, QTILE), 0:128] = lower.astype(jnp.bfloat16)
        dq[pl.ds(base, QTILE), 128:192] = upper[:, 64:128].astype(jnp.bfloat16)

    @pl.loop(0, tiles)
    def _(t):
        start = pl.multiple_of(t * KTILE, KTILE)
        low_kv[pl.ds(start, KTILE), :] = dkv[pl.ds(start, KTILE), :].astype(jnp.bfloat16)

    copies = []
    for out, masks in zip(outs, out_where):
        for slot, mask in enumerate(masks):
            for flip in range(GROUPS):
                chunk = (ids[0] ^ flip) * classes + (ids[1] ^ mask)
                start = pl.multiple_of(chunk * rows, 64)
                copies.append(
                    pltpu.make_async_copy(
                        low_kv.at[pl.ds(start, rows), :], out.at[slot, flip], sem.at[len(copies)]
                    )
                )
    for copy in copies:
        copy.start()
    for copy in copies:
        copy.wait()


VMEM_SPEC = pl.BlockSpec(memory_space=pltpu.VMEM)
SMEM_SPEC = pl.BlockSpec(memory_space=pltpu.SMEM)
ANY_SPEC = pl.BlockSpec(memory_space=pl.ANY)
PARAMS = pltpu.CompilerParams(vmem_limit_bytes=56 * 1024 * 1024)


def attend_forward(ids, flags, first_q, last_q, spans, pieces, where, rows, classes):
    length = rows * classes * GROUPS
    queries = GROUPS * rows
    copies = sum(len(flips) for _, flips in where)
    return pl.pallas_call(
        functools.partial(forward_kernel, where, rows, classes),
        out_shape=(
            jax.ShapeDtypeStruct((GROUPS, rows * 3 // 2, 128), jnp.bfloat16),
            jax.ShapeDtypeStruct((queries, 128), jnp.float32),
            jax.ShapeDtypeStruct((queries, 128), jnp.float32),
            jax.ShapeDtypeStruct((8, queries), jnp.float32),
        ),
        in_specs=[SMEM_SPEC, SMEM_SPEC, VMEM_SPEC, VMEM_SPEC, VMEM_SPEC]
        + [ANY_SPEC] * len(pieces),
        out_specs=(VMEM_SPEC,) * 4,
        scratch_shapes=[
            pltpu.VMEM((queries, 256), jnp.bfloat16),
            pltpu.VMEM((queries, WIDTH), jnp.bfloat16),
            pltpu.VMEM((length, 384), jnp.bfloat16),
            pltpu.VMEM((256, length), jnp.bfloat16),
            pltpu.VMEM((OWN, QTILE, 128), jnp.bfloat16),
            pltpu.VMEM((8, QTILE), jnp.float32),
            pltpu.VMEM((8, QTILE), jnp.float32),
            pltpu.VMEM((WIDTH, QTILE), jnp.float32),
            pltpu.VMEM((OWN, KTILE, QTILE), jnp.float32),
            pltpu.VMEM((OWN, KTILE, QTILE), jnp.float32),
            pltpu.SemaphoreType.DMA((copies,)),
        ],
        compiler_params=PARAMS,
        cost_estimate=pl.CostEstimate(
            flops=queries * length * WIDTH * 4, bytes_accessed=8 << 20, transcendentals=0
        ),
        name="attend_forward",
    )(ids, flags, first_q, last_q, spans, *pieces)


def attend_backward(
    ids, flags, first_q, last_q, spans, grads, outputs, lse, pieces, after, where, rows, classes, out_where
):
    length = rows * classes * GROUPS
    queries = GROUPS * rows
    copies = sum(len(flips) for _, flips in where)
    return pl.pallas_call(
        functools.partial(backward_kernel, where, rows, classes, out_where, len(after)),
        out_shape=tuple(
            jax.ShapeDtypeStruct((len(masks), GROUPS, rows, 384), jnp.bfloat16)
            for masks in out_where
        )
        + (jax.ShapeDtypeStruct((queries, WIDTH), jnp.bfloat16),),
        in_specs=[SMEM_SPEC, SMEM_SPEC] + [VMEM_SPEC] * 7 + [ANY_SPEC] * (len(pieces) + len(after)),
        out_specs=(ANY_SPEC,) * len(out_where) + (VMEM_SPEC,),
        scratch_shapes=[
            pltpu.VMEM((queries, 256), jnp.bfloat16),
            pltpu.VMEM((queries, 256), jnp.bfloat16),
            pltpu.VMEM((length, 384), jnp.bfloat16),
            pltpu.VMEM((256, length), jnp.bfloat16),
            pltpu.VMEM((OWN, QTILE, 128), jnp.bfloat16),
            pltpu.VMEM((OWN, QTILE, 128), jnp.bfloat16),
            pltpu.VMEM((8, QTILE), jnp.float32),
            pltpu.VMEM((WIDTH, QTILE), jnp.float32),
            pltpu.VMEM((length, 384), jnp.float32),
            pltpu.VMEM((length, 384), jnp.bfloat16),
            pltpu.SemaphoreType.DMA((copies,)),
        ],
        compiler_params=PARAMS,
        cost_estimate=pl.CostEstimate(
            flops=queries * length * WIDTH * 10, bytes_accessed=16 << 20, transcendentals=0
        ),
        name="attend_backward",
    )(ids, flags, first_q, last_q, spans, *outputs, lse, grads, *pieces, *after)


def pick_kernel(ids, w_q, w_k, w_v, out):
    odd = (ids[3] & 1) == 1
    start = pl.multiple_of((ids[3] // 2) * 384 + (ids[3] & 1) * 128, 128)

    def take(weight):
        both = weight[:, pl.ds(start, 256)]
        return jnp.where(odd, both[:, 64:256], both[:, 0:192])

    q, k, v = take(w_q), take(w_k), take(w_v)
    out[...] = jnp.concatenate(
        [k[:, :128], v[:, 128:], k[:, 128:], v[:, :128], q[:, :128], jnp.zeros_like(q[:, :64]), q[:, 128:]],
        axis=1,
    )


def pick_weights(ids, w_q, w_k, w_v):
    return pl.pallas_call(
        pick_kernel,
        out_shape=jax.ShapeDtypeStruct((w_q.shape[0], 640), jnp.bfloat16),
        in_specs=[SMEM_SPEC] + [VMEM_SPEC] * 3,
        out_specs=VMEM_SPEC,
        compiler_params=PARAMS,
        name="pick_weights",
    )(ids, w_q, w_k, w_v)


def project_kernel(count, parts, ids, bias, *rest):
    tokens, weights, (kv, q) = rest[:count], rest[count : count + parts], rest[count + parts :]
    rows = weights[0].shape[0]
    for i, chunk in enumerate(tokens):
        total = bias[...]
        for part, weight in enumerate(weights):
            lanes = (0 if parts == 1 else ids[0] ^ part) * rows
            left = chunk[:, pl.ds(pl.multiple_of(lanes, 128), rows)]
            total = total + jnp.dot(left, weight[...], preferred_element_type=jnp.float32)
        kv[i] = total[:, :384].astype(jnp.bfloat16)
        q[chunk.shape[0] * i : chunk.shape[0] * (i + 1), :] = (
            total[:, 384:].astype(jnp.bfloat16) * jnp.bfloat16(0.125)
        )


def project(ids, bias, chunks, weights):
    count, rows = len(chunks), chunks[0].shape[0]
    return pl.pallas_call(
        functools.partial(project_kernel, count, len(weights)),
        out_shape=(
            jax.ShapeDtypeStruct((count, rows, 384), jnp.bfloat16),
            jax.ShapeDtypeStruct((count * rows, 256), jnp.bfloat16),
        ),
        in_specs=[SMEM_SPEC] + [VMEM_SPEC] * (1 + count + len(weights)),
        out_specs=(VMEM_SPEC, VMEM_SPEC),
        compiler_params=PARAMS,
        cost_estimate=pl.CostEstimate(
            flops=2 * count * rows * D * 640, bytes_accessed=2 << 20, transcendentals=0
        ),
        name="project",
    )(ids, bias, *chunks, *weights)


def out_kernel(parts, weight, vectors, tokens, attn, hidden, hidden_low, unit, scale):
    for g in range(GROUPS):
        attn[:, WIDTH * g : WIDTH * g + WIDTH] = jnp.concatenate(unpack(parts[g]), axis=1)
    total = jnp.dot(attn[...], weight[...], preferred_element_type=jnp.float32) + vectors[0:1, :]
    total = tokens[...].astype(jnp.float32) + total
    value, normal, spread = norm_forward(total, vectors[1:2, :], vectors[2:3, :])
    hidden[...] = value
    hidden_low[...] = value.astype(jnp.bfloat16)
    unit[...] = normal
    scale[...] = jnp.broadcast_to(spread, scale.shape)


def out_project(parts, weight, vectors, tokens):
    shape = tokens.shape
    return pl.pallas_call(
        out_kernel,
        out_shape=(
            jax.ShapeDtypeStruct(shape, jnp.bfloat16),
            jax.ShapeDtypeStruct(shape, jnp.float32),
            jax.ShapeDtypeStruct(shape, jnp.bfloat16),
            jax.ShapeDtypeStruct(shape, jnp.float32),
            jax.ShapeDtypeStruct((shape[0], 128), jnp.float32),
        ),
        in_specs=[VMEM_SPEC] * 4,
        out_specs=(VMEM_SPEC,) * 5,
        compiler_params=PARAMS,
        cost_estimate=pl.CostEstimate(
            flops=2 * shape[0] * D * D, bytes_accessed=5 << 20, transcendentals=0
        ),
        name="out_project",
    )(parts, weight, vectors, tokens)


def out_back_kernel(grad, weight, parts):
    for g in range(GROUPS):
        part = lax.dot_general(
            grad[...], weight[WIDTH * g : WIDTH * g + WIDTH, :], NT, preferred_element_type=jnp.float32
        )
        parts[g] = pack(part.astype(jnp.bfloat16))


def out_back(grad, weight):
    return pl.pallas_call(
        out_back_kernel,
        out_shape=jax.ShapeDtypeStruct((GROUPS, grad.shape[0] * 3 // 2, 128), jnp.bfloat16),
        in_specs=[VMEM_SPEC] * 2,
        out_specs=VMEM_SPEC,
        compiler_params=PARAMS,
        cost_estimate=pl.CostEstimate(
            flops=2 * grad.shape[0] * D * D, bytes_accessed=3 << 20, transcendentals=0
        ),
        name="out_back",
    )(grad, weight)


def tn(left, right):
    return lax.dot_general(
        left, right, (((0,), (0,)), ((), ())), preferred_element_type=jnp.float32
    )


def down_grad_kernel(active, g_low, after, down):
    part = tn(active[...], g_low[...]).astype(jnp.bfloat16)
    for unit in range(4):
        for half in range(2):
            row = (unit % 2) * 192 + 96 * half
            down[unit // 2, 0, row : row + 96, :] = part[
                96 * unit : 96 * unit + 96, 384 * half : 384 * half + 384
            ]


def down_grad(active, g_low, after):
    rows = active.shape[0]
    return pl.pallas_call(
        down_grad_kernel,
        out_shape=jax.ShapeDtypeStruct((4, 4, 384, 384), jnp.bfloat16),
        grid=(8,),
        in_specs=[
            pl.BlockSpec((rows, 384), lambda i: (0, i)),
            pl.BlockSpec((rows, D), lambda i: (0, 0)),
            ANY_SPEC,
        ],
        out_specs=pl.BlockSpec((2, 1, 384, 384), lambda i: (i % 2, (i // 2) % 2 * 2 + i // 4, 0, 0)),
        compiler_params=PARAMS,
        cost_estimate=pl.CostEstimate(
            flops=2 * rows * D * FF, bytes_accessed=8 << 20, transcendentals=0
        ),
        name="down_grad",
    )(active, g_low, after).reshape(2 * FF, D // 2)


def turn(index):
    return (index & 1) * 2 + index // 2


def upper_grad_kernel(ids, hid, g_raised, attn, g_att, vec, after, near, far):
    core, group = ids[1], ids[3]
    outer = tn(attn[...], g_att[...]).astype(jnp.bfloat16)
    left = hid[...].T
    for k in range(GROUPS):
        lanes = slice(384 * k, 384 * k + 384)
        part = jnp.dot(left, g_raised[:, lanes], preferred_element_type=jnp.float32)
        part = part.astype(jnp.bfloat16)
        place = turn(k ^ group)
        for target, own in ((near, core == 0), (far, core != 0)):
            target[place, 0:192, :] = jnp.where(own, part[:192], part[192:])
            first, second = (outer[192 * b + 48 * k : 192 * b + 48 * k + 48] for b in range(2))
            target[place, 192:240, :] = jnp.where(own, first, second)
            target[place, 240:256, :] = vec[k]


def upper_grad(ids, hid, g_raised, attn, g_att, vec, after):
    rows = hid.shape[0]

    def place(i, j, ids):
        return ((j ^ ids[2]) * 2 + (i ^ ids[0]), 0, 0)

    return pl.pallas_call(
        upper_grad_kernel,
        out_shape=(jax.ShapeDtypeStruct((16, 256, 384), jnp.bfloat16),) * 2,
        grid_spec=pltpu.PrefetchScalarGridSpec(
            num_scalar_prefetch=1,
            grid=(2, 2),
            in_specs=[
                pl.BlockSpec((rows, 384), lambda i, j, ids: (0, i)),
                pl.BlockSpec((rows, 1536), lambda i, j, ids: (0, j)),
                pl.BlockSpec((rows, 384), lambda i, j, ids: (0, i)),
                pl.BlockSpec((rows, 384), lambda i, j, ids: (0, j)),
                pl.BlockSpec((4, 16, 384), lambda i, j, ids: (j, 0, 0)),
                ANY_SPEC,
            ],
            out_specs=(pl.BlockSpec((4, 256, 384), place),) * 2,
        ),
        compiler_params=PARAMS,
        cost_estimate=pl.CostEstimate(
            flops=2 * rows * D * (FF + D), bytes_accessed=12 << 20, transcendentals=0
        ),
        name="upper_grad",
    )(ids, hid, g_raised, attn, g_att, vec, after)


def own_source(d, j, ids):
    return (jnp.where(d == 0, j, 1) ^ ids[2], 0, 0)


def other_source(d, j, ids):
    return (jnp.where(d == 0, 0, j) ^ ids[2], 0, 0)


def unpack_upper_kernel(ids, block_own, block_other, up, out, *vecs):
    side, core, mid, group = ids[0], ids[1], ids[2], ids[3]
    b, j = pl.program_id(0) ^ core, pl.program_id(1)
    own = pl.program_id(0) == 0
    for k in range(GROUPS):
        place = turn(k ^ group)
        part = jnp.where(own, block_own[place], block_other[place]).astype(jnp.float32)
        up[:, 384 * k : 384 * k + 384] = part[0:192]
        out[48 * k : 48 * k + 48, :] = part[192:240]

    @pl.when(b == 0)
    def _():
        for u in range(8):
            place = turn((u % 4) ^ group)
            rows = jnp.where(own, block_own[place, 240:256, :], block_other[place, 240:256, :])
            rows = rows.astype(jnp.float32)
            for r in range(3):
                row = 3 * u + r
                if row < 12:
                    target, where, half = vecs[row // 2], 0, row % 2
                elif row < 20:
                    target, where, half = vecs[6], (row - 12) % 4, (row - 12) // 4
                else:
                    continue

                @pl.when((j == u // 4) & (side == half))
                def _():
                    target[384 * where : 384 * where + 384] = rows[r]


def unpack_upper(ids, own, other):
    sizes = [384] * 6 + [1536]
    return pl.pallas_call(
        unpack_upper_kernel,
        out_shape=(
            jax.ShapeDtypeStruct((384, FF), jnp.float32),
            jax.ShapeDtypeStruct((384, D), jnp.float32),
        )
        + tuple(jax.ShapeDtypeStruct((size,), jnp.float32) for size in sizes),
        grid_spec=pltpu.PrefetchScalarGridSpec(
            num_scalar_prefetch=1,
            grid=(2, 2),
            in_specs=[
                pl.BlockSpec((4, 256, 384), own_source),
                pl.BlockSpec((4, 256, 384), other_source),
            ],
            out_specs=(
                pl.BlockSpec((192, 1536), lambda d, j, ids: (d ^ ids[1], j)),
                pl.BlockSpec((192, 384), lambda d, j, ids: (d ^ ids[1], j)),
            )
            + tuple(pl.BlockSpec((size,), lambda d, j, ids: (0,)) for size in sizes),
        ),
        compiler_params=PARAMS,
        name="unpack_upper",
    )(ids, own, other)


def unpack_down_kernel(ids, block_own, block_other, down):
    own, j = pl.program_id(0) == 0, pl.program_id(1)
    for k in range(GROUPS):
        place = turn(k ^ ids[3])
        part = jnp.where(own, block_own[place], block_other[place]).astype(jnp.float32)
        rows = pl.ds(pl.multiple_of(96 * j, 32) + 192 * k, 96)
        down[rows, 0:384] = part[0:96]
        down[rows, 384:768] = part[96:192]


def unpack_down(ids, own, other):
    return pl.pallas_call(
        unpack_down_kernel,
        out_shape=jax.ShapeDtypeStruct((FF // 2, D), jnp.float32),
        grid_spec=pltpu.PrefetchScalarGridSpec(
            num_scalar_prefetch=1,
            grid=(2, 2),
            in_specs=[
                pl.BlockSpec((4, 192, 384), own_source),
                pl.BlockSpec((4, 192, 384), other_source),
            ],
            out_specs=pl.BlockSpec((FF // 4, D), lambda d, j, ids: (d ^ ids[1], 0)),
        ),
        compiler_params=PARAMS,
        name="unpack_down",
    )(ids, own, other)


def qkv_grad_kernel(ids, t0, t1, t2, t3, *rest):
    kept, given, sent, dq, near, far, both, whole = rest
    x, c = ids[0], ids[1]
    rows = dq.shape[0] // GROUPS
    total = jnp.zeros((1, 576), jnp.float32)
    for flip in range(GROUPS):
        term = (
            kept[0, flip].astype(jnp.float32)
            + given[0, flip].astype(jnp.float32)
            + sent[flip].astype(jnp.float32)
        ).astype(jnp.bfloat16)
        own = slice(rows * flip, rows * flip + rows)
        start = pl.multiple_of((flip ^ ids[3]) * rows, 64)
        block = jnp.concatenate([term, dq[pl.ds(start, rows), :]], axis=1)
        half = rows // 2
        last = jnp.concatenate([block[:half, 512:], block[half:, 512:]], axis=1)
        both[flip ^ ids[3]] = jnp.concatenate(
            [block[:, 128 * n : 128 * n + 128] for n in range(4)] + [last], axis=0
        )
        whole[own, :] = block
        total = total + jnp.sum(block.astype(jnp.float32), axis=0, keepdims=True)
    first = lax.broadcasted_iota(jnp.int32, (16, 576), 0) == 0
    total = jnp.where(first, jnp.broadcast_to(total, (16, 576)), 0.0).astype(jnp.bfloat16)

    @pl.loop(0, 2)
    def _(i):
        lanes = pl.ds(pl.multiple_of(i * 384, 128), 384)
        left = jnp.concatenate([t[:, lanes] for t in (t0, t1, t2, t3)], axis=0)
        part = tn(left, whole[...]).astype(jnp.bfloat16)
        for b in range(2):

            def store(target):
                target[i ^ x, 0:192, :] = part[192 * b : 192 * b + 192]

            pl.when(c == b)(functools.partial(store, near))
            pl.when(c != b)(functools.partial(store, far))
        near[i ^ x, 192:208, :] = total
        far[i ^ x, 192:208, :] = total


def qkv_grads(ids, tokens, kept, given, sent, dq):
    queries = dq.shape[0]
    rows = queries // GROUPS
    return pl.pallas_call(
        qkv_grad_kernel,
        out_shape=(jax.ShapeDtypeStruct((2, 208, 576), jnp.bfloat16),) * 2
        + (jax.ShapeDtypeStruct((GROUPS, rows * 9 // 2, 128), jnp.bfloat16),),
        in_specs=[SMEM_SPEC] + [VMEM_SPEC] * 8,
        out_specs=(VMEM_SPEC,) * 3,
        scratch_shapes=[pltpu.VMEM((queries, 576), jnp.bfloat16)],
        compiler_params=PARAMS,
        cost_estimate=pl.CostEstimate(
            flops=2 * queries * D * 576, bytes_accessed=4 << 20, transcendentals=0
        ),
        name="qkv_grads",
    )(ids, *tokens, kept, given, sent, dq)


def unpack_qkv_kernel(ids, own, other, out_q, out_k, out_v, vec):
    c, h = ids[1], ids[3]
    for b in range(2):
        q, k, v = [], [], []
        for g in range(GROUPS):
            block = jnp.where(c == b, own[turn(g ^ h), 0:192, :], other[turn(g ^ h), 0:192, :]).astype(jnp.float32)
            k += [block[:, 0:128], block[:, 192:256]]
            v += [block[:, 256:384], block[:, 128:192]]
            q += [block[:, 384:576]]
        for out, parts in ((out_q, q), (out_k, k), (out_v, v)):
            out[192 * b : 192 * b + 192, :] = jnp.concatenate(parts, axis=1)
    for g in range(GROUPS):
        vec[g] = jnp.where(c == 0, own[turn(g ^ h), 192:208, :], other[turn(g ^ h), 192:208, :]).astype(jnp.float32)


def unpack_qkv(ids, own, other):
    return pl.pallas_call(
        unpack_qkv_kernel,
        out_shape=(jax.ShapeDtypeStruct((384, D), jnp.float32),) * 3
        + (jax.ShapeDtypeStruct((GROUPS, 16, 576), jnp.float32),),
        in_specs=[SMEM_SPEC, VMEM_SPEC, VMEM_SPEC],
        out_specs=(VMEM_SPEC,) * 4,
        compiler_params=PARAMS,
        name="unpack_qkv",
    )(ids, own, other)


def token_grad_kernel(base, both, weight, out):
    total = base[...]
    for g in range(GROUPS):
        w = weight[:, 640 * g : 640 * g + 576]
        block = both[g]
        if block.shape[1] == 128:
            rows = total.shape[0]
            last = block[4 * rows :]
            block = jnp.concatenate(
                [block[rows * n : rows * n + rows] for n in range(4)]
                + [jnp.concatenate([last[:, :64], last[:, 64:]], axis=0)],
                axis=1,
            )
        total = total + lax.dot_general(block, w, NT, preferred_element_type=jnp.float32)
    out[...] = total


def token_grads(base, both, weight):
    return pl.pallas_call(
        token_grad_kernel,
        out_shape=jax.ShapeDtypeStruct(base.shape, jnp.float32),
        in_specs=[VMEM_SPEC] * 3,
        out_specs=VMEM_SPEC,
        compiler_params=PARAMS,
        cost_estimate=pl.CostEstimate(
            flops=2 * base.shape[0] * D * 2304, bytes_accessed=8 << 20, transcendentals=0
        ),
        name="token_grads",
    )(base, both, weight)


def own_part(weight, core):
    half = weight.shape[0] // 2
    return lax.dynamic_slice_in_dim(weight, core * half, half, 0)


def reduce_blocks(grad):
    flat = grad.reshape((-1,) + grad.shape[2:])
    mine = lax.psum_scatter(flat, ("wa", "c"), scatter_dimension=0, tiled=True)
    mine = lax.psum_scatter(mine, "m", scatter_dimension=0, tiled=True)
    mine = lax.psum_scatter(mine, "h", scatter_dimension=0, tiled=True)
    return lax.all_gather(mine, ("c", "m", "h"), axis=0, tiled=True)


def tie(array, *others):
    return lax.optimization_barrier((array,) + others)[0]


def both_sum(near, far, *others):
    near = tie(near, *others)
    return low(widen(near) + widen(far))


def fold(near, far, *others):
    near = tie(near, *others)
    return [low(widen(near[i]) + widen(far[i])) for i in range(2)]


def double(array, axis, bit):
    return jnp.concatenate([array, swap(array, axis, bit)], axis=0)


def pick_columns(weight, group):
    q, k, v = (lax.dynamic_slice_in_dim(w, group * WIDTH, WIDTH, w.ndim - 1) for w in weight)
    return jnp.concatenate(
        [
            k[..., :128],
            v[..., 128:],
            k[..., 128:],
            v[..., :128],
            q[..., :128],
            jnp.zeros_like(q[..., :64]),
            q[..., 128:],
        ],
        axis=-1,
    )


def per_device(
    tokens,
    segment_ids,
    cotangent,
    w_query,
    w_key,
    w_value,
    w_out,
    w_up,
    w_down,
    b_query,
    b_value,
    b_out,
    gain_one,
    shift_one,
    b_up,
    b_down,
    gain_two,
    shift_two,
):
    mid = lax.axis_size("m")
    wide = lax.axis_size("wa")
    paired = mid == 2 and wide == 2
    classes = 2 * mid
    group = lax.axis_index("h")
    core = lax.axis_index("c")
    kind = lax.axis_index("m") * 2 + core
    side = lax.axis_index("wa")
    inputs = tokens[0]
    count = inputs.shape[0]
    chunks = GROUPS * classes
    length = count * chunks
    tiles = length // KTILE
    ids = jnp.stack([group, kind]).astype(jnp.int32)
    place_ids = jnp.stack([side, core, lax.axis_index("m"), group]).astype(jnp.int32)
    order = group ^ jnp.arange(GROUPS)

    second = swap(inputs, "h", 1)
    third = swap(inputs, "h", 2)
    if wide == 2:
        w_own = pick_weights(place_ids, w_query, w_key, w_value)
        w_other = swap(w_own, "wa", 1)
    else:
        w_own = None
        w_other = lax.all_gather(
            pick_columns((w_query, w_key, w_value), group), "wa", axis=0, tiled=True
        )

    smalls = [b_query, b_value, b_out, gain_one, shift_one, b_up, b_down, gain_two, shift_two]
    w_parts = [own_part(item, core) for item in (w_out, w_up, w_down)]
    joined = lax.all_gather(tie(jnp.concatenate(smalls), *w_parts), "wa", axis=0)
    second, third, w_other, joined = lax.optimization_barrier((second, third, w_other, joined))
    fourth = swap(third, "h", 1)
    full, place = [], 0
    for item in smalls:
        size = item.shape[0]
        full.append(widen(joined[:, place : place + size].reshape(-1)))
        place += size
    bias_query, bias_value, bias_out, gain_attn, shift_attn, bias_up, bias_down, gain_ffn, shift_ffn = full
    b_group = pick_columns((bias_query, jnp.zeros_like(bias_query), bias_value), group)[None]

    w_group = (w_own, w_other) if wide == 2 else (w_other,)
    full_out, full_up, full_down = (
        lax.all_gather(tie(part, w_other), ("wa", "c"), axis=0, tiled=True) for part in w_parts
    )
    where, pieces = [], []

    def spread(piece, flips):
        have = {0: piece}
        bit = 1
        while bit < mid:
            for mask in list(have):
                have[mask | (bit << 1)] = swap(have[mask], "m", bit)
            bit *= 2
        for mask in list(have):
            have[mask | 1] = swap(have[mask], "c", 1)
        for mask, item in have.items():
            where.append((mask, flips))
            pieces.append(item)

    first_kv, first_q = project(place_ids, b_group, (inputs, second, third), w_group)
    spread(first_kv, (0, 1, 2))

    segs = double(tie(segment_ids, first_kv), "c", 1)
    bit = 1
    while bit < mid:
        segs = double(segs, "m", bit)
        bit *= 2
    segs = double(double(segs, "h", 1), "h", 2)
    segs = jnp.take(segs, (group * classes + kind) ^ jnp.arange(chunks), axis=0)

    own_segs = lax.dynamic_index_in_dim(
        segs.reshape(GROUPS, classes, count), kind, 1, keepdims=False
    ).reshape(-1)

    names = jnp.arange(DOCS)
    begins = jnp.sum((segs.reshape(-1, 1) < names).astype(jnp.int32), axis=0)
    ends = jnp.sum((segs.reshape(-1, 1) <= names).astype(jnp.int32), axis=0)
    chosen = own_segs[None, :] == names[:, None]
    begins = jnp.sum(jnp.where(chosen, begins[:, None], 0), axis=0)
    ends = jnp.sum(jnp.where(chosen, ends[:, None], 0), axis=0)
    spans = jnp.concatenate(
        [begins[None], ends[None], jnp.zeros((6, begins.shape[0]), jnp.int32)], axis=0
    )
    ends_at = length // KSTEP
    edges = (jnp.arange(ends_at) * KSTEP)[None, :, None]
    meets = (begins.reshape(-1, 1, QTILE) < edges + KSTEP) & (ends.reshape(-1, 1, QTILE) > edges)
    meets = jnp.any(meets, axis=-1)
    steps = jnp.arange(ends_at)
    starts = jnp.arange(ends_at + KTILE // KSTEP + 1)
    later = meets[:, None, :] & (steps[None, None, :] >= starts[None, :, None])
    flags = jnp.min(jnp.where(later, steps, ends_at), axis=-1).astype(jnp.int32).reshape(-1)

    last_kv, last_q = project(place_ids, b_group, (fourth,), w_group)
    spread(last_kv, (3,))
    where = tuple(where)
    group_tokens = [inputs, second, third, fourth]

    o_parts, o_first, o_second, lse = attend_forward(
        ids, flags, first_q, last_q, spans, pieces, where, count, classes
    )

    w_query, w_key, w_value = (tie(item, lse) for item in (w_query, w_key, w_value))
    columns = []
    for g in range(GROUPS):
        low_part, high_part = slice(192 * g, 192 * g + 128), slice(192 * g + 128, 192 * g + 192)
        columns += [w_key[:, low_part], w_value[:, high_part], w_key[:, high_part], w_value[:, low_part]]
        columns += [w_query[:, 192 * g : 192 * g + 192], jnp.zeros_like(w_query[:, :64])]
    by_group = own_part(jnp.concatenate(columns, axis=1), core)
    by_group = lax.all_gather(by_group, ("wa", "c"), axis=0, tiled=True)

    def send_back(parts):
        return lax.all_to_all(parts, "h", 0, 0, tiled=True)

    zeros = jnp.zeros_like(bias_out)
    attn_low, hidden, hidden_low, unit_one, scale_one = out_project(
        send_back(o_parts),
        full_out,
        jnp.stack([bias_out, gain_attn, shift_attn] + [zeros] * 5),
        inputs,
    )
    scale_one = scale_one[:, :1]
    raised = mm(hidden_low, full_up) + bias_up
    active, slope = gelu_pair(raised)
    active_low = low(active)
    lowered = mm(active_low, full_down) + bias_down
    result, unit_two, scale_two = norm_forward(hidden + lowered, gain_ffn, shift_ffn)
    grad_sum_two, grad_gain_two, grad_shift_two = norm_backward(
        widen(cotangent[0]), unit_two, scale_two, gain_ffn
    )
    grad_lowered = low(grad_sum_two)
    grad_b_down = jnp.sum(widen(grad_lowered), axis=0)
    grad_raised = low(back_product(grad_lowered, full_down) * slope)
    grad_b_up = jnp.sum(widen(grad_raised), axis=0)
    grad_hidden = grad_sum_two + back_product(grad_raised, full_up)
    grad_sum_one, grad_gain_one, grad_shift_one = norm_backward(
        grad_hidden, unit_one, scale_one, gain_attn
    )
    grad_attended = low(grad_sum_one)
    grad_b_out = jnp.sum(widen(grad_attended), axis=0)

    grad_rows = send_back(out_back(grad_attended, full_out))

    vectors = jnp.concatenate(
        [grad_b_out, grad_gain_one, grad_shift_one, grad_b_down, grad_gain_two, grad_shift_two, grad_b_up]
    )
    blocks = 2 * wide
    if paired:
        vectors = jnp.pad(low(vectors), (0, 9216 - 7680)).reshape(8, 3, 384)
        vectors = jnp.pad(vectors, ((0, 0), (0, 13), (0, 0)))
        near, far = upper_grad(
            place_ids, hidden_low, grad_raised, attn_low, grad_attended, vectors, grad_attended
        )
        shape = (2, 2, 2, 2, 256, 384)
        near, far = near.reshape(shape), swap(far, "c", 1).reshape(shape)
        grad_rows = tie(grad_rows, near)
        down_sum = down_grad(active_low, grad_lowered, near)
        upper, give = fold(near, far, down_sum)
        after = (give,)
        give = swap(give, "m", 1)
        down_sum = tie(down_sum, grad_rows, by_group)
        down_sum = lax.psum_scatter(down_sum, ("h", "c"), scatter_dimension=0, tiled=True)
    else:
        grad_w_down = low(outer_sum(active_low, grad_lowered))
        grad_w_up = low(outer_sum(hidden_low, grad_raised))
        grad_w_out = low(outer_sum(attn_low, grad_attended))
        vectors = jnp.pad(low(vectors).reshape(-1, D), ((0, 6), (0, 0)))
        down_rows, out_rows = FF // blocks, D // blocks
        ffn = jnp.concatenate(
            [
                grad_w_down.reshape(blocks, down_rows, D),
                grad_w_up.reshape(blocks, down_rows, D),
                grad_w_out.reshape(blocks, out_rows, D),
                jnp.broadcast_to(vectors[None], (blocks, 16, D)),
            ],
            axis=1,
        )
        after = ()
        ffn_sum = reduce_blocks(ffn).reshape(2, -1, D)
        out_down = widen(ffn_sum[:, :down_rows]).reshape(-1, D)
        out_up = widen(ffn_sum[:, down_rows : 2 * down_rows]).reshape(-1, FF)
        place = 2 * down_rows
        out_out = widen(ffn_sum[:, place : place + out_rows]).reshape(-1, D)
        small = widen(ffn_sum[0, place + out_rows :])

        def share(row, rows):
            vector = small[row : row + rows].reshape(-1)
            size = vector.shape[0] // wide
            return lax.dynamic_slice_in_dim(vector, side * size, size, 0)

        vectors = [share(row, 1) for row in range(6)] + [share(6, 4)]

    stay_masks, leave_masks = tuple(range(0, classes, 2)), tuple(range(1, classes, 2))
    out_where = (stay_masks,) + tuple((mask,) for mask in leave_masks)

    kept, *given, dq = attend_backward(
        ids, flags, first_q, last_q, spans, grad_rows, (o_first, o_second), lse,
        pieces, after, where, count, classes, out_where,
    )

    given = [swap(item, "c", 1) for item in given]
    if paired:
        upper, give = fold(upper, give, dq)
        kept = tie(kept, give)
        sent = low(widen(kept[1]) + widen(given[1][0]))
        down_sum = lax.psum_scatter(tie(down_sum, sent), "wa", scatter_dimension=0, tiled=True)
        give = swap(give, "wa", 1)
        upper = tie(upper, sent)
        sent = swap(sent, "m", 1)
        upper, give = fold(upper, give)
        kept = tie(kept, give)
        give = swap(give, "h", 1)
    else:
        partial = widen(kept) + widen(jnp.concatenate(given, axis=0))
        stay = list(stay_masks)
        bit = mid // 2
        while bit >= 1:
            mask = bit << 1
            near = [i for i, m in enumerate(stay) if not m & mask]
            far = [i for i, m in enumerate(stay) if m & mask]
            sent = swap(low(partial[far[0] : far[-1] + 1]), "m", bit)
            partial = widen(low(partial[near[0] : near[-1] + 1])) + widen(sent)
            stay = [stay[i] for i in near]
            bit //= 2
        dkv = low(partial[0]).reshape(GROUPS * count, 384)

    part = D // wide
    if paired:
        near, far, parts = qkv_grads(place_ids, group_tokens, kept, given[0], sent, dq)
        far = swap(far, "c", 1)
        down_sum = lax.psum_scatter(tie(down_sum, near), "m", scatter_dimension=0, tiled=True)
        upper, give = fold(upper, give, near)
        near = tie(near, give)
        give = swap(give, "h", 2)
        qkv, other = fold(near, far)
        other = swap(other, "wa", 1)
        down_other = swap(down_sum, "h", 2)
        upper = both_sum(upper, give, qkv)
        upper_other = swap(upper, "h", 2)
        qkv = both_sum(qkv, other, upper)
        other = swap(qkv, "m", 1)
        down_sum = jnp.stack([tie(down_sum, qkv), down_other])
        down_other = swap(down_sum, "h", 1)
        upper = jnp.stack([tie(upper, down_sum), upper_other])
        upper_other = swap(upper, "h", 1)
        qkv = both_sum(qkv, other, upper)
        other = swap(qkv, "h", 2)
        down_sum = jnp.stack([tie(down_sum, qkv), down_other])
        down_other = swap(down_sum, "m", 1)
        upper = jnp.stack([tie(upper, down_sum), upper_other])
        upper_other = swap(upper, "m", 1)
        parts = send_back(tie(parts, upper))
        qkv = jnp.stack([tie(qkv, upper), other])
        other = swap(qkv, "h", 1)
        down_sum = jnp.stack([tie(down_sum, qkv), down_other])
        down_other = swap(down_sum, "c", 1)
        qkv = jnp.concatenate([tie(qkv, down_sum), other], axis=0)
        other = swap(qkv, "c", 1)
        down_sum, down_other = (item.reshape(8, 192, 384) for item in (tie(down_sum, qkv), down_other))
        out_down = unpack_down(place_ids, down_sum, down_other)
        upper = jnp.stack([tie(upper, out_down), upper_other])
        upper_other = swap(upper, "c", 1)
        out_query, out_key, out_value, sums = unpack_qkv(place_ids, tie(qkv, upper), other)
        upper, upper_other = (item.reshape(8, 256, 384) for item in (tie(upper, out_query), upper_other))
        out_up, out_out, *vectors = unpack_upper(place_ids, upper, upper_other)
        grad_inputs = token_grads(tie(grad_sum_one, out_up), parts, by_group)
        sums = sums[:, 0]
        sums_v = jnp.concatenate([sums[:, 256:384], sums[:, 128:192]], axis=1).reshape(-1)
        sums_q = sums[:, 384:576].reshape(-1)
    else:
        dq = jnp.take(dq.reshape(GROUPS, count, WIDTH), order, axis=0).reshape(-1, WIDTH)
        both = jnp.concatenate([dkv, dq], axis=1)
        width = both.shape[1]
        parts = send_back(jnp.take(both.reshape(GROUPS, count, width), order, axis=0))
        w_grad = low(outer_sum(jnp.concatenate(group_tokens, axis=0), both)).reshape(blocks, D // blocks, width)
        b_grad = low(jnp.sum(widen(both), axis=0))
        b_grad = jnp.pad(b_grad[None], ((0, 15), (0, 0)))
        qkv = jnp.concatenate([w_grad, jnp.broadcast_to(b_grad[None], (blocks, 16, width))], axis=1)
        rows = qkv.shape[1]
        mine = lax.psum_scatter(
            qkv.reshape(blocks * rows, width), ("wa", "c"), scatter_dimension=0, tiled=True
        )
        mine = lax.psum(mine, "m")
        every = widen(lax.all_gather(mine, ("c", "h"), axis=0).reshape(2, GROUPS, rows, width))

        def columns(block):
            k = jnp.concatenate([block[..., :128], block[..., 192:256]], axis=-1)
            v = jnp.concatenate([block[..., 256:384], block[..., 128:192]], axis=-1)
            q = block[..., 384:576]
            return [jnp.transpose(item, (0, 2, 1, 3)).reshape(2, -1, D) for item in (q, k, v)]

        out_query, out_key, out_value = (
            item.reshape(-1, D) for item in columns(every[:, :, : rows - 16])
        )
        sums_q, _, sums_v = (item[0, 0] for item in columns(every[:, :, rows - 16 : rows - 15]))
        grad_inputs = token_grads(grad_sum_one, parts, by_group)
    out_b_query = lax.dynamic_slice_in_dim(sums_q, side * part, part, 0)
    out_b_value = lax.dynamic_slice_in_dim(sums_v, side * part, part, 0)

    return (
        low(result)[None],
        grad_inputs[None],
        out_query,
        out_key,
        out_value,
        out_out,
        out_up,
        out_down,
        out_b_query,
        out_b_value,
        vectors[0],
        vectors[1],
        vectors[2],
        vectors[6],
        vectors[3],
        vectors[4],
        vectors[5],
    )


def solution(mesh):
    chunks, wide = mesh.devices.shape
    finer = Mesh(
        mesh.devices.reshape(GROUPS, chunks // (2 * GROUPS), 2, wide), ("h", "m", "c", "wa")
    )
    ctx = ("h", "m", "c")
    seq3, seq2 = P("wa", ctx, None), P("wa", ctx)
    matrix, vector = P("wa", None), P("wa")
    return jax.shard_map(
        per_device,
        mesh=finer,
        in_specs=(seq3, seq2, seq3) + (matrix,) * 6 + (vector,) * 9,
        out_specs=(seq3, seq3) + (matrix,) * 6 + (vector,) * 9,
        check_vma=False,
    )
```
